128 devices in a mesh: seq: 4 (over z), shard: 2 (over x_hi), dp: 16 (over y, x_lo, core).
Axes of the slice: x: 4 (x_hi: 2, x_lo: 2; x = x_hi * 2 + x_lo), y: 4, z: 4, core: 2. Of those that a mesh axis runs over, the one named last changes fastest.
Arguments:
- inputs: float32 [64, 320, 1024], P(('shard', 'dp'), 'seq'), may hold values from -6 to 6
- segment_ids: int32 [64, 320], P(('shard', 'dp'), 'seq'), may hold values from 0 to 2, never falling along the last dimension, each value on 1 to 160 neighbouring positions
- weight_qkv: bfloat16 [2, 1024, 3072], P(None, ('seq', 'shard')), may hold values from -30 to 30
- weight_out: bfloat16 [2, 1024, 1024], P(None, ('seq', 'shard')), may hold values from -0.75 to 0.75
- weight_up: bfloat16 [2, 1024, 4096], P(None, ('seq', 'shard')), may hold values from -0.1875 to 0.1875
- weight_down: bfloat16 [2, 4096, 1024], P(None, ('seq', 'shard')), may hold values from -0.09375 to 0.09375
- bias_qv: bfloat16 [2, 2048], P(None, ('seq', 'shard')), may hold values from -3 to 3
- bias_out: bfloat16 [2, 1024], P(None, ('seq', 'shard')), may hold values from -3 to 3
- bias_up: bfloat16 [2, 4096], P(None, ('seq', 'shard')), may hold values from -3 to 3
- bias_down: bfloat16 [2, 1024], P(None, ('seq', 'shard')), may hold values from -3 to 3
- gain_one: bfloat16 [2, 1024], P(None, ('seq', 'shard')), may hold values from 0.5 to 1.5
- shift_one: bfloat16 [2, 1024], P(None, ('seq', 'shard')), may hold values from -3 to 3
- gain_two: bfloat16 [2, 1024], P(None, ('seq', 'shard')), may hold values from 0.5 to 1.5
- shift_two: bfloat16 [2, 1024], P(None, ('seq', 'shard')), may hold values from -3 to 3
- cotangent: float32 [64, 320, 1024], P(('shard', 'dp'), 'seq'), may hold values from -0.75 to 0.75
Outputs:
- outputs: float32 [64, 320, 1024], P(('shard', 'dp'), 'seq')
- input_grad: float32 [64, 320, 1024], P(('shard', 'dp'), 'seq')
- grad_weight_qkv: float32 [2, 1024, 3072], P(None, ('seq', 'shard'))
- grad_weight_out: float32 [2, 1024, 1024], P(None, ('seq', 'shard'))
- grad_weight_up: float32 [2, 1024, 4096], P(None, ('seq', 'shard'))
- grad_weight_down: float32 [2, 4096, 1024], P(None, ('seq', 'shard'))
- grad_bias_qv: float32 [2, 2048], P(None, ('seq', 'shard'))
- grad_bias_out: float32 [2, 1024], P(None, ('seq', 'shard'))
- grad_bias_up: float32 [2, 4096], P(None, ('seq', 'shard'))
- grad_bias_down: float32 [2, 1024], P(None, ('seq', 'shard'))
- grad_gain_one: float32 [2, 1024], P(None, ('seq', 'shard'))
- grad_shift_one: float32 [2, 1024], P(None, ('seq', 'shard'))
- grad_gain_two: float32 [2, 1024], P(None, ('seq', 'shard'))
- grad_shift_two: float32 [2, 1024], P(None, ('seq', 'shard'))
The draws below stay inside these ranges and needn't reach their ends.
All inputs are finite; a program needn't handle non-finite values.
Results may differ from the reference program's by a relative error of at most 0.03.
Values may be sent and summed in bfloat16 or wider, within the bound.
A program may use at most 256 MiB of HBM per device.

```python
import math
import jax
import jax.numpy as jnp
import numpy as np
from jax import lax

D = 1024
H = 16
FF = 4096
HD = 64
LEN = 320
LAYERS = 2
SEQS_DEV = 2
SEQS = 64


def draw_weight_qkv(key, part):
    base = jnp.clip(jax.random.normal(key, (LAYERS, D, 3 * D), jnp.float32), -6.0, 6.0) / math.sqrt(D)
    return base.astype(jnp.bfloat16)


def block_scale(stream_key, extent, shards, least, high):
    level, own = 1.0, jax.random.fold_in(stream_key, 6)
    for dim, parts in shards:
        draws = jnp.exp(jax.random.uniform(jax.random.fold_in(own, dim), (parts,), jnp.float32, least / len(shards), high / len(shards)))
        level = level * jnp.repeat(draws, extent[dim] // parts).reshape([-1 if axis == dim else 1 for axis in range(len(extent))])
    return level


def profile(number_of, total, most, lean):
    portions = [(1 << 20) // math.isqrt(rank ** lean) + 1 for rank in range(2, number_of + 1)]
    surplus, counts = total - most - (number_of - 1), [1] * (number_of - 1)
    while surplus > 0:
        free = [i for i in range(number_of - 1) if counts[i] < most]
        whole, left = sum([portions[i] for i in free]), surplus
        for i in free:
            addition = min(most - counts[i], max(1, left * portions[i] // whole), surplus)
            counts[i] = counts[i] + addition
            surplus = surplus - addition
    return np.array([most] + counts)


def uneven_parts(rng, amount, total, most, lean):
    if amount == 2:
        one = jax.random.randint(rng, (), max(1, total - most), min(most, total - 1) + 1)
        return jnp.stack([one, total - one])
    tallies = jnp.asarray(profile(amount, total, most, lean), jnp.int32)
    couples = (amount - 1) // 2
    donor, receiver = tallies[1:1 + 2 * couples:2], tallies[2:2 + 2 * couples:2]
    room = jnp.minimum(donor - 1, most - receiver)
    passed = jax.random.randint(jax.random.fold_in(rng, 1), (couples,), 0, 1 << 20) % (room + 1)
    tallies = tallies.at[1:1 + 2 * couples:2].set(donor - passed).at[2:2 + 2 * couples:2].set(receiver + passed)
    return tallies[jax.random.permutation(jax.random.fold_in(rng, 2), amount)]


def bell_draw(own_key, extent, scale, reach, cuts=(), kind=jnp.bfloat16):
    level = block_scale(own_key, extent, cuts, -0.22, 0.18) if cuts else 1.0
    array = jax.random.normal(own_key, extent, jnp.float32) * scale * level
    return jnp.minimum(jnp.maximum(array, -reach), reach).astype(kind)


def setup_inputs(seed: int = 0) -> dict:
    key_of = jax.random.split(jax.random.key(seed), 16)
    inputs = bell_draw(key_of[0], (SEQS, LEN, D), 1.0, 6.0, ((0, 32), (1, 4)), jnp.float32)
    segment_ids = jax.vmap(lambda own: jnp.searchsorted(jnp.cumsum(uneven_parts(own, 3, LEN, LEN // 2, 0)), jnp.arange(LEN), side="right"))(jax.random.split(key_of[1], SEQS)).reshape((SEQS, LEN)).astype(jnp.int32)
    weight_qkv = draw_weight_qkv(jax.random.fold_in(key_of[15], 71), 0)
    weight_out = bell_draw(key_of[3], (LAYERS, D, D), (D // 16) ** -0.5, 0.75, ((1, 8),))
    weight_up = bell_draw(key_of[4], (LAYERS, D, FF), D ** -0.5, 0.1875, ((1, 8),))
    weight_down = bell_draw(key_of[5], (LAYERS, FF, D), FF ** -0.5, 0.09375, ((1, 8),))
    bias_qv = bell_draw(key_of[6], (LAYERS, 2 * D), 0.5, 3.0, ((1, 8),))
    bias_out = bell_draw(key_of[7], (LAYERS, D), 0.5, 3.0, ((1, 8),))
    bias_up = bell_draw(key_of[8], (LAYERS, FF), 0.5, 3.0, ((1, 8),))
    bias_down = bell_draw(key_of[9], (LAYERS, D), 0.5, 3.0, ((1, 8),))
    gain_one = jnp.clip(1.0 + 0.1 * jax.random.normal(key_of[10], (LAYERS, D), jnp.float32), 0.5, 1.5).astype(jnp.bfloat16)
    shift_one = bell_draw(key_of[11], (LAYERS, D), 0.5, 3.0, ((1, 8),))
    gain_two = jnp.clip(1.0 + 0.1 * jax.random.normal(key_of[12], (LAYERS, D), jnp.float32), 0.5, 1.5).astype(jnp.bfloat16)
    shift_two = bell_draw(key_of[13], (LAYERS, D), 0.5, 3.0, ((1, 8),))
    cotangent = bell_draw(key_of[14], (SEQS, LEN, D), 0.125, 0.75, ((0, 32), (1, 4)), jnp.float32)
    return dict(inputs=inputs, segment_ids=segment_ids, weight_qkv=weight_qkv, weight_out=weight_out, weight_up=weight_up, weight_down=weight_down, bias_qv=bias_qv, bias_out=bias_out, bias_up=bias_up, bias_down=bias_down, gain_one=gain_one, shift_one=shift_one, gain_two=gain_two, shift_two=shift_two, cotangent=cotangent)


NORM_EPS = 1e-05
GELU_COEF = 0.7978845608028654
CUBIC_COEF = 0.044715

def layer_norm(state, gain, shift):
    center = state - lax.optimization_barrier(jnp.mean(state, axis=-1, keepdims=True))
    factor = lax.rsqrt(lax.optimization_barrier(jnp.mean(center * center, axis=-1, keepdims=True)) + NORM_EPS)
    normed = center * factor
    return (normed, factor, normed * gain.astype(jnp.float32) + shift.astype(jnp.float32))

def norm_backward(d_act, normed, factor, gain):
    d_norm = d_act * gain.astype(jnp.float32)
    return factor * (d_norm - lax.optimization_barrier(jnp.mean(d_norm, axis=-1, keepdims=True)) - normed * lax.optimization_barrier(jnp.mean(d_norm * normed, axis=-1, keepdims=True)))

def gelu_pair(pre_act):
    cubic = pre_act * pre_act * pre_act
    tangent = jnp.tanh(GELU_COEF * (pre_act + CUBIC_COEF * cubic))
    gelu_value = 0.5 * pre_act * (1.0 + tangent)
    gelu_slope = 0.5 * (1.0 + tangent) + 0.5 * pre_act * (1.0 - tangent * tangent) * GELU_COEF * (1.0 + 3.0 * CUBIC_COEF * pre_act * pre_act)
    return (gelu_value, gelu_slope)

def product(form, left, right):
    return jnp.einsum(form, left.astype(jnp.float32), right.astype(jnp.float32), precision=lax.Precision.HIGHEST)

def masked_scores(queries, keys_all, allowed, scale):
    raw_scores = product('bqhd,bkhd->bhqk', queries, keys_all) * scale
    return jnp.where(allowed[:, None], raw_scores, -jnp.inf)

def attention_backward(queries, keys_all, values, attn_heads, lse, d_attn, allowed, scale):
    scores = masked_scores(queries, keys_all, allowed, scale)
    prob_full = jnp.exp(scores - lse)
    probs = prob_full.astype(jnp.bfloat16)
    delta = lax.optimization_barrier(jnp.sum(d_attn.astype(jnp.float32) * attn_heads.astype(jnp.float32), axis=-1))
    delta = jnp.transpose(delta, (0, 2, 1))[..., None]
    d_prob = product('bqhd,bkhd->bhqk', d_attn, values)
    d_scores = (prob_full * (d_prob - delta)).astype(jnp.bfloat16)
    d_query = product('bhqk,bkhd->bqhd', d_scores, keys_all) * scale
    d_key = product('bhqk,bqhd->bkhd', d_scores, queries) * scale
    d_value = product('bhqk,bqhd->bkhd', probs, d_attn)
    return (d_query, d_key, d_value)

def forward_layer(state, params, allowed, batch, scale):
    weight_qkv, weight_out, weight_up, weight_down, bias_qv, bias_out, bias_up, bias_down, gain_one, shift_one, gain_two, shift_two = params
    norm_one, factor_one, act_one = layer_norm(state, gain_one, shift_one)
    act_one = act_one.astype(jnp.bfloat16)
    bias_qkv = jnp.concatenate([bias_qv[:D].astype(jnp.float32), jnp.zeros((D,), jnp.float32), bias_qv[D:].astype(jnp.float32)])
    qkv = (jnp.dot(act_one, weight_qkv, preferred_element_type=jnp.float32) + bias_qkv).astype(jnp.bfloat16)
    qkv = qkv.reshape(batch, LEN, 3, H, HD)
    queries, keys_all, values = (qkv[:, :, 0], qkv[:, :, 1], qkv[:, :, 2])
    scores = masked_scores(queries, keys_all, allowed, scale)
    row_top = lax.optimization_barrier(jnp.max(scores, axis=-1, keepdims=True))
    lse = row_top + jnp.log(lax.optimization_barrier(jnp.sum(jnp.exp(scores - row_top), axis=-1, keepdims=True)))
    probs = jnp.exp(scores - lse).astype(jnp.bfloat16)
    attn = product('bhqk,bkhd->bqhd', probs, values).astype(jnp.bfloat16).reshape(batch * LEN, D)
    middle = state + jnp.dot(attn, weight_out, preferred_element_type=jnp.float32) + bias_out.astype(jnp.float32)
    norm_two, factor_two, act_two = layer_norm(middle, gain_two, shift_two)
    act_two = act_two.astype(jnp.bfloat16)
    pre_act = jnp.dot(act_two, weight_up, preferred_element_type=jnp.float32) + bias_up.astype(jnp.float32)
    gelu_value, gelu_slope = gelu_pair(pre_act)
    hidden = gelu_value.astype(jnp.bfloat16)
    new_state = middle + jnp.dot(hidden, weight_down, preferred_element_type=jnp.float32) + bias_down.astype(jnp.float32)
    record = (norm_one, factor_one, act_one, queries, keys_all, values, lse, attn, norm_two, factor_two, act_two, gelu_slope, hidden)
    return (record, new_state)

def backward_layer(grad_state, record, params, allowed, batch, scale):
    weight_qkv, weight_out, weight_up, weight_down, bias_qv, bias_out, bias_up, bias_down, gain_one, shift_one, gain_two, shift_two = params
    norm_one, factor_one, act_one, queries, keys_all, values, lse, attn, norm_two, factor_two, act_two, gelu_slope, hidden = record
    rows_all = batch * LEN
    grad_low = grad_state.astype(jnp.bfloat16)
    grad_w_down = jnp.dot(hidden.T, grad_low, preferred_element_type=jnp.float32)
    grad_b_down = lax.optimization_barrier(jnp.sum(grad_state, axis=0))
    d_pre = jnp.dot(grad_low, weight_down.T, preferred_element_type=jnp.float32) * gelu_slope
    d_pre_low = d_pre.astype(jnp.bfloat16)
    grad_w_up = jnp.dot(act_two.T, d_pre_low, preferred_element_type=jnp.float32)
    grad_b_up = lax.optimization_barrier(jnp.sum(d_pre, axis=0))
    d_act_two = jnp.dot(d_pre_low, weight_up.T, preferred_element_type=jnp.float32)
    grad_g_two = lax.optimization_barrier(jnp.sum(d_act_two * norm_two, axis=0))
    grad_s_two = lax.optimization_barrier(jnp.sum(d_act_two, axis=0))
    grad_middle = grad_state + norm_backward(d_act_two, norm_two, factor_two, gain_two)
    grad_attn_low = grad_middle.astype(jnp.bfloat16)
    grad_w_out = jnp.dot(attn.T, grad_attn_low, preferred_element_type=jnp.float32)
    grad_b_out = lax.optimization_barrier(jnp.sum(grad_middle, axis=0))
    d_attn = jnp.dot(grad_attn_low, weight_out.T, preferred_element_type=jnp.float32).astype(jnp.bfloat16)
    d_attn = d_attn.reshape(batch, LEN, H, HD)
    attn_heads = attn.reshape(batch, LEN, H, HD)
    d_query, d_key, d_value = attention_backward(queries, keys_all, values, attn_heads, lse, d_attn, allowed, scale)
    d_query = d_query.reshape(rows_all, D)
    d_value = d_value.reshape(rows_all, D)
    d_qkv = jnp.concatenate([d_query, d_key.reshape(rows_all, D), d_value], axis=1).astype(jnp.bfloat16)
    grad_w_qkv = jnp.dot(act_one.T, d_qkv, preferred_element_type=jnp.float32)
    grad_b_qv = jnp.concatenate([lax.optimization_barrier(jnp.sum(d_query, axis=0)), lax.optimization_barrier(jnp.sum(d_value, axis=0))])
    d_act_one = jnp.dot(d_qkv, weight_qkv.T, preferred_element_type=jnp.float32)
    grad_g_one = lax.optimization_barrier(jnp.sum(d_act_one * norm_one, axis=0))
    grad_s_one = lax.optimization_barrier(jnp.sum(d_act_one, axis=0))
    grad_input = grad_middle + norm_backward(d_act_one, norm_one, factor_one, gain_one)
    grads = (grad_w_qkv, grad_w_out, grad_w_up, grad_w_down, grad_b_qv, grad_b_out, grad_b_up, grad_b_down, grad_g_one, grad_s_one, grad_g_two, grad_s_two)
    return (grads, grad_input)

def run_block(inputs_blk, segs_blk, cot_blk, weights):
    batch = inputs_blk.shape[0]
    scale = 1.0 / math.sqrt(HD)
    position = jnp.arange(LEN, dtype=jnp.int32)
    allowed = (segs_blk[:, :, None] == segs_blk[:, None, :]) & (position[:, None] >= position[None, :])[None]
    state = inputs_blk.reshape(batch * LEN, D)
    records = []
    for layer_at in range(LAYERS):
        params = tuple((member[layer_at] for member in weights))
        record, state = forward_layer(state, params, allowed, batch, scale)
        records.append(record)
    grad_state = cot_blk.reshape(batch * LEN, D)
    layer_grads = [None] * LAYERS
    for layer_at in reversed(range(LAYERS)):
        params = tuple((member[layer_at] for member in weights))
        layer_grads[layer_at], grad_state = backward_layer(grad_state, records[layer_at], params, allowed, batch, scale)
    stacked = tuple((jnp.stack([layer_grads[layer_at][member_at] for layer_at in range(LAYERS)]) for member_at in range(12)))
    return (state.reshape(batch, LEN, D), grad_state.reshape(batch, LEN, D), stacked)

def reference(inputs, segment_ids, weight_qkv, weight_out, weight_up, weight_down, bias_qv, bias_out, bias_up, bias_down, gain_one, shift_one, gain_two, shift_two, cotangent):
    weights = (weight_qkv, weight_out, weight_up, weight_down, bias_qv, bias_out, bias_up, bias_down, gain_one, shift_one, gain_two, shift_two)
    blocks = SEQS // SEQS_DEV

    def scan_step(totals, pieces):
        inputs_blk, segs_blk, cot_blk = pieces
        outs_blk, grad_blk, grads = run_block(inputs_blk, segs_blk, cot_blk, weights)
        return (tuple((total + grad for total, grad in zip(totals, grads))), (outs_blk, grad_blk))
    initial = tuple((jnp.zeros(member.shape, jnp.float32) for member in weights))
    totals, (outs_all, grads_all) = lax.scan(scan_step, initial, (inputs.reshape(blocks, SEQS_DEV, LEN, D), segment_ids.reshape(blocks, SEQS_DEV, LEN), cotangent.reshape(blocks, SEQS_DEV, LEN, D)))
    return (outs_all.reshape(SEQS, LEN, D), grads_all.reshape(SEQS, LEN, D), totals[0], totals[1], totals[2], totals[3], totals[4], totals[5], totals[6], totals[7], totals[8], totals[9], totals[10], totals[11])
```

```python
import functools
import math

import jax
import jax.numpy as jnp
from jax import lax
from jax.experimental import pallas as pl
from jax.experimental.pallas import tpu as pltpu
from jax.sharding import Mesh
from jax.sharding import PartitionSpec as P

AXES = ("z", "xh", "y", "xl", "core")
RING = 4
ORDERS = ("xyz", "zxy", "yzx", "yzx")


def positions():
    return {
        "z": lax.axis_index("z"),
        "x": lax.axis_index("xh") * 2 + lax.axis_index("xl"),
        "y": lax.axis_index("y"),
    }


def neighbour(pos, axis, step):
    at = lax.rem(pos[axis] + step + RING, RING)
    if axis == "x":
        return {"xh": at // 2, "xl": lax.rem(at, 2)}
    return {axis: at}


def remote(src, dst, send, recv, target):
    return pltpu.make_async_remote_copy(
        src_ref=src,
        dst_ref=dst,
        send_sem=send,
        recv_sem=recv,
        device_id=target,
        device_id_type=pl.DeviceIdType.MESH,
    )


def greet(pos, with_column):
    barrier = pltpu.get_barrier_semaphore()
    targets = [neighbour(pos, axis, step) for axis in "xyz" for step in (1, -1)]
    if with_column:
        targets.append(neighbour(pos, "z", 2))
    targets.append({"core": 1 - lax.axis_index("core")})
    for target in targets:
        pl.semaphore_signal(
            barrier, inc=1, device_id=target, device_id_type=pl.DeviceIdType.MESH
        )
    pl.semaphore_wait(barrier, len(targets))


def half(ref, which, rows, cols):
    lead = (slice(None),) * (len(ref.shape) - 2)
    if rows % 16 == 0:
        return ref.at[lead + (pl.ds(which * (rows // 2), rows // 2), slice(None))]
    return ref.at[lead + (slice(None), pl.ds(which * (cols // 2), cols // 2))]


class Gather:
    def __init__(self, pos, order, own, full, send, recv):
        self.pos, self.order, self.own, self.full = pos, order, own, full
        self.send, self.recv = send, recv
        self.rows, self.cols = full.shape[-2:]

    def view(self, stage, shift):
        index = {}
        for place, axis in enumerate(self.order):
            if place < stage:
                index[axis] = slice(None)
            elif place == stage:
                index[axis] = lax.rem(self.pos[axis] + shift + RING, RING)
            else:
                index[axis] = self.pos[axis]
        return self.full.at[index["z"], index["x"], index["y"]]

    def copy(self, stage, kind):
        axis = self.order[stage]
        sems = (self.send.at[stage * 4 + kind], self.recv.at[stage * 4 + kind])
        target = neighbour(self.pos, axis, 1 if kind % 2 == 0 else -1)
        if kind < 2:
            src = self.own if stage == 0 else self.view(stage, 0)
            return remote(src, self.view(stage, 0), *sems, target)
        piece = half(self.view(stage, -1 if kind == 2 else 1), kind - 2, self.rows, self.cols)
        return remote(piece, piece, *sems, target)

    def arrive(self, stage, kind):
        sems = (self.send.at[stage * 4 + kind], self.recv.at[stage * 4 + kind])
        axis = self.order[stage]
        if kind < 2:
            piece = self.view(stage, -1 if kind == 0 else 1)
        else:
            piece = half(self.view(stage, 2), kind - 2, self.rows, self.cols)
        remote(piece, piece, *sems, neighbour(self.pos, axis, 1)).wait_recv()

    def begin(self, stage):
        for kind in (0, 1):
            self.copy(stage, kind).start()

    def onward(self, stage):
        for kind in (0, 1):
            self.arrive(stage, kind)
            self.copy(stage, kind + 2).start()

    def finish(self, stage):
        for kind in (2, 3):
            self.arrive(stage, kind)

    def drain(self):
        for stage in range(3):
            for kind in range(4):
                self.copy(stage, kind).wait_send()


def gather_kernel(count, moved, *refs):
    owns, parts = refs[:count], refs[count : count + moved]
    refs = refs[count + moved :]
    fulls, wholes = refs[:count], refs[count : count + moved]
    send, recv, local, send_t, recv_t, core_s, core_r, local_t = refs[count + moved :]
    pos = positions()
    core = lax.axis_index("core")
    greet(pos, True)
    for a in range(moved):
        for b in range(2):
            home = 2 * core + b
            here = home == pos["z"]

            @pl.when(here)
            def _():
                pltpu.make_async_copy(
                    parts[a].at[b], wholes[a].at[pos["z"]], local_t.at[a]
                ).start()

            @pl.when(jnp.logical_not(here))
            def _():
                remote(
                    parts[a].at[b],
                    wholes[a].at[pos["z"]],
                    send_t.at[a, b],
                    recv_t.at[a, pos["z"]],
                    {"z": home},
                ).start()

    streams = []
    for m in range(count):
        pltpu.make_async_copy(
            owns[m], fulls[m].at[pos["z"], pos["x"], pos["y"]], local.at[m]
        ).start()
        streams.append(
            Gather(pos, ORDERS[m % 4], owns[m], fulls[m], send.at[m], recv.at[m])
        )
    for s in streams:
        s.begin(0)
    receiver = pos["z"] // 2 == core

    def crossing(a, q):
        return remote(
            wholes[a].at[q],
            wholes[a].at[q],
            core_s.at[a, q],
            core_r.at[a, q],
            {"core": 1 - core},
        )

    @pl.when(receiver)
    def _():
        for a in range(moved):
            for q in range(RING):

                @pl.when(q == pos["z"])
                def _():
                    pltpu.make_async_copy(
                        parts[a].at[0], wholes[a].at[q], local_t.at[a]
                    ).wait()

                @pl.when(q != pos["z"])
                def _():
                    remote(
                        wholes[a].at[q],
                        wholes[a].at[q],
                        send_t.at[a, 0],
                        recv_t.at[a, q],
                        {"z": lax.rem(pos["z"] + 1, RING)},
                    ).wait_recv()

                crossing(a, q).start()

    for stage in range(3):
        for s in streams:
            s.onward(stage)
        for m, s in enumerate(streams):
            if stage == 0:
                pltpu.make_async_copy(
                    owns[m], fulls[m].at[pos["z"], pos["x"], pos["y"]], local.at[m]
                ).wait()
            s.finish(stage)
            if stage < 2:
                s.begin(stage + 1)
    for s in streams:
        s.drain()
    for a in range(moved):
        for b in range(2):

            @pl.when(2 * core + b != pos["z"])
            def _():
                remote(
                    parts[a].at[b],
                    wholes[a].at[pos["z"]],
                    send_t.at[a, b],
                    recv_t.at[a, pos["z"]],
                    {"z": lax.rem(pos["z"] + 1, RING)},
                ).wait_send()

        for q in range(RING):

            @pl.when(receiver)
            def _():
                crossing(a, q).wait_send()

            @pl.when(jnp.logical_not(receiver))
            def _():
                crossing(a, q).wait_recv()


def gather_all(owns, parts):
    count, moved = len(owns), len(parts)
    anyspec = pl.BlockSpec(memory_space=pl.ANY)
    shapes = [jax.ShapeDtypeStruct((RING, RING, RING) + o.shape, o.dtype) for o in owns]
    shapes += [jax.ShapeDtypeStruct((RING,) + p.shape[1:], p.dtype) for p in parts]
    dma = pltpu.SemaphoreType.DMA
    out = pl.pallas_call(
        functools.partial(gather_kernel, count, moved),
        out_shape=shapes,
        in_specs=[anyspec] * (count + moved),
        out_specs=[anyspec] * (count + moved),
        scratch_shapes=[
            dma((count, 12)),
            dma((count, 12)),
            dma((count,)),
            dma((moved, 2)),
            dma((moved, RING)),
            dma((moved, RING)),
            dma((moved, RING)),
            dma((moved,)),
        ],
        compiler_params=pltpu.CompilerParams(collective_id=0, has_side_effects=True),
        name="gather_all",
    )(*owns, *parts)
    return out[:count], out[count:]


class Scatter:
    def __init__(self, pos, order, grad, bufs, final, send, recv, local, sends_f, recvs_f):
        self.pos, self.order, self.grad, self.final = pos, order, grad, final
        self.own, self.boxes, self.sums = bufs[0], bufs[1:4], bufs[4:7]
        self.send, self.recv, self.local = send, recv, local
        self.sends_f, self.recvs_f = sends_f, recvs_f
        self.rows, self.cols = grad.shape[-2:]
        self.part = self.cols // 2
        self.core = lax.axis_index("core")
        self.xl = lax.axis_index("xl")

    def piece(self, stage, shift, which=None):
        axis = self.order[stage]
        left = [a for a in "zxy" if a in self.order[stage:]]
        source = self.grad if stage == 0 else self.sums[stage - 1]
        at = lax.rem(self.pos[axis] + shift + RING, RING)
        index = tuple(at if a == axis else slice(None) for a in left) + (slice(None),)
        if which is None:
            return source.at[index + (slice(None),)]
        return source.at[index + (pl.ds(which * self.part, self.part),)]

    def box(self, stage, kind):
        return self.boxes[stage].at[kind]

    def copy(self, stage, kind):
        src, step = {
            0: (lambda: self.piece(stage, 2, 0), 1),
            1: (lambda: self.piece(stage, 1, 1), 1),
            2: (lambda: self.piece(stage, -2, 1), -1),
            3: (lambda: self.piece(stage, -1, 0), -1),
            4: (lambda: self.box(stage, 0), 1),
            5: (lambda: self.box(stage, 2), -1),
        }[kind]
        return remote(
            src(),
            self.box(stage, kind),
            self.send.at[stage * 6 + kind],
            self.recv.at[stage * 6 + kind],
            neighbour(self.pos, self.order[stage], step),
        )

    def loads(self):
        for slot, (shift, which) in enumerate(((1, 0), (-1, 1), (0, 0), (0, 1))):
            yield pltpu.make_async_copy(
                self.piece(0, shift, which), self.own.at[slot], self.local.at[slot]
            )

    def begin(self, stage):
        for kind in range(4):
            self.copy(stage, kind).start()
        if stage == 0:
            for load in self.loads():
                load.start()

    def term(self, stage, slot):
        if stage == 0:
            return self.own.at[slot]
        shift, which = ((1, 0), (-1, 1), (0, 0), (0, 1))[slot]
        return self.piece(stage, shift, which)

    def add(self, stage, target, terms):
        lead = 2 - stage

        def one(index):
            total = terms[0][index].astype(jnp.float32)
            for t in terms[1:]:
                total = total + t[index].astype(jnp.float32)
            target[index] = total.astype(target.dtype)

        if lead == 0:
            one((slice(None), slice(None)))
            return

        def body(i, carry):
            where = (i // RING, lax.rem(i, RING)) if lead == 2 else (i,)
            one(where + (slice(None), slice(None)))
            return carry

        lax.fori_loop(0, RING**lead, body, 0)

    def onward(self, stage):
        if stage == 0:
            for load in self.loads():
                load.wait()
        for slot, kind in ((0, 0), (1, 2)):
            self.copy(stage, kind).wait_recv()
            box = self.box(stage, kind)
            self.add(stage, box, (box, self.term(stage, slot)))
            self.copy(stage, 4 + slot).start()

    def finish(self, stage):
        for kind in (1, 3, 4, 5):
            self.copy(stage, kind).wait_recv()
        lead = (slice(None),) * (3 - stage)
        for which, kinds in ((0, (3, 4)), (1, (1, 5))):
            target = self.sums[stage].at[lead + (pl.ds(which * self.part, self.part),)]
            self.add(
                stage,
                target,
                (self.term(stage, 2 + which),) + tuple(self.box(stage, k) for k in kinds),
            )

    def across_first(self):
        return self.order[0] != "y"

    def block(self, shift):
        yi = lax.rem(self.pos["y"] + shift + RING, RING)
        xs = slice(None) if self.across_first() else self.xl
        return self.final.at[self.core, xs, yi]

    def spread(self, kind, own=False):
        sems = (self.sends_f.at[kind], self.recvs_f.at[kind])
        if kind == 5:
            whole = self.final.at[self.core]
            return remote(whole, whole, *sems, {"core": 1 - self.core})
        if kind == 4:
            if self.across_first():
                dst = self.final.at[self.core, self.xl, self.pos["y"]]
                src = self.sums[2]
            else:
                src = dst = self.final.at[self.core, self.xl]
            return remote(src, dst, *sems, {"xl": 1 - self.xl})
        target = neighbour(self.pos, "y", 1 if kind % 2 == 0 else -1)
        if kind < 2:
            dst = self.block(0)
            src = dst if self.across_first() else self.sums[2]
            return remote(src, dst, *sems, target)
        ref = self.block(-1 if kind == 2 else 1)
        lead = (slice(None),) * (len(ref.shape) - 1)
        ref = ref.at[lead + (pl.ds((kind - 2) * self.part, self.part),)]
        return remote(ref, ref, *sems, target)

    def spread_arrives(self, kind):
        sems = (self.sends_f.at[kind], self.recvs_f.at[kind])
        if kind == 5:
            ref = self.final.at[1 - self.core]
        elif kind == 4:
            ref = self.final.at[self.core, 1 - self.xl]
            if self.across_first():
                ref = ref.at[self.pos["y"]]
        elif kind < 2:
            ref = self.block(-1 if kind == 0 else 1)
        else:
            ref = self.block(2)
            lead = (slice(None),) * (len(ref.shape) - 1)
            ref = ref.at[lead + (pl.ds((kind - 2) * self.part, self.part),)]
        remote(ref, ref, *sems, {"core": 1 - self.core}).wait_recv()

    def keep(self):
        return pltpu.make_async_copy(
            self.sums[2],
            self.final.at[self.core, self.xl, self.pos["y"]],
            self.local.at[4],
        )

    def publish(self, step):
        if step == 0:
            self.keep().start()
            for kind in (4,) if self.across_first() else (0, 1):
                self.spread(kind).start()
            self.keep().wait()
        elif self.across_first():
            if step == 1:
                self.spread_arrives(4)
                for kind in (0, 1):
                    self.spread(kind).start()
            elif step == 2:
                for kind in (0, 1):
                    self.spread_arrives(kind)
                    self.spread(kind + 2).start()
            elif step == 3:
                for kind in (2, 3):
                    self.spread_arrives(kind)
        else:
            if step == 1:
                for kind in (0, 1):
                    self.spread_arrives(kind)
                    self.spread(kind + 2).start()
            elif step == 2:
                for kind in (2, 3):
                    self.spread_arrives(kind)
                self.spread(4).start()
            elif step == 3:
                self.spread_arrives(4)
        if step == 3:
            self.spread(5).start()
        if step == 4:
            self.spread_arrives(5)

    def drain(self):
        for stage in range(3):
            for kind in range(6):
                self.copy(stage, kind).wait_send()
        for kind in range(6):
            self.spread(kind).wait_send()


def scatter_kernel(count, moved, *refs):
    grads, wholes = refs[:count], refs[count : count + moved]
    refs = refs[count + moved :]
    finals, parts = refs[:count], refs[count : count + moved]
    refs = refs[count + moved :]
    bufs, refs = refs[: 7 * count], refs[7 * count :]
    send, recv, local, sends_f, recvs_f, send_t, recv_t, local_t = refs
    pos = positions()
    core = lax.axis_index("core")
    greet(pos, True)
    streams = [
        Scatter(
            pos,
            ORDERS[m % 4],
            grads[m],
            bufs[7 * m : 7 * m + 7],
            finals[m],
            send.at[m],
            recv.at[m],
            local.at[m],
            sends_f.at[m],
            recvs_f.at[m],
        )
        for m in range(count)
    ]
    for s in streams:
        s.begin(0)
    sender = pos["z"] // 2 == core
    slot = lax.rem(pos["z"], 2)

    def homeward(a, q):
        return remote(
            wholes[a].at[q], parts[a].at[slot], send_t.at[a, q], recv_t.at[a, slot], {"z": q}
        )

    def staying(a):
        return pltpu.make_async_copy(wholes[a].at[pos["z"]], parts[a].at[slot], local_t.at[a])

    for a in range(moved):
        for q in range(RING):

            @pl.when(sender & (pos["z"] == q))
            def _():
                staying(a).start()

            @pl.when(sender & (pos["z"] != q))
            def _():
                homeward(a, q).start()

    for stage in range(3):
        for s in streams:
            s.onward(stage)
        for s in streams:
            s.finish(stage)
            if stage < 2:
                s.begin(stage + 1)
            else:
                s.publish(0)
    for step in range(1, 5):
        for s in streams:
            s.publish(step)
    for s in streams:
        s.drain()
    for a in range(moved):
        for q in range(RING):

            @pl.when(sender & (pos["z"] == q))
            def _():
                staying(a).wait()

            @pl.when(sender & (pos["z"] != q))
            def _():
                homeward(a, q).wait_send()

        for b in range(2):

            @pl.when(2 * core + b != pos["z"])
            def _():
                remote(
                    parts[a].at[b],
                    parts[a].at[b],
                    send_t.at[a, 0],
                    recv_t.at[a, b],
                    {"z": lax.rem(pos["z"] + 1, RING)},
                ).wait_recv()


def scatter_all(grads, wholes):
    count, moved = len(grads), len(wholes)
    anyspec = pl.BlockSpec(memory_space=pl.ANY)
    shapes = [jax.ShapeDtypeStruct((2, 2, RING) + g.shape[3:], g.dtype) for g in grads]
    shapes += [jax.ShapeDtypeStruct((2,) + w.shape[1:], w.dtype) for w in wholes]
    dma = pltpu.SemaphoreType.DMA
    scratch = []
    for g in grads:
        r, c = g.shape[3:]
        scratch.append(pltpu.VMEM((4, RING, RING, r, c // 2), g.dtype))
        for lead in ((RING, RING), (RING,), ()):
            scratch.append(pltpu.VMEM((6,) + lead + (r, c // 2), g.dtype))
        for lead in ((RING, RING), (RING,), ()):
            scratch.append(pltpu.VMEM(lead + (r, c), g.dtype))
    out = pl.pallas_call(
        functools.partial(scatter_kernel, count, moved),
        out_shape=shapes,
        in_specs=[anyspec] * (count + moved),
        out_specs=[anyspec] * (count + moved),
        scratch_shapes=scratch
        + [
            dma((count, 18)),
            dma((count, 18)),
            dma((count, 5)),
            dma((count, 6)),
            dma((count, 6)),
            dma((moved, RING)),
            dma((moved, 2)),
            dma((moved,)),
        ],
        compiler_params=pltpu.CompilerParams(
            collective_id=1, has_side_effects=True, vmem_limit_bytes=62 * 1024 * 1024
        ),
        name="scatter_all",
    )(*grads, *wholes)
    return out[:count], out[count:]


NORM_EPS = 1e-05
GELU_COEF = 0.7978845608028654
CUBIC_COEF = 0.044715
HEAD_DIM = 64
LOW = jnp.bfloat16
F32 = jnp.float32


def dot(left, right, dims=((1,), (0,))):
    return lax.dot_general(left, right, (dims, ((), ())), preferred_element_type=F32)


def head_probs(q, k, allowed, scale):
    scores = jnp.where(allowed, dot(q, k, ((1,), (1,))) * scale, -jnp.inf)
    top = jnp.max(scores, axis=-1, keepdims=True)
    lse = top + jnp.log(jnp.sum(jnp.exp(scores - top), axis=-1, keepdims=True))
    return jnp.exp(scores - lse)


def allowed_pairs(seg_col, seg_row):
    length = seg_col.shape[0]
    row = lax.broadcasted_iota(jnp.int32, (length, length), 0)
    col = lax.broadcasted_iota(jnp.int32, (length, length), 1)
    return (row >= col) & (seg_col == seg_row)


def attention_kernel(qkv_ref, seg_col_ref, seg_row_ref, attn_ref):
    width = attn_ref.shape[1]
    scale = 1.0 / math.sqrt(HEAD_DIM)
    allowed = allowed_pairs(seg_col_ref[...], seg_row_ref[...])
    for h in range(width // HEAD_DIM):
        q, k, v = (
            qkv_ref[:, pl.ds(t * width + h * HEAD_DIM, HEAD_DIM)] for t in range(3)
        )
        probs = head_probs(q, k, allowed, scale).astype(LOW)
        attn_ref[:, pl.ds(h * HEAD_DIM, HEAD_DIM)] = dot(probs, v).astype(LOW)


def attention_back_kernel(qkv_ref, attn_ref, grad_ref, seg_col_ref, seg_row_ref, out_ref, sum_ref):
    width = attn_ref.shape[1]
    scale = 1.0 / math.sqrt(HEAD_DIM)
    allowed = allowed_pairs(seg_col_ref[...], seg_row_ref[...])
    for h in range(width // HEAD_DIM):
        q, k, v = (
            qkv_ref[:, pl.ds(t * width + h * HEAD_DIM, HEAD_DIM)] for t in range(3)
        )
        here = pl.ds(h * HEAD_DIM, HEAD_DIM)
        d_attn = grad_ref[:, here]
        full = head_probs(q, k, allowed, scale)
        delta = jnp.sum(
            d_attn.astype(F32) * attn_ref[:, here].astype(F32), axis=-1, keepdims=True
        )
        d_scores = (full * (dot(d_attn, v, ((1,), (1,))) - delta)).astype(LOW)
        terms = (
            dot(d_scores, k) * scale,
            dot(d_scores, q, ((0,), (0,))) * scale,
            dot(full.astype(LOW), d_attn, ((0,), (0,))),
        )
        for t, term in enumerate(terms):
            place = pl.ds(t * width + h * HEAD_DIM, HEAD_DIM)
            out_ref[:, place] = term.astype(LOW)
            sum_ref[:, place] = jnp.sum(term, axis=0, keepdims=True)


def attention(qkv, seg_col, seg_row):
    length, width = qkv.shape[0], qkv.shape[1] // 3
    return pl.pallas_call(
        attention_kernel,
        out_shape=jax.ShapeDtypeStruct((length, width), LOW),
        name="attention",
    )(qkv, seg_col, seg_row)


def attention_back(qkv, attn, d_attn, seg_col, seg_row):
    length, width = attn.shape
    return pl.pallas_call(
        attention_back_kernel,
        out_shape=(
            jax.ShapeDtypeStruct((length, 3 * width), LOW),
            jax.ShapeDtypeStruct((1, 3 * width), F32),
        ),
        name="attention_back",
    )(qkv, attn, d_attn, seg_col, seg_row)


def layer_norm(state, gain, shift):
    center = state - jnp.mean(state, axis=-1, keepdims=True)
    factor = lax.rsqrt(jnp.mean(center * center, axis=-1, keepdims=True) + NORM_EPS)
    normed = center * factor
    return normed, factor, (normed * gain + shift).astype(LOW)


def norm_backward(d_act, normed, factor, gain):
    d_norm = d_act * gain
    return factor * (
        d_norm
        - jnp.mean(d_norm, axis=-1, keepdims=True)
        - normed * jnp.mean(d_norm * normed, axis=-1, keepdims=True)
    )


def gelu_pair(pre_act):
    cubic = pre_act * pre_act * pre_act
    tangent = jnp.tanh(GELU_COEF * (pre_act + CUBIC_COEF * cubic))
    gelu_value = 0.5 * pre_act * (1.0 + tangent)
    gelu_slope = 0.5 * (1.0 + tangent) + 0.5 * pre_act * (1.0 - tangent * tangent) * GELU_COEF * (
        1.0 + 3.0 * CUBIC_COEF * pre_act * pre_act
    )
    return gelu_value, gelu_slope


def pair_sum(partial):
    return partial + lax.ppermute(partial, "core", ((0, 1), (1, 0)))


def pick(array, at, axis):
    return lax.dynamic_index_in_dim(array, at, axis, keepdims=False)


def per_device(
    inputs,
    segment_ids,
    weight_qkv,
    weight_out,
    weight_up,
    weight_down,
    bias_qv,
    bias_out,
    bias_up,
    bias_down,
    gain_one,
    shift_one,
    gain_two,
    shift_two,
    cotangent,
):
    layers, rows, _ = weight_qkv.shape
    width = inputs.shape[-1]
    inner = weight_up.shape[-1]
    length = inputs.shape[1] * RING
    core = lax.axis_index("core")
    sub = lax.axis_index("xl") * 4 + lax.axis_index("y")
    owns = []
    for l in range(layers):
        up = pick(weight_up[l].reshape(8, rows // 8, 8, 2, inner // 16), sub, 0)
        owns.append(pick(up, core, 2).reshape(rows // 8, inner // 2))
        down = weight_down[l].reshape(2, 8, inner // 128, width)
        owns.append(pick(pick(down, core, 0), sub, 0))
        qkv = pick(weight_qkv[l].reshape(8, rows // 8, 24, 2, HEAD_DIM), sub, 0)
        owns.append(pick(qkv, core, 2).reshape(rows // 8, 3 * width // 2))
        out = weight_out[l].reshape(2, 8, rows // 16, width)
        owns.append(pick(pick(out, core, 0), sub, 0))
    vectors = (bias_qv, bias_out, bias_up, bias_down, gain_one, shift_one, gain_two, shift_two)
    sizes = [v.shape[1] for v in vectors]
    total = sum(sizes)
    packed = jnp.concatenate(vectors, axis=1).reshape(8, layers * total // 8)
    packed = jnp.pad(pick(packed, sub, 0), (0, 2048 - layers * total // 8))
    owns.append(packed.reshape(8, 256))
    segs = jnp.pad(segment_ids.astype(F32), ((0, 0), (0, 1024 - segment_ids.shape[1])))
    fulls, wholes = gather_all(owns, [inputs, cotangent, segs.reshape(2, 8, 128)])
    state = wholes[0].reshape(length, width)
    grad_state = wholes[1].reshape(length, width)
    seg = wholes[2].reshape(RING, 1024)[:, : length // RING].reshape(length)
    seg_col, seg_row = seg[:, None], seg[None, :]
    packed = fulls[-1].reshape(8, 8, 2048)[:, :, : layers * total // 8].reshape(8, layers, total)
    packed = packed.astype(F32)
    params = []
    for l in range(layers):
        weights = [w.reshape(-1, w.shape[-1]) for w in fulls[4 * l : 4 * l + 4]]
        offset, vecs = 0, []
        for size in sizes:
            vecs.append(packed[:, l, offset : offset + size].reshape(8 * size))
            offset += size
        b_qv = pick(vecs[0].reshape(2, 8, 2, HEAD_DIM), core, 2).reshape(2, width // 2)
        b_qkv = jnp.concatenate([b_qv[0], jnp.zeros((width // 2,), F32), b_qv[1]])
        b_up = pick(vecs[2].reshape(8, 2, inner // 16), core, 1).reshape(inner // 2)
        params.append((weights, b_qkv, vecs[1], b_up, vecs[3], vecs[4:]))
    records = []
    for l in range(layers):
        (w_up, w_down, w_qkv, w_out), b_qkv, b_out, b_up, b_down, (g1, s1, g2, s2) = params[l]
        norm_one, factor_one, act_one = layer_norm(state, g1, s1)
        qkv = (dot(act_one, w_qkv) + b_qkv).astype(LOW)
        attn = attention(qkv, seg_col, seg_row)
        middle = state + pair_sum(dot(attn, w_out)) + b_out
        norm_two, factor_two, act_two = layer_norm(middle, g2, s2)
        gelu_value, gelu_slope = gelu_pair(dot(act_two, w_up) + b_up)
        hidden = gelu_value.astype(LOW)
        state = middle + pair_sum(dot(hidden, w_down)) + b_down
        records.append(
            (norm_one, factor_one, act_one, qkv, attn, norm_two, factor_two, act_two, gelu_slope, hidden)
        )
    grads, small = [None] * layers, [None] * layers
    first = (core == 0).astype(F32)
    for l in reversed(range(layers)):
        (w_up, w_down, w_qkv, w_out), _, _, _, _, (g1, _, g2, _) = params[l]
        norm_one, factor_one, act_one, qkv, attn, norm_two, factor_two, act_two, gelu_slope, hidden = records[l]
        grad_low = grad_state.astype(LOW)
        gb_down = jnp.sum(grad_state, axis=0)
        d_pre = dot(grad_low, w_down, ((1,), (1,))) * gelu_slope
        d_pre_low = d_pre.astype(LOW)
        gb_up = jnp.sum(d_pre, axis=0)
        d_act_two = pair_sum(dot(d_pre_low, w_up, ((1,), (1,))))
        gg_two = jnp.sum(d_act_two * norm_two, axis=0)
        gs_two = jnp.sum(d_act_two, axis=0)
        grad_middle = grad_state + norm_backward(d_act_two, norm_two, factor_two, g2)
        grad_attn_low = grad_middle.astype(LOW)
        gb_out = jnp.sum(grad_middle, axis=0)
        d_attn = dot(grad_attn_low, w_out, ((1,), (1,))).astype(LOW)
        d_qkv, gb_qkv = attention_back(qkv, attn, d_attn, seg_col, seg_row)
        d_act_one = pair_sum(dot(d_qkv, w_qkv, ((1,), (1,))))
        gg_one = jnp.sum(d_act_one * norm_one, axis=0)
        gs_one = jnp.sum(d_act_one, axis=0)
        grad_state = grad_middle + norm_backward(d_act_one, norm_one, factor_one, g1)
        tokens = ((0,), (0,))
        grads[l] = [
            dot(act_two, d_pre_low, tokens),
            dot(hidden, grad_low, tokens),
            dot(act_one, d_qkv, tokens),
            dot(attn, grad_attn_low, tokens),
        ]
        gb_qkv = gb_qkv.reshape(3, 8, HEAD_DIM)
        mine = lambda v, axis: jnp.stack(
            [jnp.where(core == c, v, 0.0) for c in range(2)], axis=axis
        )
        gb_qv = mine(jnp.stack([gb_qkv[0], gb_qkv[2]]), 2)
        gb_up = mine(gb_up.reshape(8, inner // 16), 1)
        parts = (gb_qv, gb_out * first, gb_up, gb_down * first)
        parts += (gg_one * first, gs_one * first, gg_two * first, gs_two * first)
        small[l] = jnp.concatenate(
            [v.reshape(8, size) for v, size in zip(parts, sizes)], axis=1
        )
    small = jnp.stack(small, axis=1).reshape(8, 8, layers * total // 8)
    small = jnp.pad(small, ((0, 0), (0, 0), (0, 2048 - layers * total // 8)))
    pieces = [
        g.astype(LOW).reshape(RING, RING, RING, -1, g.shape[-1]) for l in range(layers) for g in grads[l]
    ]
    pieces.append(small.astype(LOW).reshape(RING, RING, RING, 8, 256))
    finals, parts = scatter_all(
        pieces,
        [state.reshape(RING, length // RING, width), grad_state.reshape(RING, length // RING, width)],
    )
    outs = [[], [], [], []]
    for l in range(layers):
        up, down, qkv, out = (f.astype(F32) for f in finals[4 * l : 4 * l + 4])
        up = up.reshape(2, rows, 8, inner // 16).transpose(1, 2, 0, 3)
        outs[2].append(up.reshape(rows, inner))
        outs[3].append(down.reshape(inner // 8, width))
        qkv = qkv.reshape(2, rows, 24, HEAD_DIM).transpose(1, 2, 0, 3)
        outs[0].append(qkv.reshape(rows, 3 * width))
        outs[1].append(out.reshape(rows, width))
    small = jnp.sum(finals[-1].astype(F32), axis=0).reshape(8, 2048)[:, : layers * total // 8]
    small = small.reshape(layers, total)
    ends = []
    offset = 0
    for size in sizes:
        ends.append(small[:, offset : offset + size])
        offset += size
    return (parts[0], parts[1]) + tuple(jnp.stack(o) for o in outs) + tuple(ends)


def solution(mesh):
    torus = Mesh(mesh.devices.reshape(4, 2, 4, 2, 2), AXES)
    tokens = P(("xh", "y", "xl", "core"), "z", None)
    weight = P(None, ("z", "xh"), None)
    vector = P(None, ("z", "xh"))
    return jax.shard_map(
        per_device,
        mesh=torus,
        in_specs=(tokens, P(("xh", "y", "xl", "core"), "z")) + (weight,) * 4 + (vector,) * 8 + (tokens,),
        out_specs=(tokens, tokens) + (weight,) * 4 + (vector,) * 8,
        check_vma=False,
    )
```

```python
import functools
import math

import jax
import jax.numpy as jnp
from jax import lax
from jax.experimental import pallas as pl
from jax.experimental.pallas import tpu as pltpu
from jax.sharding import Mesh
from jax.sharding import PartitionSpec as P

AXES = ("z", "xh", "y", "xl", "core")
RING = 4
ANY = pl.BlockSpec(memory_space=pl.ANY)
VMEM = pl.BlockSpec(memory_space=pltpu.VMEM)
DMA = pltpu.SemaphoreType.DMA
ORDERS = ("xyz", "zxy", "yzx", "yzx")


def positions():
    return {
        "z": lax.axis_index("z"),
        "x": lax.axis_index("xh") * 2 + lax.axis_index("xl"),
        "y": lax.axis_index("y"),
    }


def neighbour(pos, axis, step):
    at = lax.rem(pos[axis] + step + RING, RING)
    if axis == "x":
        return {"xh": at // 2, "xl": lax.rem(at, 2)}
    return {axis: at}


def remote(src, dst, send, recv, target):
    return pltpu.make_async_remote_copy(
        src_ref=src,
        dst_ref=dst,
        send_sem=send,
        recv_sem=recv,
        device_id=target,
        device_id_type=pl.DeviceIdType.MESH,
    )


def greet(pos, with_column):
    barrier = pltpu.get_barrier_semaphore()
    targets = [neighbour(pos, axis, step) for axis in "xyz" for step in (1, -1)]
    if with_column:
        targets.append(neighbour(pos, "z", 2))
    targets.append({"core": 1 - lax.axis_index("core")})
    for target in targets:
        pl.semaphore_signal(
            barrier, inc=1, device_id=target, device_id_type=pl.DeviceIdType.MESH
        )
    pl.semaphore_wait(barrier, len(targets))


def half(ref, which, rows, cols):
    lead = (slice(None),) * (len(ref.shape) - 2)
    if rows % 16 == 0:
        return ref.at[lead + (pl.ds(which * (rows // 2), rows // 2), slice(None))]
    return ref.at[lead + (slice(None), pl.ds(which * (cols // 2), cols // 2))]


class Gather:
    def __init__(self, pos, order, own, full, send, recv):
        self.pos, self.order, self.own, self.full = pos, order, own, full
        self.send, self.recv = send, recv
        self.rows, self.cols = full.shape[-2:]

    def view(self, stage, shift):
        index = {}
        for place, axis in enumerate(self.order):
            if place < stage:
                index[axis] = slice(None)
            elif place == stage:
                index[axis] = lax.rem(self.pos[axis] + shift + RING, RING)
            else:
                index[axis] = self.pos[axis]
        return self.full.at[index["z"], index["x"], index["y"]]

    def copy(self, stage, kind):
        axis = self.order[stage]
        sems = (self.send.at[stage * 4 + kind], self.recv.at[stage * 4 + kind])
        target = neighbour(self.pos, axis, 1 if kind % 2 == 0 else -1)
        if kind < 2:
            src = self.own if stage == 0 else self.view(stage, 0)
            return remote(src, self.view(stage, 0), *sems, target)
        piece = half(self.view(stage, -1 if kind == 2 else 1), kind - 2, self.rows, self.cols)
        return remote(piece, piece, *sems, target)

    def arrive(self, stage, kind):
        sems = (self.send.at[stage * 4 + kind], self.recv.at[stage * 4 + kind])
        axis = self.order[stage]
        if kind < 2:
            piece = self.view(stage, -1 if kind == 0 else 1)
        else:
            piece = half(self.view(stage, 2), kind - 2, self.rows, self.cols)
        remote(piece, piece, *sems, neighbour(self.pos, axis, 1)).wait_recv()

    def begin(self, stage):
        for kind in (0, 1):
            self.copy(stage, kind).start()

    def onward(self, stage):
        for kind in (0, 1):
            self.arrive(stage, kind)
            self.copy(stage, kind + 2).start()

    def finish(self, stage):
        for kind in (2, 3):
            self.arrive(stage, kind)

    def drain(self, stages):
        for stage in stages:
            for kind in range(4):
                self.copy(stage, kind).wait_send()


class Sequences:
    def __init__(self, pos, parts, wholes, sems):
        self.pos, self.parts, self.wholes = pos, parts, wholes
        self.send, self.recv, self.core_send, self.core_recv, self.local = sems
        self.core = lax.axis_index("core")
        self.receiver = pos["z"] // 2 == self.core

    def outward(self, a, b, home):
        return remote(
            self.parts[a].at[b],
            self.wholes[a].at[self.pos["z"]],
            self.send.at[a, b],
            self.recv.at[a, self.pos["z"]],
            {"z": home},
        )

    def crossing(self, a, q):
        piece = self.wholes[a].at[q]
        return remote(
            piece, piece, self.core_send.at[a, q], self.core_recv.at[a, q], {"core": 1 - self.core}
        )

    def staying(self, a, b):
        return pltpu.make_async_copy(
            self.parts[a].at[b], self.wholes[a].at[self.pos["z"]], self.local.at[a]
        )

    def begin(self):
        for a in range(len(self.parts)):
            for b in range(2):
                home = 2 * self.core + b

                @pl.when(home == self.pos["z"])
                def _():
                    self.staying(a, b).start()

                @pl.when(home != self.pos["z"])
                def _():
                    self.outward(a, b, home).start()

    def cross(self):
        @pl.when(self.receiver)
        def _():
            for a in range(len(self.parts)):
                for q in range(RING):

                    @pl.when(q == self.pos["z"])
                    def _():
                        self.staying(a, 0).wait()

                    @pl.when(q != self.pos["z"])
                    def _():
                        piece = self.wholes[a].at[q]
                        remote(
                            piece,
                            piece,
                            self.send.at[a, 0],
                            self.recv.at[a, q],
                            {"z": lax.rem(self.pos["z"] + 1, RING)},
                        ).wait_recv()

                    self.crossing(a, q).start()

    def drain(self):
        for a in range(len(self.parts)):
            for b in range(2):
                home = 2 * self.core + b

                @pl.when(home != self.pos["z"])
                def _():
                    self.outward(a, b, lax.rem(self.pos["z"] + 1, RING)).wait_send()

            for q in range(RING):

                @pl.when(self.receiver)
                def _():
                    self.crossing(a, q).wait_send()

                @pl.when(jnp.logical_not(self.receiver))
                def _():
                    self.crossing(a, q).wait_recv()


def sequence_scratch(moved):
    sems = [DMA((moved, 2)), DMA((moved, RING)), DMA((moved, RING)), DMA((moved, RING)), DMA((moved,))]
    return sems if moved else []


def sequence_shapes(parts):
    return [jax.ShapeDtypeStruct((RING,) + p.shape[1:], p.dtype) for p in parts]


def gather_kernel(count, whole, moved, *refs):
    owns, parts = refs[:count], refs[count : count + moved]
    refs = refs[count + moved :]
    fulls, wholes = refs[:count], refs[count : count + moved]
    send, recv, local = refs[count + moved : count + moved + 3]
    pos = positions()
    greet(pos, True)
    sequences = Sequences(pos, parts, wholes, refs[count + moved + 3 :])
    streams, keeps = [], []
    for m in range(count):
        keeps.append(
            pltpu.make_async_copy(
                owns[m], fulls[m].at[pos["z"], pos["x"], pos["y"]], local.at[m]
            )
        )
        streams.append(
            Gather(pos, ORDERS[m % whole % 4], owns[m], fulls[m], send.at[m], recv.at[m])
        )
    for keep in keeps:
        keep.start()
    for s in streams:
        s.begin(0)
    sequences.begin()
    for stage in range(3):
        running = streams if stage < 2 else streams[:whole]
        for s in running:
            s.onward(stage)
        if stage == 0:
            for keep in keeps:
                keep.wait()
        for m, s in enumerate(running):
            s.finish(stage)
            if stage == 0 or (stage == 1 and m < whole):
                s.begin(stage + 1)
        if stage == 1:
            sequences.cross()
    for m, s in enumerate(streams):
        s.drain(range(3 if m < whole else 2))
    sequences.drain()


def gather_all(owns, begun, parts):
    count, moved = len(owns) + len(begun), len(parts)
    shapes = [
        jax.ShapeDtypeStruct((RING, RING, RING) + o.shape, o.dtype) for o in owns + begun
    ]
    out = pl.pallas_call(
        functools.partial(gather_kernel, count, len(owns), moved),
        out_shape=shapes + sequence_shapes(parts),
        in_specs=[ANY] * (count + moved),
        out_specs=[ANY] * (count + moved),
        scratch_shapes=[DMA((count, 12)), DMA((count, 12)), DMA((count,))]
        + sequence_scratch(moved),
        compiler_params=pltpu.CompilerParams(collective_id=0, has_side_effects=True),
        name="gather_all",
    )(*owns, *begun, *parts)
    return out[: len(owns)], out[len(owns) : count], out[count:]


def scatter_scratch(ends, kinds, stages):
    scratch = []
    for (r, c), kind in zip(ends, kinds):
        if 0 in stages:
            scratch.append(pltpu.VMEM((4, RING, RING, r, c // 2), kind))
        for stage in stages:
            scratch.append(pltpu.VMEM((6,) + (RING,) * (2 - stage) + (r, c // 2), kind))
        if len(stages) > 1:
            for stage in stages:
                scratch.append(pltpu.VMEM((RING,) * (2 - stage) + (r, c), kind))
    return scratch


class Scatter:
    def __init__(self, pos, order, grad, own, boxes, sums, send, recv, local):
        self.pos, self.order, self.grad = pos, order, grad
        self.own, self.boxes, self.sums = own, boxes, sums
        self.send, self.recv, self.local = send, recv, local
        self.part = sums[0].shape[-1] // 2

    def piece(self, stage, shift, which=None):
        axis = self.order[stage]
        left = [a for a in "zxy" if a in self.order[stage:]]
        source = self.grad if stage == 0 else self.sums[stage - 1]
        at = lax.rem(self.pos[axis] + shift + RING, RING)
        index = tuple(at if a == axis else slice(None) for a in left) + (slice(None),)
        if which is None:
            return source.at[index + (slice(None),)]
        return source.at[index + (pl.ds(which * self.part, self.part),)]

    def box(self, stage, kind):
        return self.boxes[stage].at[kind]

    def copy(self, stage, kind):
        src, step = {
            0: (lambda: self.piece(stage, 2, 0), 1),
            1: (lambda: self.piece(stage, 1, 1), 1),
            2: (lambda: self.piece(stage, -2, 1), -1),
            3: (lambda: self.piece(stage, -1, 0), -1),
            4: (lambda: self.box(stage, 0), 1),
            5: (lambda: self.box(stage, 2), -1),
        }[kind]
        return remote(
            src(),
            self.box(stage, kind),
            self.send.at[stage * 6 + kind],
            self.recv.at[stage * 6 + kind],
            neighbour(self.pos, self.order[stage], step),
        )

    def loads(self):
        for slot, (shift, which) in enumerate(((1, 0), (-1, 1), (0, 0), (0, 1))):
            yield pltpu.make_async_copy(
                self.piece(0, shift, which), self.own.at[slot], self.local.at[slot]
            )

    def begin(self, stage):
        for kind in range(4):
            self.copy(stage, kind).start()
        if stage == 0:
            for load in self.loads():
                load.start()

    def term(self, stage, slot):
        if stage == 0:
            return self.own.at[slot]
        shift, which = ((1, 0), (-1, 1), (0, 0), (0, 1))[slot]
        return self.piece(stage, shift, which)

    def add(self, stage, target, terms):
        lead = 2 - stage

        def one(index):
            total = terms[0][index].astype(jnp.float32)
            for t in terms[1:]:
                total = total + t[index].astype(jnp.float32)
            target[index] = total.astype(target.dtype)

        if lead == 0:
            one((slice(None), slice(None)))
            return

        def body(i, carry):
            where = (i // RING, lax.rem(i, RING)) if lead == 2 else (i,)
            one(where + (slice(None), slice(None)))
            return carry

        lax.fori_loop(0, RING**lead, body, 0)

    def onward(self, stage):
        if stage == 0:
            for load in self.loads():
                load.wait()
        for slot, kind in ((0, 0), (1, 2)):
            self.copy(stage, kind).wait_recv()
            box = self.box(stage, kind)
            self.add(stage, box, (box, self.term(stage, slot)))
            self.copy(stage, 4 + slot).start()

    def finish(self, stage):
        for kind in (1, 3, 4, 5):
            self.copy(stage, kind).wait_recv()
        lead = (slice(None),) * (3 - stage)
        for which, kinds in ((0, (3, 4)), (1, (1, 5))):
            target = self.sums[stage].at[lead + (pl.ds(which * self.part, self.part),)]
            self.add(
                stage,
                target,
                (self.term(stage, 2 + which),) + tuple(self.box(stage, k) for k in kinds),
            )

    def drain(self, stages):
        for stage in stages:
            for kind in range(6):
                self.copy(stage, kind).wait_send()


class Publish:
    def __init__(self, pos, order, source, final, sends, recvs, local):
        self.pos, self.order, self.source, self.final = pos, order, source, final
        self.sends_f, self.recvs_f, self.local = sends, recvs, local
        self.core, self.xl = lax.axis_index("core"), lax.axis_index("xl")
        self.part = source.shape[-1] // 2

    def across_first(self):
        return self.order[0] != "y"

    def block(self, shift):
        yi = lax.rem(self.pos["y"] + shift + RING, RING)
        xs = slice(None) if self.across_first() else self.xl
        return self.final.at[self.core, xs, yi]

    def spread(self, kind, own=False):
        sems = (self.sends_f.at[kind], self.recvs_f.at[kind])
        if kind == 5:
            whole = self.final.at[self.core]
            return remote(whole, whole, *sems, {"core": 1 - self.core})
        if kind == 4:
            if self.across_first():
                dst = self.final.at[self.core, self.xl, self.pos["y"]]
                src = self.source
            else:
                src = dst = self.final.at[self.core, self.xl]
            return remote(src, dst, *sems, {"xl": 1 - self.xl})
        target = neighbour(self.pos, "y", 1 if kind % 2 == 0 else -1)
        if kind < 2:
            dst = self.block(0)
            src = dst if self.across_first() else self.source
            return remote(src, dst, *sems, target)
        ref = self.block(-1 if kind == 2 else 1)
        lead = (slice(None),) * (len(ref.shape) - 1)
        ref = ref.at[lead + (pl.ds((kind - 2) * self.part, self.part),)]
        return remote(ref, ref, *sems, target)

    def spread_arrives(self, kind):
        sems = (self.sends_f.at[kind], self.recvs_f.at[kind])
        if kind == 5:
            ref = self.final.at[1 - self.core]
        elif kind == 4:
            ref = self.final.at[self.core, 1 - self.xl]
            if self.across_first():
                ref = ref.at[self.pos["y"]]
        elif kind < 2:
            ref = self.block(-1 if kind == 0 else 1)
        else:
            ref = self.block(2)
            lead = (slice(None),) * (len(ref.shape) - 1)
            ref = ref.at[lead + (pl.ds((kind - 2) * self.part, self.part),)]
        remote(ref, ref, *sems, {"core": 1 - self.core}).wait_recv()

    def keep(self):
        return pltpu.make_async_copy(
            self.source,
            self.final.at[self.core, self.xl, self.pos["y"]],
            self.local,
        )

    def publish(self, step):
        if step == 0:
            self.keep().start()
            for kind in (4,) if self.across_first() else (0, 1):
                self.spread(kind).start()
            self.keep().wait()
        elif self.across_first():
            if step == 1:
                self.spread_arrives(4)
                for kind in (0, 1):
                    self.spread(kind).start()
            elif step == 2:
                for kind in (0, 1):
                    self.spread_arrives(kind)
                    self.spread(kind + 2).start()
            elif step == 3:
                for kind in (2, 3):
                    self.spread_arrives(kind)
        else:
            if step == 1:
                for kind in (0, 1):
                    self.spread_arrives(kind)
                    self.spread(kind + 2).start()
            elif step == 2:
                for kind in (2, 3):
                    self.spread_arrives(kind)
                self.spread(4).start()
            elif step == 3:
                self.spread_arrives(4)
        if step == 3:
            self.spread(5).start()
        if step == 4:
            self.spread_arrives(5)

    def drain(self):
        for kind in range(6):
            self.spread(kind).wait_send()


def scatter_kernel(count, done, moved, *refs):
    grads, given, wholes = refs[:count], refs[count : count + done], refs[count + done : count + done + moved]
    refs = refs[count + done + moved :]
    finals, parts = refs[: count + done], refs[count + done : count + done + moved]
    refs = refs[count + done + moved :]
    bufs, more = refs[: 7 * count], refs[7 * count : 7 * count + 4 * done]
    send, recv, local, sends_f, recvs_f, keeps, send_t, recv_t, local_t = refs[7 * count + 4 * done :]
    pos = positions()
    core = lax.axis_index("core")
    greet(pos, True)
    streams = []
    for m in range(count):
        own = bufs[7 * m : 7 * m + 7]
        streams.append((ORDERS[m % 4], grads[m], own[0], own[1:4], own[4:7]))
    for m in range(done):
        own = more[4 * m : 4 * m + 4]
        streams.append((ORDERS[m % 4], None, None, (None,) + own[:2], (given[m],) + own[2:]))
    streams = [
        Scatter(pos, *args, send.at[m], recv.at[m], local.at[m]) for m, args in enumerate(streams)
    ]
    news = [
        Publish(pos, s.order, s.sums[2], finals[m], sends_f.at[m], recvs_f.at[m], keeps.at[m])
        for m, s in enumerate(streams)
    ]
    late, ahead = streams[:count], streams[count:]
    last, early = news[:count], news[count:]
    for s in ahead:
        s.begin(1)
    for s in late:
        s.begin(0)
    sender = pos["z"] // 2 == core
    slot = lax.rem(pos["z"], 2)

    def homeward(a, q):
        return remote(
            wholes[a].at[q], parts[a].at[slot], send_t.at[a, q], recv_t.at[a, slot], {"z": q}
        )

    def staying(a):
        return pltpu.make_async_copy(wholes[a].at[pos["z"]], parts[a].at[slot], local_t.at[a])

    for a in range(moved):
        for q in range(RING):

            @pl.when(sender & (pos["z"] == q))
            def _():
                staying(a).start()

            @pl.when(sender & (pos["z"] != q))
            def _():
                homeward(a, q).start()

    def move(group, places, stage):
        for s, n in zip(group, places):
            s.finish(stage)
            if stage < 2:
                s.begin(stage + 1)
            else:
                n.publish(0)

    def step(places, at):
        for n in places:
            n.publish(at)

    for s in ahead:
        s.onward(1)
    for s in late:
        s.onward(0)
    move(ahead, early, 1)
    move(late, last, 0)
    for s in ahead:
        s.onward(2)
    for s in late:
        s.onward(1)
    move(ahead, early, 2)
    move(late, last, 1)
    step(early, 1)
    for s in late:
        s.onward(2)
    step(early, 2)
    move(late, last, 2)
    step(early, 3)
    step(last, 1)
    step(last, 2)
    step(early, 4)
    step(last, 3)
    step(last, 4)
    for s in late:
        s.drain((0, 1, 2))
    for s in ahead:
        s.drain((1, 2))
    for n in news:
        n.drain()
    for a in range(moved):
        for q in range(RING):

            @pl.when(sender & (pos["z"] == q))
            def _():
                staying(a).wait()

            @pl.when(sender & (pos["z"] != q))
            def _():
                homeward(a, q).wait_send()

        for b in range(2):

            @pl.when(2 * core + b != pos["z"])
            def _():
                remote(
                    parts[a].at[b],
                    parts[a].at[b],
                    send_t.at[a, 0],
                    recv_t.at[a, b],
                    {"z": lax.rem(pos["z"] + 1, RING)},
                ).wait_recv()


def scatter_all(grads, given, wholes):
    count, done, moved = len(grads), len(given), len(wholes)
    ends = [g.shape[-2:] for g in grads + given]
    kinds = [g.dtype for g in grads + given]
    shapes = [jax.ShapeDtypeStruct((2, 2, RING) + e, k) for e, k in zip(ends, kinds)]
    shapes += [jax.ShapeDtypeStruct((2,) + w.shape[1:], w.dtype) for w in wholes]
    bufs = scatter_scratch(ends[:count], kinds[:count], (0, 1, 2))
    bufs += scatter_scratch(ends[count:], kinds[count:], (1, 2))
    out = pl.pallas_call(
        functools.partial(scatter_kernel, count, done, moved),
        out_shape=shapes,
        in_specs=[ANY] * count + [VMEM] * done + [ANY] * moved,
        out_specs=[ANY] * (count + done + moved),
        scratch_shapes=bufs
        + [
            DMA((count + done, 18)),
            DMA((count + done, 18)),
            DMA((count + done, 5)),
            DMA((count + done, 6)),
            DMA((count + done, 6)),
            DMA((count + done,)),
            DMA((moved, RING)),
            DMA((moved, 2)),
            DMA((moved,)),
        ],
        compiler_params=pltpu.CompilerParams(
            collective_id=1, has_side_effects=True, vmem_limit_bytes=62 * 1024 * 1024
        ),
        name="scatter_all",
    )(*grads, *given, *wholes)
    return out[: count + done], out[count + done :]


NORM_EPS = 1e-05
GELU_COEF = 0.7978845608028654
CUBIC_COEF = 0.044715
HEAD_DIM = 64
LOW = jnp.bfloat16
F32 = jnp.float32
TILE = 256
ROWS = 32
B_QV, B_OUT, B_UP, B_DOWN, G_ONE, S_ONE, G_TWO, S_TWO = range(8)


def dot(left, right, dims=((1,), (0,))):
    return lax.dot_general(left, right, (dims, ((), ())), preferred_element_type=F32)


def tile_at(t, size=TILE):
    return pl.ds(pl.multiple_of(t * size, size), size)


def over_rows(count, body):
    def step(i, carry):
        body(pl.ds(pl.multiple_of(i * ROWS, ROWS), ROWS))
        return carry

    lax.fori_loop(0, count // ROWS, step, 0)


def over_tiles(count, body):
    def step(t, carry):
        body(t)
        return carry

    lax.fori_loop(0, count, step, 0)


def head_probs(q, k, allowed, scale):
    scores = jnp.where(allowed, dot(q, k, ((1,), (1,))) * scale, -jnp.inf)
    top = jnp.max(scores, axis=-1, keepdims=True)
    lse = top + jnp.log(jnp.sum(jnp.exp(scores - top), axis=-1, keepdims=True))
    return jnp.exp(scores - lse)


def allowed_pairs(seg_col, seg_row):
    length = seg_col.shape[0]
    row = lax.broadcasted_iota(jnp.int32, (length, length), 0)
    col = lax.broadcasted_iota(jnp.int32, (length, length), 1)
    return (row >= col) & (seg_col == seg_row)


def norm_of(x):
    center = x - jnp.mean(x, axis=-1, keepdims=True)
    factor = lax.rsqrt(jnp.mean(center * center, axis=-1, keepdims=True) + NORM_EPS)
    return center * factor, factor


def norm_backward(d_act, normed, factor, gain):
    d_norm = d_act * gain
    return factor * (
        d_norm
        - jnp.mean(d_norm, axis=-1, keepdims=True)
        - normed * jnp.mean(d_norm * normed, axis=-1, keepdims=True)
    )


def gelu_pair(pre_act):
    cubic = pre_act * pre_act * pre_act
    tangent = jnp.tanh(GELU_COEF * (pre_act + CUBIC_COEF * cubic))
    gelu_value = 0.5 * pre_act * (1.0 + tangent)
    gelu_slope = 0.5 * (1.0 + tangent) + 0.5 * pre_act * (1.0 - tangent * tangent) * GELU_COEF * (
        1.0 + 3.0 * CUBIC_COEF * pre_act * pre_act
    )
    return gelu_value, gelu_slope


def vector_row(small, shard, vector, layer, part, size):
    return small[shard, vector, pl.ds(2 * layer + part, 1), pl.ds(0, size)]


def fill_vector(target, small, vector, layer):
    for s in range(8):
        target[:, pl.ds(s * 128, 128)] = vector_row(small, s, vector, layer, 0, 128)


class Pair:
    def __init__(self, terms, box, send, recv):
        self.terms, self.box, self.send, self.recv = terms, box, send, recv
        self.other = {"core": 1 - lax.axis_index("core")}

    def copy(self, which, t):
        return remote(
            self.terms.at[which, t],
            self.box.at[which, t],
            self.send.at[which, t],
            self.recv.at[which, t],
            self.other,
        )

    def fill(self, which, make):
        count = self.terms.shape[1]

        def body(t):
            self.terms[which, t] = make(t)

            @pl.when(t > 0)
            def _():
                self.copy(which, t - 1).start()

        over_tiles(count, body)
        self.copy(which, count - 1).start()

    def wait(self, which):
        for t in range(self.terms.shape[1]):
            self.copy(which, t).wait()

    def total(self, which, rows):
        return jnp.concatenate(
            [
                self.terms[which, t, rows, :] + self.box[which, t, rows, :]
                for t in range(self.terms.shape[1])
            ],
            axis=-1,
        )


def greet_pair():
    barrier = pltpu.get_barrier_semaphore()
    pl.semaphore_signal(
        barrier,
        inc=1,
        device_id={"core": 1 - lax.axis_index("core")},
        device_id_type=pl.DeviceIdType.MESH,
    )
    pl.semaphore_wait(barrier, 1)


def nothing(*_):
    pass


def seg_row_col(segs):
    row = jnp.concatenate([segs[q, 0:1, 0:80] for q in range(RING)], axis=-1)
    length = row.shape[1]
    at = lax.broadcasted_iota(jnp.int32, (length, length), 0)
    to = lax.broadcasted_iota(jnp.int32, (length, length), 1)
    return row, jnp.sum(jnp.where(at == to, row, 0.0), axis=-1, keepdims=True)


def forward_kernel(layer, count, moved, *refs):
    state, segs, small, w_up, w_down, w_qkv, w_out = refs[:7]
    parts, refs = refs[7 + count : 7 + count + moved], refs[7 + count + moved :]
    new_state, act_one, qkv, attn, middle, act_two, slope, hidden = refs[:8]
    fulls, wholes = refs[8 : 8 + count], refs[8 + count : 8 + count + moved]
    refs = refs[8 + count + moved :]
    v_qkv, v_out, v_up, v_down, terms, box, vec, vec_up = refs[:8]
    load, p_send, p_recv = refs[8:11]
    rings = refs[11:]
    core = lax.axis_index("core")
    length, width = state.shape
    half_width = width // 2
    loads = [
        pltpu.make_async_copy(w, v, load.at[i])
        for i, (w, v) in enumerate(((w_qkv, v_qkv), (w_out, v_out), (w_up, v_up), (w_down, v_down)))
    ]
    for copy in loads:
        copy.start()
    pos = positions()
    streams = sequences = None
    if count:
        greet(pos, False)
        streams = [
            Gather(pos, ORDERS[m], None, fulls[m], rings[0].at[m], rings[1].at[m])
            for m in range(count)
        ]
        for s in streams:
            s.begin(2)
    elif moved:
        greet(pos, True)
        sequences = Sequences(pos, parts, wholes, rings)
        sequences.begin()
    else:
        greet_pair()
    pair = Pair(terms, box, p_send, p_recv)
    for i, vector in enumerate((G_ONE, S_ONE, B_OUT, G_TWO, S_TWO, B_DOWN)):
        fill_vector(vec.at[i], small, vector, layer)
    for s in range(8):
        vec_up[0:1, pl.ds(s * TILE, TILE)] = vector_row(small, s, B_UP, layer, core, TILE)
    q_bias = []
    for s in range(8):
        row = vector_row(small, s, B_QV, layer, 0, 256)
        for at in (0, 2 * HEAD_DIM):
            q_bias.append(
                jnp.where(
                    core == 0,
                    row[:, at : at + HEAD_DIM],
                    row[:, at + HEAD_DIM : at + 2 * HEAD_DIM],
                )
            )
    vec_up[1:2, pl.ds(0, half_width)] = jnp.concatenate(q_bias[:8], axis=-1)
    vec_up[1:2, pl.ds(half_width, half_width)] = jnp.zeros((1, half_width), F32)
    vec_up[1:2, pl.ds(2 * half_width, half_width)] = jnp.concatenate(q_bias[8:], axis=-1)

    def first_norm(rows):
        normed, _ = norm_of(state[rows, :])
        act_one[rows, :] = (normed * vec[0] + vec[1]).astype(LOW)

    over_rows(length, first_norm)
    loads[0].wait()

    def project(t):
        here = tile_at(t)
        bias = vec_up[1:2, here]
        qkv[:, here] = (dot(act_one[...], v_qkv[:, here]) + bias).astype(LOW)

    over_tiles(3 * half_width // TILE, project)
    seg_row, seg_col = seg_row_col(segs)
    allowed = allowed_pairs(seg_col, seg_row)
    scale = 1.0 / math.sqrt(HEAD_DIM)
    for h in range(half_width // HEAD_DIM):
        q, k, v = (qkv[:, pl.ds(t * half_width + h * HEAD_DIM, HEAD_DIM)] for t in range(3))
        probs = head_probs(q, k, allowed, scale).astype(LOW)
        attn[:, pl.ds(h * HEAD_DIM, HEAD_DIM)] = dot(probs, v).astype(LOW)
    loads[1].wait()
    pair.fill(0, lambda t: dot(attn[...], v_out[:, tile_at(t)]))
    if moved:
        sequences.cross()
    pair.wait(0)

    def second_norm(rows):
        x = state[rows, :] + pair.total(0, rows) + vec[2]
        middle[rows, :] = x
        normed, _ = norm_of(x)
        act_two[rows, :] = (normed * vec[3] + vec[4]).astype(LOW)

    over_rows(length, second_norm)
    loads[2].wait()

    def expand(t):
        here = tile_at(t)
        value, rise = gelu_pair(dot(act_two[...], v_up[:, here]) + vec_up[0:1, here])
        hidden[:, here] = value.astype(LOW)
        slope[:, here] = rise

    over_tiles(slope.shape[1] // TILE, expand)
    if count:
        for s in streams:
            s.onward(2)
    loads[3].wait()
    pair.fill(1, lambda t: dot(hidden[...], v_down[:, tile_at(t)]))
    pair.wait(1)

    def close(rows):
        new_state[rows, :] = middle[rows, :] + pair.total(1, rows) + vec[5]

    over_rows(length, close)
    if count:
        for s in streams:
            s.finish(2)
        for s in streams:
            s.drain((2,))
    if moved:
        sequences.drain()


def weight_scratch(weights):
    w_up, w_down, w_qkv, w_out = weights
    return [pltpu.VMEM(w.shape, LOW) for w in (w_qkv, w_out, w_up, w_down)]


def pair_scratch(length, width):
    shape = (2, width // TILE, length, TILE)
    return [pltpu.VMEM(shape, F32), pltpu.VMEM(shape, F32)]


def forward_block(layer, state, segs, small, weights, begun, parts):
    count, moved = len(begun), len(parts)
    length, width = state.shape
    inner = weights[0].shape[1]
    shapes = [
        ((length, width), F32),
        ((length, width), LOW),
        ((length, 3 * width // 2), LOW),
        ((length, width // 2), LOW),
        ((length, width), F32),
        ((length, width), LOW),
        ((length, inner), F32),
        ((length, inner), LOW),
    ]
    shapes = [jax.ShapeDtypeStruct(*s) for s in shapes]
    shapes += [jax.ShapeDtypeStruct(b.shape, b.dtype) for b in begun]
    out = pl.pallas_call(
        functools.partial(forward_kernel, layer, count, moved),
        out_shape=shapes + sequence_shapes(parts),
        in_specs=[VMEM] * 3 + [ANY] * (4 + count + moved),
        out_specs=[VMEM] * 8 + [ANY] * (count + moved),
        input_output_aliases={7 + m: 8 + m for m in range(count)},
        scratch_shapes=weight_scratch(weights)
        + pair_scratch(length, width)
        + [
            pltpu.VMEM((6, 1, width), F32),
            pltpu.VMEM((2, inner), F32),
            DMA((4,)),
            DMA((2, width // TILE)),
            DMA((2, width // TILE)),
        ]
        + ([DMA((count, 12)), DMA((count, 12))] if count else [])
        + sequence_scratch(moved),
        compiler_params=pltpu.CompilerParams(
            collective_id=2 + layer, has_side_effects=True, vmem_limit_bytes=60 * 1024 * 1024
        ),
        name="forward_block",
    )(state, segs, small, *weights, *begun, *parts)
    return out[:8], out[8 : 8 + count], out[8 + count :]


def column_sum(target, row, value):
    target[row : row + 1, :] += jnp.sum(value, axis=0, keepdims=True)


def backward_kernel(layer, count, *refs):
    grad_state, state, middle, qkv, attn, slope, segs, small = refs[:8]
    w_up, w_down, w_qkv, w_out = refs[8:12]
    grads, refs = refs[12 : 12 + count], refs[12 + count :]
    new_grad, grad_low, d_pre_low, mid_low, d_qkv, small_grad = refs[:6]
    sums, refs = refs[6 : 6 + count], refs[6 + count :]
    v_qkv, v_out, v_up, v_down, terms, box, vec, acc, acc_up, acc_qkv, d_attn, grad_mid = refs[:12]
    load, p_send, p_recv = refs[12:15]
    rings = refs[15:]
    core = lax.axis_index("core")
    length, width = state.shape
    half_width = width // 2
    inner = slope.shape[1]
    loads = [
        pltpu.make_async_copy(w, v, load.at[i])
        for i, (w, v) in enumerate(((w_down, v_down), (w_up, v_up), (w_out, v_out), (w_qkv, v_qkv)))
    ]
    for copy in loads:
        copy.start()
    if count:
        pos = positions()
        greet(pos, False)
        send, recv, local = rings[2 * count :]
        streams = [
            Scatter(
                pos,
                ORDERS[m % 4],
                grads[m],
                rings[2 * m],
                (rings[2 * m + 1],),
                (sums[m],),
                send.at[m],
                recv.at[m],
                local.at[m],
            )
            for m in range(count)
        ]
        for s in streams:
            s.begin(0)
    else:
        greet_pair()
        streams = ()
    pair = Pair(terms, box, p_send, p_recv)
    fill_vector(vec.at[0], small, G_ONE, layer)
    fill_vector(vec.at[1], small, G_TWO, layer)
    acc[...] = jnp.zeros_like(acc)

    def lower(rows):
        g = grad_state[rows, :]
        grad_low[rows, :] = g.astype(LOW)
        column_sum(acc, 0, g)

    over_rows(length, lower)
    loads[0].wait()

    def contract(t):
        here = tile_at(t)
        d_pre = dot(grad_low[...], v_down[here, :], ((1,), (1,))) * slope[:, here]
        d_pre_low[:, here] = d_pre.astype(LOW)
        acc_up[:, here] = jnp.sum(d_pre, axis=0, keepdims=True)

    over_tiles(inner // TILE, contract)
    loads[1].wait()
    pair.fill(0, lambda t: dot(d_pre_low[...], v_up[tile_at(t), :], ((1,), (1,))))
    pair.wait(0)

    def second_norm(rows):
        d_act = pair.total(0, rows)
        normed, factor = norm_of(middle[rows, :])
        column_sum(acc, 1, d_act * normed)
        column_sum(acc, 2, d_act)
        g = grad_state[rows, :] + norm_backward(d_act, normed, factor, vec[1])
        grad_mid[rows, :] = g
        mid_low[rows, :] = g.astype(LOW)
        column_sum(acc, 3, g)

    over_rows(length, second_norm)
    loads[2].wait()

    def attn_grad(t):
        here = tile_at(t)
        d_attn[:, here] = dot(mid_low[...], v_out[here, :], ((1,), (1,))).astype(LOW)

    over_tiles(half_width // TILE, attn_grad)
    for s in streams:
        s.onward(0)
    seg_row, seg_col = seg_row_col(segs)
    allowed = allowed_pairs(seg_col, seg_row)
    scale = 1.0 / math.sqrt(HEAD_DIM)
    for h in range(half_width // HEAD_DIM):
        q, k, v = (qkv[:, pl.ds(t * half_width + h * HEAD_DIM, HEAD_DIM)] for t in range(3))
        here = pl.ds(h * HEAD_DIM, HEAD_DIM)
        d_head = d_attn[:, here]
        full = head_probs(q, k, allowed, scale)
        delta = jnp.sum(
            d_head.astype(F32) * attn[:, here].astype(F32), axis=-1, keepdims=True
        )
        d_scores = (full * (dot(d_head, v, ((1,), (1,))) - delta)).astype(LOW)
        ends = (
            dot(d_scores, k) * scale,
            dot(d_scores, q, ((0,), (0,))) * scale,
            dot(full.astype(LOW), d_head, ((0,), (0,))),
        )
        for t, end in enumerate(ends):
            place = pl.ds(t * half_width + h * HEAD_DIM, HEAD_DIM)
            d_qkv[:, place] = end.astype(LOW)
            acc_qkv[:, place] = jnp.sum(end, axis=0, keepdims=True)
    loads[3].wait()
    pair.fill(1, lambda t: dot(d_qkv[...], v_qkv[tile_at(t), :], ((1,), (1,))))
    pair.wait(1)

    def first_norm(rows):
        d_act = pair.total(1, rows)
        normed, factor = norm_of(state[rows, :])
        column_sum(acc, 4, d_act * normed)
        column_sum(acc, 5, d_act)
        new_grad[rows, :] = grad_mid[rows, :] + norm_backward(d_act, normed, factor, vec[0])

    over_rows(length, first_norm)
    small_grad[...] = jnp.zeros_like(small_grad)
    first = (core == 0).astype(F32)
    for s in range(8):
        here = pl.ds(s * 128, 128)
        for vector, row in ((B_DOWN, 0), (G_TWO, 1), (S_TWO, 2), (B_OUT, 3), (G_ONE, 4), (S_ONE, 5)):
            small_grad[s, vector, 0:1, 0:128] = acc[row : row + 1, here] * first
        block = acc_up[:, pl.ds(s * TILE, TILE)]
        small_grad[s, B_UP, 0:1, :] = block * first
        small_grad[s, B_UP, 1:2, :] = block * (1.0 - first)
        at = (s // 4) * 2 * half_width + (s % 4) * 2 * HEAD_DIM
        heads = []
        for k in range(2):
            value = acc_qkv[:, pl.ds(at + k * HEAD_DIM, HEAD_DIM)]
            heads += [value * first, value * (1.0 - first)]
        small_grad[s, B_QV, 0:1, :] = jnp.concatenate(heads, axis=-1)
    for s in streams:
        s.finish(0)
    for s in streams:
        s.drain((0,))


def backward_block(layer, grad_state, record, segs, small, weights, grads):
    state, middle, qkv, attn, slope = record
    count = len(grads)
    length, width = state.shape
    inner = slope.shape[1]
    shapes = [
        ((length, width), F32),
        ((length, width), LOW),
        ((length, inner), LOW),
        ((length, width), LOW),
        ((length, 3 * width // 2), LOW),
        ((8, 8, 8, 256), F32),
    ]
    shapes = [jax.ShapeDtypeStruct(*s) for s in shapes]
    shapes += [jax.ShapeDtypeStruct(g.shape[1:], g.dtype) for g in grads]
    bufs = scatter_scratch([g.shape[3:] for g in grads], [g.dtype for g in grads], (0,))
    sems = [DMA((count, 18)), DMA((count, 18)), DMA((count, 5))] if count else []
    out = pl.pallas_call(
        functools.partial(backward_kernel, layer, count),
        out_shape=shapes,
        in_specs=[VMEM] * 8 + [ANY] * (4 + count),
        out_specs=[VMEM] * (6 + count),
        scratch_shapes=weight_scratch(weights)
        + pair_scratch(length, width)
        + [
            pltpu.VMEM((2, 1, width), F32),
            pltpu.VMEM((6, width), F32),
            pltpu.VMEM((1, inner), F32),
            pltpu.VMEM((1, 3 * width // 2), F32),
            pltpu.VMEM((length, width // 2), LOW),
            pltpu.VMEM((length, width), F32),
            DMA((4,)),
            DMA((2, width // TILE)),
            DMA((2, width // TILE)),
        ]
        + bufs
        + sems,
        compiler_params=pltpu.CompilerParams(
            collective_id=4 + layer, has_side_effects=True, vmem_limit_bytes=63 * 1024 * 1024
        ),
        name="backward_block",
    )(grad_state, state, middle, qkv, attn, slope, segs, small, *weights, *grads)
    return out[:6], out[6:]


def finish_kernel(layers, *refs):
    ins, outs = refs[: 5 * layers], refs[5 * layers :]
    o_qkv, o_out, o_up, o_down = outs[:4]
    for l in range(layers):
        up, down, qkv, out, small = ins[5 * l : 5 * l + 5]
        for s in range(8):
            for c in range(2):
                o_up[l, :, pl.ds((2 * s + c) * TILE, TILE)] = up[c, 0, :, pl.ds(s * TILE, TILE)].astype(F32)
        for c in range(2):
            o_down[l, c, 0] = down[c, 0].astype(F32)
            o_out[l, c, 0] = out[c, 0].astype(F32)
        for k in range(24):
            here = pl.ds(k * HEAD_DIM, HEAD_DIM)
            both = jnp.concatenate([qkv[0, 0, :, here], qkv[1, 0, :, here]], axis=-1)
            o_qkv[l, :, pl.ds(k * 128, 128)] = both.astype(F32)

        @pl.when(pl.program_id(0) == 0)
        def _():
            for v in range(8):
                o = outs[4 + v]
                size = o.shape[1]
                for part in range((size + 255) // 256):
                    span = min(size, 256)
                    o[l : l + 1, pl.ds(part * 256, span)] = (
                        small[0, v, part : part + 1, 0:span] + small[1, v, part : part + 1, 0:span]
                    )


def finish(finals, sizes):
    layers = len(finals)
    in_specs, args = [], []
    for f in finals:
        for m, a in enumerate(f):
            r, c = a.shape[3:]
            args.append(a.reshape(2, 8, r, c))
            if m < 4:
                in_specs.append(pl.BlockSpec((2, 1, r, c), lambda p: (0, p, 0, 0)))
            else:
                in_specs.append(pl.BlockSpec((2, 8, r, c), lambda p: (0, 0, 0, 0)))
    up, down, qkv, out = (a.shape[2:] for a in args[:4])
    shapes, specs = [], []
    for rows, cols in ((qkv[0], 2 * qkv[1]), (0, 0), (up[0], 2 * up[1])):
        if rows:
            shapes.append(jax.ShapeDtypeStruct((layers, 8 * rows, cols), F32))
            specs.append(pl.BlockSpec((layers, rows, cols), lambda p: (0, p, 0)))
        else:
            shapes.append(jax.ShapeDtypeStruct((layers, 2, 8) + out, F32))
            specs.append(pl.BlockSpec((layers, 2, 1) + out, lambda p: (0, 0, p, 0, 0)))
    shapes.append(jax.ShapeDtypeStruct((layers, 2, 8) + down, F32))
    specs.append(pl.BlockSpec((layers, 2, 1) + down, lambda p: (0, 0, p, 0, 0)))
    for size in sizes:
        shapes.append(jax.ShapeDtypeStruct((layers, size), F32))
        specs.append(pl.BlockSpec((layers, size), lambda p: (0, 0)))
    res = pl.pallas_call(
        functools.partial(finish_kernel, layers),
        out_shape=shapes,
        grid=(8,),
        in_specs=in_specs,
        out_specs=specs,
        name="finish",
    )(*args)
    o_out = res[1].reshape(layers, 16 * out[0], out[1])
    o_down = res[3].reshape(layers, 16 * down[0], down[1])
    return (res[0], o_out, res[2], o_down) + tuple(res[4:])


def prepare_kernel(where, up, down, qkv, out, segment_ids, *refs):
    vectors, refs = refs[:8], refs[8:]
    layers = up.shape[0]
    sub, core = where[0], where[1]
    for l in range(layers):
        o_up, o_down, o_qkv, o_out = refs[4 * l : 4 * l + 4]
        o_down[...] = down[l]
        o_out[...] = out[l]
        for s in range(8):
            at = pl.multiple_of((2 * s + core) * TILE, TILE)
            o_up[:, pl.ds(s * TILE, TILE)] = up[l, :, pl.ds(at, TILE)]
        for k in range(12):
            two = []
            for j in range(2):
                pair = qkv[l, :, pl.ds((2 * k + j) * 128, 128)]
                two.append(jnp.where(core == 0, pair[:, :HEAD_DIM], pair[:, HEAD_DIM:]))
            o_qkv[:, pl.ds(k * 128, 128)] = jnp.concatenate(two, axis=-1)
    small, segs = refs[4 * layers :]
    small[...] = jnp.zeros_like(small)
    for v, vector in enumerate(vectors):

        @pl.when(sub == v)
        def _():
            size = vector.shape[1]
            for part in range((size + 255) // 256):
                span = min(size, 256)
                block = vector[:, pl.ds(part * 256, span)].astype(F32)
                for l in range(layers):
                    small[2 * l + part : 2 * l + part + 1, 0:span] = block[l : l + 1]

    segs[...] = jnp.zeros_like(segs)
    for b in range(segs.shape[0]):
        segs[b, 0:1, 0 : segment_ids.shape[1]] = segment_ids[b : b + 1, :].astype(F32)


def prepare(weights, segment_ids, vectors):
    up, down, qkv, out = weights
    layers, rows = up.shape[:2]
    piece, down_rows, out_rows = rows // 8, down.shape[1] // 16, rows // 16
    where = jnp.stack(
        [lax.axis_index("xl") * 4 + lax.axis_index("y"), lax.axis_index("core")]
    ).astype(jnp.int32)
    per_layer = [
        (piece, up.shape[2] // 2),
        (down_rows, down.shape[2]),
        (piece, qkv.shape[2] // 2),
        (out_rows, out.shape[2]),
    ]
    shapes = [jax.ShapeDtypeStruct(e, LOW) for e in per_layer] * layers
    shapes += [jax.ShapeDtypeStruct((8, 256), F32), jax.ShapeDtypeStruct((2, 8, 128), F32)]
    by_row = lambda i, where: (0, where[0], 0)
    by_half = lambda i, where: (0, 8 * where[1] + where[0], 0)
    whole = lambda a: pl.BlockSpec(a.shape, lambda i, where: (0,) * len(a.shape))
    made = pl.pallas_call(
        prepare_kernel,
        out_shape=shapes,
        grid_spec=pltpu.PrefetchScalarGridSpec(
            num_scalar_prefetch=1,
            grid=(1,),
            in_specs=[
                pl.BlockSpec((layers, piece, up.shape[2]), by_row),
                pl.BlockSpec((layers, down_rows, down.shape[2]), by_half),
                pl.BlockSpec((layers, piece, qkv.shape[2]), by_row),
                pl.BlockSpec((layers, out_rows, out.shape[2]), by_half),
                whole(segment_ids),
            ]
            + [whole(v) for v in vectors],
            out_specs=[whole(e) for e in shapes],
        ),
        name="prepare",
    )(where, up, down, qkv, out, segment_ids, *vectors)
    owns = [made[4 * l : 4 * l + 4] for l in range(layers)]
    return owns, made[4 * layers], made[4 * layers + 1]


def per_device(
    inputs,
    segment_ids,
    weight_qkv,
    weight_out,
    weight_up,
    weight_down,
    bias_qv,
    bias_out,
    bias_up,
    bias_down,
    gain_one,
    shift_one,
    gain_two,
    shift_two,
    cotangent,
):
    layers, width = weight_qkv.shape[0], inputs.shape[-1]
    length = inputs.shape[1] * RING
    vectors = (bias_qv, bias_out, bias_up, bias_down, gain_one, shift_one, gain_two, shift_two)
    sizes = [v.shape[1] for v in vectors]
    owns, packed, segs = prepare((weight_up, weight_down, weight_qkv, weight_out), segment_ids, vectors)
    fulls, begun, wholes = gather_all(list(owns[0]) + [packed], list(owns[1]), [inputs, segs])
    state, segs = wholes[0].reshape(length, width), wholes[1]
    small = fulls[4].reshape(8, 8, 8, 256)
    records = []
    weights = [[w.reshape(-1, w.shape[-1]) for w in fulls[:4]]]
    for l in range(layers):
        carried, parts = (begun, []) if l == 0 else ([], [cotangent])
        made, fulls, wholes = forward_block(l, state, segs, small, weights[l], list(carried), parts)
        weights.append([w.reshape(-1, w.shape[-1]) for w in fulls])
        new_state, act_one, qkv, attn, middle, act_two, slope, hidden = made
        records.append(((state, middle, qkv, attn, slope), (act_one, act_two, hidden, attn)))
        state = new_state
    grad_state = wholes[0].reshape(length, width)
    pieces, sums = [], []
    for l in reversed(range(layers)):
        kept, (act_one, act_two, hidden, attn) = records[l]
        made, done = backward_block(l, grad_state, kept, segs, small, weights[l], pieces)
        sums += done
        grad_state, grad_low, d_pre_low, mid_low, d_qkv, small_grad = made
        tokens = ((0,), (0,))
        pieces = [
            dot(act_two, d_pre_low, tokens),
            dot(hidden, grad_low, tokens),
            dot(act_one, d_qkv, tokens),
            dot(attn, mid_low, tokens),
        ]
        pieces = [g.astype(LOW).reshape(RING, RING, RING, -1, g.shape[-1]) for g in pieces]
        pieces.append(small_grad.reshape(RING, RING, RING, 8, 256))
    quarter = (RING, length // RING, width)
    finals, parts = scatter_all(
        pieces, sums, [state.reshape(quarter), grad_state.reshape(quarter)]
    )
    finals = [finals[5 * l : 5 * l + 5] for l in range(layers)]
    return (parts[0], parts[1]) + finish(finals, sizes)


def solution(mesh):
    torus = Mesh(mesh.devices.reshape(4, 2, 4, 2, 2), AXES)
    tokens = P(("xh", "y", "xl", "core"), "z", None)
    weight = P(None, ("z", "xh"), None)
    vector = P(None, ("z", "xh"))
    return jax.shard_map(
        per_device,
        mesh=torus,
        in_specs=(tokens, P(("xh", "y", "xl", "core"), "z")) + (weight,) * 4 + (vector,) * 8 + (tokens,),
        out_specs=(tokens, tokens) + (weight,) * 4 + (vector,) * 8,
        check_vma=False,
    )
```

```python
import functools
import math

import jax
import jax.numpy as jnp
from jax import lax
from jax.experimental import pallas as pl
from jax.experimental.pallas import tpu as pltpu
from jax.sharding import Mesh
from jax.sharding import PartitionSpec as P

AXES = ("z", "xh", "y", "xl", "core")
RING = 4
ANY = pl.BlockSpec(memory_space=pl.ANY)
VMEM = pl.BlockSpec(memory_space=pltpu.VMEM)
DMA = pltpu.SemaphoreType.DMA
SCATTERS = ("xyz", "yzx", "zxy", "yxz", "xyz", "zyx", "yzx", "yxz", "yzx")
SPLIT = 4
UP_PART, DOWN_PART = (5, 8), (3, 4)
ORDERS = ("xyz", "zxy", "yzx", "yzx")


def positions():
    return {
        "z": lax.axis_index("z"),
        "x": lax.axis_index("xh") * 2 + lax.axis_index("xl"),
        "y": lax.axis_index("y"),
    }


def neighbour(pos, axis, step):
    at = lax.rem(pos[axis] + step + RING, RING)
    if axis == "x":
        return {"xh": at // 2, "xl": lax.rem(at, 2)}
    return {axis: at}


def remote(src, dst, send, recv, target):
    return pltpu.make_async_remote_copy(
        src_ref=src,
        dst_ref=dst,
        send_sem=send,
        recv_sem=recv,
        device_id=target,
        device_id_type=pl.DeviceIdType.MESH,
    )


def greet(pos, with_column):
    barrier = pltpu.get_barrier_semaphore()
    targets = [neighbour(pos, axis, step) for axis in "xyz" for step in (1, -1)]
    if with_column:
        targets.append(neighbour(pos, "z", 2))
    targets.append({"core": 1 - lax.axis_index("core")})
    for target in targets:
        pl.semaphore_signal(
            barrier, inc=1, device_id=target, device_id_type=pl.DeviceIdType.MESH
        )
    pl.semaphore_wait(barrier, len(targets))


def half(ref, which, rows, cols):
    lead = (slice(None),) * (len(ref.shape) - 2)
    if rows % 16 == 0:
        return ref.at[lead + (pl.ds(which * (rows // 2), rows // 2), slice(None))]
    return ref.at[lead + (slice(None), pl.ds(which * (cols // 2), cols // 2))]


class Gather:
    def __init__(self, pos, order, own, full, send, recv):
        self.pos, self.order, self.own, self.full = pos, order, own, full
        self.send, self.recv = send, recv
        self.rows, self.cols = full.shape[-2:]

    def view(self, stage, shift):
        index = {}
        for place, axis in enumerate(self.order):
            if place < stage:
                index[axis] = slice(None)
            elif place == stage:
                index[axis] = lax.rem(self.pos[axis] + shift + RING, RING)
            else:
                index[axis] = self.pos[axis]
        return self.full.at[index["z"], index["x"], index["y"]]

    def copy(self, stage, kind):
        axis = self.order[stage]
        sems = (self.send.at[stage * 4 + kind], self.recv.at[stage * 4 + kind])
        target = neighbour(self.pos, axis, 1 if kind % 2 == 0 else -1)
        if kind < 2:
            src = self.own if stage == 0 else self.view(stage, 0)
            return remote(src, self.view(stage, 0), *sems, target)
        piece = half(self.view(stage, -1 if kind == 2 else 1), kind - 2, self.rows, self.cols)
        return remote(piece, piece, *sems, target)

    def arrive(self, stage, kind):
        sems = (self.send.at[stage * 4 + kind], self.recv.at[stage * 4 + kind])
        axis = self.order[stage]
        if kind < 2:
            piece = self.view(stage, -1 if kind == 0 else 1)
        else:
            piece = half(self.view(stage, 2), kind - 2, self.rows, self.cols)
        remote(piece, piece, *sems, neighbour(self.pos, axis, 1)).wait_recv()

    def begin(self, stage):
        for kind in (0, 1):
            self.copy(stage, kind).start()

    def onward(self, stage):
        for kind in (0, 1):
            self.arrive(stage, kind)
            self.copy(stage, kind + 2).start()

    def finish(self, stage):
        for kind in (2, 3):
            self.arrive(stage, kind)

    def drain(self, stages):
        for stage in stages:
            for kind in range(4):
                self.copy(stage, kind).wait_send()


class Sequences:
    def __init__(self, pos, parts, wholes, sems):
        self.pos, self.parts, self.wholes = pos, parts, wholes
        self.send, self.recv, self.core_send, self.core_recv, self.local = sems
        self.core = lax.axis_index("core")
        self.receiver = pos["z"] // 2 == self.core

    def outward(self, a, b, home):
        return remote(
            self.parts[a].at[b],
            self.wholes[a].at[self.pos["z"]],
            self.send.at[a, b],
            self.recv.at[a, self.pos["z"]],
            {"z": home},
        )

    def crossing(self, a, q):
        piece = self.wholes[a].at[q]
        return remote(
            piece, piece, self.core_send.at[a, q], self.core_recv.at[a, q], {"core": 1 - self.core}
        )

    def staying(self, a, b):
        return pltpu.make_async_copy(
            self.parts[a].at[b], self.wholes[a].at[self.pos["z"]], self.local.at[a]
        )

    def begin(self):
        for a in range(len(self.parts)):
            for b in range(2):
                home = 2 * self.core + b

                @pl.when(home == self.pos["z"])
                def _():
                    self.staying(a, b).start()

                @pl.when(home != self.pos["z"])
                def _():
                    self.outward(a, b, home).start()

    def cross(self):
        @pl.when(self.receiver)
        def _():
            for a in range(len(self.parts)):
                for q in range(RING):

                    @pl.when(q == self.pos["z"])
                    def _():
                        self.staying(a, 0).wait()

                    @pl.when(q != self.pos["z"])
                    def _():
                        piece = self.wholes[a].at[q]
                        remote(
                            piece,
                            piece,
                            self.send.at[a, 0],
                            self.recv.at[a, q],
                            {"z": lax.rem(self.pos["z"] + 1, RING)},
                        ).wait_recv()

                    self.crossing(a, q).start()

    def drain(self):
        for a in range(len(self.parts)):
            for b in range(2):
                home = 2 * self.core + b

                @pl.when(home != self.pos["z"])
                def _():
                    self.outward(a, b, lax.rem(self.pos["z"] + 1, RING)).wait_send()

            for q in range(RING):

                @pl.when(self.receiver)
                def _():
                    self.crossing(a, q).wait_send()

                @pl.when(jnp.logical_not(self.receiver))
                def _():
                    self.crossing(a, q).wait_recv()


def sequence_scratch(moved):
    sems = [DMA((moved, 2)), DMA((moved, RING)), DMA((moved, RING)), DMA((moved, RING)), DMA((moved,))]
    return sems if moved else []


def sequence_shapes(parts):
    return [jax.ShapeDtypeStruct((RING,) + p.shape[1:], p.dtype) for p in parts]


def gather_kernel(count, whole, moved, *refs):
    owns, parts = refs[:count], refs[count : count + moved]
    refs = refs[count + moved :]
    fulls, wholes = refs[:count], refs[count : count + moved]
    send, recv, local = refs[count + moved : count + moved + 3]
    pos = positions()
    greet(pos, True)
    sequences = Sequences(pos, parts, wholes, refs[count + moved + 3 :])
    streams, keeps = [], []
    for m in range(count):
        keeps.append(
            pltpu.make_async_copy(
                owns[m], fulls[m].at[pos["z"], pos["x"], pos["y"]], local.at[m]
            )
        )
        streams.append(
            Gather(pos, ORDERS[m % whole % 4], owns[m], fulls[m], send.at[m], recv.at[m])
        )
    for keep in keeps:
        keep.start()
    for s in streams:
        s.begin(0)
    sequences.begin()
    for stage in range(3):
        running = streams if stage < 2 else streams[:whole]
        for s in running:
            s.onward(stage)
        if stage == 0:
            for keep in keeps:
                keep.wait()
        for m, s in enumerate(running):
            s.finish(stage)
            if stage == 0 or (stage == 1 and m < whole):
                s.begin(stage + 1)
        if stage == 1:
            sequences.cross()
    for m, s in enumerate(streams):
        s.drain(range(3 if m < whole else 2))
    sequences.drain()


def gather_all(owns, begun, parts):
    count, moved = len(owns) + len(begun), len(parts)
    shapes = [
        jax.ShapeDtypeStruct((RING, RING, RING) + o.shape, o.dtype) for o in owns + begun
    ]
    out = pl.pallas_call(
        functools.partial(gather_kernel, count, len(owns), moved),
        out_shape=shapes + sequence_shapes(parts),
        in_specs=[ANY] * (count + moved),
        out_specs=[ANY] * (count + moved),
        scratch_shapes=[DMA((count, 12)), DMA((count, 12)), DMA((count,))]
        + sequence_scratch(moved),
        compiler_params=pltpu.CompilerParams(collective_id=0, has_side_effects=True),
        name="gather_all",
    )(*owns, *begun, *parts)
    return out[: len(owns)], out[len(owns) : count], out[count:]


def scatter_scratch(end, kind, start, last):
    r, c = end
    scratch = [] if start else [pltpu.VMEM((4, RING, RING, r, c // 2), kind)]
    for stage in range(start, 3):
        scratch.append(pltpu.VMEM((6,) + (RING,) * (2 - stage) + (r, c // 2), kind))
    for stage in range(start, 3 if last else 2):
        scratch.append(pltpu.VMEM((RING,) * (2 - stage) + (r, c), kind))
    return scratch


def scatter_of(pos, m, source, bufs, sums, sems):
    start = 1 if m < SPLIT else 0
    stages = 3 - start
    own = None if start else bufs[0]
    rest = list(bufs[1 - start :])
    boxes, more = [None] * start + rest[:stages], rest[stages:]
    sums = ([source] if start else []) + more + list(sums)
    return Scatter(pos, SCATTERS[m], start, None if start else source, own, boxes, sums, *sems)


class Scatter:
    def __init__(self, pos, order, start, grad, own, boxes, sums, send, recv, local, base=0):
        self.pos, self.order, self.start, self.grad = pos, order, start, grad
        self.own, self.boxes, self.sums = own, boxes, sums
        self.send, self.recv, self.local = send, recv, local
        self.part, self.base = sums[0].shape[-1] // 2, base

    def piece(self, stage, shift, which):
        axis = self.order[stage]
        left = [a for a in "zxy" if a in self.order[stage:]]
        source = self.grad if stage == 0 else self.sums[stage - 1]
        at = lax.rem(self.pos[axis] + shift + RING, RING)
        index = tuple(at if a == axis else slice(None) for a in left) + (slice(None),)
        base = self.base if stage == 0 else 0
        return source.at[index + (pl.ds(base + which * self.part, self.part),)]

    def box(self, stage, kind):
        return self.boxes[stage].at[kind]

    def copy(self, stage, kind):
        src, step = {
            0: (lambda: self.piece(stage, 2, 0), 1),
            1: (lambda: self.piece(stage, 1, 1), 1),
            2: (lambda: self.piece(stage, -2, 1), -1),
            3: (lambda: self.piece(stage, -1, 0), -1),
            4: (lambda: self.box(stage, 0), 1),
            5: (lambda: self.box(stage, 2), -1),
        }[kind]
        return remote(
            src(),
            self.box(stage, kind),
            self.send.at[stage * 6 + kind],
            self.recv.at[stage * 6 + kind],
            neighbour(self.pos, self.order[stage], step),
        )

    def loads(self):
        for slot, (shift, which) in enumerate(((1, 0), (-1, 1), (0, 0), (0, 1))):
            yield pltpu.make_async_copy(
                self.piece(0, shift, which), self.own.at[slot], self.local.at[slot]
            )

    def begin(self, stage):
        for kind in range(4):
            self.copy(stage, kind).start()
        if stage == 0 and self.own is not None:
            for load in self.loads():
                load.start()

    def term(self, stage, slot):
        if stage == 0 and self.own is not None:
            return self.own.at[slot]
        shift, which = ((1, 0), (-1, 1), (0, 0), (0, 1))[slot]
        return self.piece(stage, shift, which)

    def add(self, stage, target, terms):
        lead = 2 - stage

        def one(index):
            total = terms[0][index].astype(jnp.float32)
            for t in terms[1:]:
                total = total + t[index].astype(jnp.float32)
            target[index] = total.astype(target.dtype)

        if lead < 2:
            one((slice(None),) * (lead + 2))
            return

        def body(i, carry):
            one((i, slice(None), slice(None), slice(None)))
            return carry

        lax.fori_loop(0, RING, body, 0)

    def onward(self, stage):
        if stage == 0 and self.own is not None:
            for load in self.loads():
                load.wait()
        for slot, kind in ((0, 0), (1, 2)):
            self.copy(stage, kind).wait_recv()
            box = self.box(stage, kind)
            self.add(stage, box, (box, self.term(stage, slot)))
            self.copy(stage, 4 + slot).start()

    def finish(self, stage):
        for kind in (1, 3, 4, 5):
            self.copy(stage, kind).wait_recv()
        lead = (slice(None),) * (3 - stage)
        for which, kinds in ((0, (3, 4)), (1, (1, 5))):
            target = self.sums[stage].at[lead + (pl.ds(which * self.part, self.part),)]
            self.add(
                stage,
                target,
                (self.term(stage, 2 + which),) + tuple(self.box(stage, k) for k in kinds),
            )

    def steps(self):
        return 2 * (3 - self.start) + 1

    def step(self, at):
        if at == 0:
            self.begin(self.start)
        elif at < self.steps():
            stage = self.start + (at - 1) // 2
            if at % 2:
                self.onward(stage)
            else:
                self.finish(stage)
                if stage < 2:
                    self.begin(stage + 1)

    def drain(self, stages=None):
        for stage in range(self.start, 3) if stages is None else stages:
            for kind in range(6):
                self.copy(stage, kind).wait_send()


class Publish:
    def __init__(self, pos, across, source, final, sends, recvs, local):
        self.pos, self.across, self.source, self.final = pos, across, source, final
        self.sends_f, self.recvs_f, self.local = sends, recvs, local
        self.core, self.xl = lax.axis_index("core"), lax.axis_index("xl")
        self.part = source.shape[-1] // 2

    def across_first(self):
        return self.across

    def block(self, shift):
        yi = lax.rem(self.pos["y"] + shift + RING, RING)
        xs = slice(None) if self.across_first() else self.xl
        return self.final.at[self.core, xs, yi]

    def spread(self, kind, own=False):
        sems = (self.sends_f.at[kind], self.recvs_f.at[kind])
        if kind == 5:
            whole = self.final.at[self.core]
            return remote(whole, whole, *sems, {"core": 1 - self.core})
        if kind == 4:
            if self.across_first():
                dst = self.final.at[self.core, self.xl, self.pos["y"]]
                src = self.source
            else:
                src = dst = self.final.at[self.core, self.xl]
            return remote(src, dst, *sems, {"xl": 1 - self.xl})
        target = neighbour(self.pos, "y", 1 if kind % 2 == 0 else -1)
        if kind < 2:
            dst = self.block(0)
            src = dst if self.across_first() else self.source
            return remote(src, dst, *sems, target)
        ref = self.block(-1 if kind == 2 else 1)
        lead = (slice(None),) * (len(ref.shape) - 1)
        ref = ref.at[lead + (pl.ds((kind - 2) * self.part, self.part),)]
        return remote(ref, ref, *sems, target)

    def spread_arrives(self, kind):
        sems = (self.sends_f.at[kind], self.recvs_f.at[kind])
        if kind == 5:
            ref = self.final.at[1 - self.core]
        elif kind == 4:
            ref = self.final.at[self.core, 1 - self.xl]
            if self.across_first():
                ref = ref.at[self.pos["y"]]
        elif kind < 2:
            ref = self.block(-1 if kind == 0 else 1)
        else:
            ref = self.block(2)
            lead = (slice(None),) * (len(ref.shape) - 1)
            ref = ref.at[lead + (pl.ds((kind - 2) * self.part, self.part),)]
        remote(ref, ref, *sems, {"core": 1 - self.core}).wait_recv()

    def keep(self):
        return pltpu.make_async_copy(
            self.source,
            self.final.at[self.core, self.xl, self.pos["y"]],
            self.local,
        )

    def publish(self, step):
        if step == 0:
            self.keep().start()
            for kind in (4,) if self.across_first() else (0, 1):
                self.spread(kind).start()
            self.keep().wait()
        elif self.across_first():
            if step == 1:
                self.spread_arrives(4)
                for kind in (0, 1):
                    self.spread(kind).start()
            elif step == 2:
                for kind in (0, 1):
                    self.spread_arrives(kind)
                    self.spread(kind + 2).start()
            elif step == 3:
                for kind in (2, 3):
                    self.spread_arrives(kind)
        else:
            if step == 1:
                for kind in (0, 1):
                    self.spread_arrives(kind)
                    self.spread(kind + 2).start()
            elif step == 2:
                for kind in (2, 3):
                    self.spread_arrives(kind)
                self.spread(4).start()
            elif step == 3:
                self.spread_arrives(4)
        if step == 3:
            self.spread(5).start()
        if step == 4:
            self.spread_arrives(5)

    def drain(self):
        for kind in range(6):
            self.spread(kind).wait_send()


MATRICES = 9


def scatter_kernel(moved, *refs):
    grads, given = refs[:MATRICES], refs[MATRICES : 2 * MATRICES]
    wholes, refs = refs[2 * MATRICES : 2 * MATRICES + moved], refs[2 * MATRICES + moved :]
    finals, parts = refs[: 2 * MATRICES], refs[2 * MATRICES : 2 * MATRICES + moved]
    refs = refs[2 * MATRICES + moved :]
    send, recv, local, sends_f, recvs_f, keeps, send_t, recv_t, local_t = refs[-9:]
    pos = positions()
    core = lax.axis_index("core")
    greet(pos, True)
    streams, at = [], 0
    for m in range(MATRICES):
        take = 4 if m < SPLIT else 7
        sems = (send.at[m], recv.at[m], local.at[m])
        streams.append(scatter_of(pos, m, grads[m], refs[at : at + take], (), sems))
        at += take
    news = [
        Publish(
            pos, m % MATRICES in (0, 1, 4, 5, 6), source, finals[m], sends_f.at[m], recvs_f.at[m], keeps.at[m]
        )
        for m, source in enumerate([s.sums[2] for s in streams] + list(given))
    ]
    sender = pos["z"] // 2 == core
    slot = lax.rem(pos["z"], 2)

    def homeward(a, q):
        return remote(
            wholes[a].at[q], parts[a].at[slot], send_t.at[a, q], recv_t.at[a, slot], {"z": q}
        )

    def staying(a):
        return pltpu.make_async_copy(wholes[a].at[pos["z"]], parts[a].at[slot], local_t.at[a])

    for a in range(moved):
        for q in range(RING):

            @pl.when(sender & (pos["z"] == q))
            def _():
                staying(a).start()

            @pl.when(sender & (pos["z"] != q))
            def _():
                homeward(a, q).start()

    for at in range(11):
        for n in news[MATRICES:]:
            if at < 5:
                n.publish(at)
        for s, n in zip(streams, news):
            s.step(at)
            if 0 <= at - s.steps() + 1 < 5:
                n.publish(at - s.steps() + 1)
    for s in streams:
        s.drain()
    for n in news:
        n.drain()
    for a in range(moved):
        for q in range(RING):

            @pl.when(sender & (pos["z"] == q))
            def _():
                staying(a).wait()

            @pl.when(sender & (pos["z"] != q))
            def _():
                homeward(a, q).wait_send()

        for b in range(2):

            @pl.when(2 * core + b != pos["z"])
            def _():
                remote(
                    parts[a].at[b],
                    parts[a].at[b],
                    send_t.at[a, 0],
                    recv_t.at[a, b],
                    {"z": lax.rem(pos["z"] + 1, RING)},
                ).wait_recv()


def scatter_all(grads, given, wholes):
    moved = len(wholes)
    ends = [g.shape[-2:] for g in grads] * 2
    kinds = [g.dtype for g in grads] * 2
    shapes = [jax.ShapeDtypeStruct((2, 2, RING) + e, k) for e, k in zip(ends, kinds)]
    shapes += [jax.ShapeDtypeStruct((2,) + w.shape[1:], w.dtype) for w in wholes]
    bufs = []
    for m in range(MATRICES):
        bufs += scatter_scratch(ends[m], kinds[m], 1 if m < SPLIT else 0, True)
    out = pl.pallas_call(
        functools.partial(scatter_kernel, moved),
        out_shape=shapes,
        in_specs=[VMEM] * SPLIT + [ANY] * (2 * MATRICES - SPLIT + moved),
        out_specs=[ANY] * (2 * MATRICES + moved),
        scratch_shapes=bufs
        + [
            DMA((MATRICES, 18)),
            DMA((MATRICES, 18)),
            DMA((MATRICES, 5)),
            DMA((2 * MATRICES, 6)),
            DMA((2 * MATRICES, 6)),
            DMA((2 * MATRICES,)),
            DMA((moved, RING)),
            DMA((moved, 2)),
            DMA((moved,)),
        ],
        compiler_params=pltpu.CompilerParams(
            collective_id=1, has_side_effects=True, vmem_limit_bytes=62 * 1024 * 1024
        ),
        name="scatter_all",
    )(*grads, *given, *wholes)
    return out[:MATRICES], out[MATRICES : 2 * MATRICES], out[2 * MATRICES :]


NORM_EPS = 1e-05
GELU_COEF = 0.7978845608028654
CUBIC_COEF = 0.044715
HEAD_DIM = 64
LOW = jnp.bfloat16
F32 = jnp.float32
TILE = 256
ROWS = 32
B_QV, B_OUT, B_UP, B_DOWN, G_ONE, S_ONE, G_TWO, S_TWO = range(8)


def dot(left, right, dims=((1,), (0,))):
    return lax.dot_general(left, right, (dims, ((), ())), preferred_element_type=F32)


def tile_at(t, size=TILE):
    return pl.ds(pl.multiple_of(t * size, size), size)


def over_rows(count, body):
    def step(i, carry):
        body(pl.ds(pl.multiple_of(i * ROWS, ROWS), ROWS))
        return carry

    lax.fori_loop(0, count // ROWS, step, 0)


def over_tiles(count, body):
    def step(t, carry):
        body(t)
        return carry

    lax.fori_loop(0, count, step, 0)


def head_probs(q, k, allowed, scale):
    scores = jnp.where(allowed, dot(q, k, ((1,), (1,))) * scale, -jnp.inf)
    top = jnp.max(scores, axis=-1, keepdims=True)
    lse = top + jnp.log(jnp.sum(jnp.exp(scores - top), axis=-1, keepdims=True))
    return jnp.exp(scores - lse)


def allowed_pairs(seg_col, seg_row):
    length = seg_col.shape[0]
    row = lax.broadcasted_iota(jnp.int32, (length, length), 0)
    col = lax.broadcasted_iota(jnp.int32, (length, length), 1)
    return (row >= col) & (seg_col == seg_row)


def norm_of(x):
    center = x - jnp.mean(x, axis=-1, keepdims=True)
    factor = lax.rsqrt(jnp.mean(center * center, axis=-1, keepdims=True) + NORM_EPS)
    return center * factor, factor


def norm_backward(d_act, normed, factor, gain):
    d_norm = d_act * gain
    return factor * (
        d_norm
        - jnp.mean(d_norm, axis=-1, keepdims=True)
        - normed * jnp.mean(d_norm * normed, axis=-1, keepdims=True)
    )


def gelu_pair(pre_act):
    cubic = pre_act * pre_act * pre_act
    tangent = jnp.tanh(GELU_COEF * (pre_act + CUBIC_COEF * cubic))
    gelu_value = 0.5 * pre_act * (1.0 + tangent)
    gelu_slope = 0.5 * (1.0 + tangent) + 0.5 * pre_act * (1.0 - tangent * tangent) * GELU_COEF * (
        1.0 + 3.0 * CUBIC_COEF * pre_act * pre_act
    )
    return gelu_value, gelu_slope


def vector_row(small, shard, vector, layer, part, size):
    return small[shard, vector, pl.ds(2 * layer + part, 1), pl.ds(0, size)]


def fill_vector(target, small, vector, layer):
    for s in range(8):
        target[:, pl.ds(s * 128, 128)] = vector_row(small, s, vector, layer, 0, 128)


class Pair:
    def __init__(self, terms, box, send, recv):
        self.terms, self.box, self.send, self.recv = terms, box, send, recv
        self.other = {"core": 1 - lax.axis_index("core")}

    def copy(self, which, t):
        return remote(
            self.terms.at[which, t],
            self.box.at[which, t],
            self.send.at[which, t],
            self.recv.at[which, t],
            self.other,
        )

    def fill(self, which, make):
        count = self.terms.shape[1]

        def body(t):
            self.terms[which, t] = make(t)

            @pl.when(t > 0)
            def _():
                self.copy(which, t - 1).start()

        over_tiles(count, body)
        self.copy(which, count - 1).start()

    def wait(self, which):
        for t in range(self.terms.shape[1]):
            self.copy(which, t).wait()

    def total(self, which, rows):
        return jnp.concatenate(
            [
                self.terms[which, t, rows, :] + self.box[which, t, rows, :]
                for t in range(self.terms.shape[1])
            ],
            axis=-1,
        )


def greet_pair():
    barrier = pltpu.get_barrier_semaphore()
    pl.semaphore_signal(
        barrier,
        inc=1,
        device_id={"core": 1 - lax.axis_index("core")},
        device_id_type=pl.DeviceIdType.MESH,
    )
    pl.semaphore_wait(barrier, 1)


def nothing(*_):
    pass


def seg_row_col(segs):
    row = jnp.concatenate([segs[q, 0:1, 0:80] for q in range(RING)], axis=-1)
    length = row.shape[1]
    at = lax.broadcasted_iota(jnp.int32, (length, length), 0)
    to = lax.broadcasted_iota(jnp.int32, (length, length), 1)
    return row, jnp.sum(jnp.where(at == to, row, 0.0), axis=-1, keepdims=True)


def forward_kernel(layer, count, moved, *refs):
    state, segs, small, w_up, w_down, w_qkv, w_out = refs[:7]
    parts, refs = refs[7 + count : 7 + count + moved], refs[7 + count + moved :]
    new_state, act_one, qkv, attn, middle, act_two, slope, hidden = refs[:8]
    fulls, wholes = refs[8 : 8 + count], refs[8 + count : 8 + count + moved]
    refs = refs[8 + count + moved :]
    v_qkv, v_out, v_up, v_down, terms, box, vec, vec_up = refs[:8]
    load, p_send, p_recv = refs[8:11]
    rings = refs[11:]
    core = lax.axis_index("core")
    length, width = state.shape
    half_width = width // 2
    loads = [
        pltpu.make_async_copy(w, v, load.at[i])
        for i, (w, v) in enumerate(((w_qkv, v_qkv), (w_out, v_out), (w_up, v_up), (w_down, v_down)))
    ]
    for copy in loads:
        copy.start()
    pos = positions()
    streams = sequences = None
    if count:
        greet(pos, False)
        streams = [
            Gather(pos, ORDERS[m], None, fulls[m], rings[0].at[m], rings[1].at[m])
            for m in range(count)
        ]
        for s in streams:
            s.begin(2)
    elif moved:
        greet(pos, True)
        sequences = Sequences(pos, parts, wholes, rings)
        sequences.begin()
    else:
        greet_pair()
    pair = Pair(terms, box, p_send, p_recv)
    for i, vector in enumerate((G_ONE, S_ONE, B_OUT, G_TWO, S_TWO, B_DOWN)):
        fill_vector(vec.at[i], small, vector, layer)
    for s in range(8):
        vec_up[0:1, pl.ds(s * TILE, TILE)] = vector_row(small, s, B_UP, layer, core, TILE)
    q_bias = []
    for s in range(8):
        row = vector_row(small, s, B_QV, layer, 0, 256)
        for at in (0, 2 * HEAD_DIM):
            q_bias.append(
                jnp.where(
                    core == 0,
                    row[:, at : at + HEAD_DIM],
                    row[:, at + HEAD_DIM : at + 2 * HEAD_DIM],
                )
            )
    vec_up[1:2, pl.ds(0, half_width)] = jnp.concatenate(q_bias[:8], axis=-1)
    vec_up[1:2, pl.ds(half_width, half_width)] = jnp.zeros((1, half_width), F32)
    vec_up[1:2, pl.ds(2 * half_width, half_width)] = jnp.concatenate(q_bias[8:], axis=-1)

    def first_norm(rows):
        normed, _ = norm_of(state[rows, :])
        act_one[rows, :] = (normed * vec[0] + vec[1]).astype(LOW)

    over_rows(length, first_norm)
    loads[0].wait()

    def project(t):
        here = tile_at(t)
        bias = vec_up[1:2, here]
        qkv[:, here] = (dot(act_one[...], v_qkv[:, here]) + bias).astype(LOW)

    over_tiles(3 * half_width // TILE, project)
    seg_row, seg_col = seg_row_col(segs)
    allowed = allowed_pairs(seg_col, seg_row)
    scale = 1.0 / math.sqrt(HEAD_DIM)
    for h in range(half_width // HEAD_DIM):
        q, k, v = (qkv[:, pl.ds(t * half_width + h * HEAD_DIM, HEAD_DIM)] for t in range(3))
        probs = head_probs(q, k, allowed, scale).astype(LOW)
        attn[:, pl.ds(h * HEAD_DIM, HEAD_DIM)] = dot(probs, v).astype(LOW)
    loads[1].wait()
    pair.fill(0, lambda t: dot(attn[...], v_out[:, tile_at(t)]))
    if moved:
        sequences.cross()
    pair.wait(0)

    def second_norm(rows):
        x = state[rows, :] + pair.total(0, rows) + vec[2]
        middle[rows, :] = x
        normed, _ = norm_of(x)
        act_two[rows, :] = (normed * vec[3] + vec[4]).astype(LOW)

    over_rows(length, second_norm)
    loads[2].wait()

    def expand(t):
        here = tile_at(t)
        value, rise = gelu_pair(dot(act_two[...], v_up[:, here]) + vec_up[0:1, here])
        hidden[:, here] = value.astype(LOW)
        slope[:, here] = rise

    over_tiles(slope.shape[1] // TILE, expand)
    if count:
        for s in streams:
            s.onward(2)
    loads[3].wait()
    pair.fill(1, lambda t: dot(hidden[...], v_down[:, tile_at(t)]))
    pair.wait(1)

    def close(rows):
        new_state[rows, :] = middle[rows, :] + pair.total(1, rows) + vec[5]

    over_rows(length, close)
    if count:
        for s in streams:
            s.finish(2)
        for s in streams:
            s.drain((2,))
    if moved:
        sequences.drain()


def weight_scratch(weights):
    w_up, w_down, w_qkv, w_out = weights
    return [pltpu.VMEM(w.shape, LOW) for w in (w_qkv, w_out, w_up, w_down)]


def pair_scratch(length, width):
    shape = (2, width // TILE, length, TILE)
    return [pltpu.VMEM(shape, F32), pltpu.VMEM(shape, F32)]


def forward_block(layer, state, segs, small, weights, begun, parts):
    count, moved = len(begun), len(parts)
    length, width = state.shape
    inner = weights[0].shape[1]
    shapes = [
        ((length, width), F32),
        ((length, width), LOW),
        ((length, 3 * width // 2), LOW),
        ((length, width // 2), LOW),
        ((length, width), F32),
        ((length, width), LOW),
        ((length, inner), F32),
        ((length, inner), LOW),
    ]
    shapes = [jax.ShapeDtypeStruct(*s) for s in shapes]
    shapes += [jax.ShapeDtypeStruct(b.shape, b.dtype) for b in begun]
    out = pl.pallas_call(
        functools.partial(forward_kernel, layer, count, moved),
        out_shape=shapes + sequence_shapes(parts),
        in_specs=[VMEM] * 3 + [ANY] * (4 + count + moved),
        out_specs=[VMEM] * 8 + [ANY] * (count + moved),
        input_output_aliases={7 + m: 8 + m for m in range(count)},
        scratch_shapes=weight_scratch(weights)
        + pair_scratch(length, width)
        + [
            pltpu.VMEM((6, 1, width), F32),
            pltpu.VMEM((2, inner), F32),
            DMA((4,)),
            DMA((2, width // TILE)),
            DMA((2, width // TILE)),
        ]
        + ([DMA((count, 12)), DMA((count, 12))] if count else [])
        + sequence_scratch(moved),
        compiler_params=pltpu.CompilerParams(
            collective_id=2 + layer, has_side_effects=True, vmem_limit_bytes=60 * 1024 * 1024
        ),
        name="forward_block",
    )(state, segs, small, *weights, *begun, *parts)
    return out[:8], out[8 : 8 + count], out[8 + count :]


def column_sum(target, row, value):
    target[row : row + 1, :] += jnp.sum(value, axis=0, keepdims=True)


def backward_kernel(layer, count, *refs):
    grad_state, state, middle, qkv, attn, slope, hidden, act_one, act_two, segs, small = refs[:11]
    w_up, w_down, w_qkv, w_out = refs[11:15]
    given, refs = refs[15 : 15 + count], refs[15 + count :]
    new_grad, totals = refs[0], refs[1:5]
    g_heads, g_out, small_grad = refs[5:8], refs[8], refs[9]
    sums, refs = refs[10 : 10 + count], refs[10 + count :]
    v_qkv, v_out, v_up, v_down, terms, box, vec, acc, acc_up, acc_qkv = refs[:10]
    grad_low, d_pre_low, mid_low, d_qkv, d_attn = refs[10:15]
    boxes, refs = refs[15:19], refs[19:]
    load, p_send, p_recv, o_send, o_recv = refs[:5]
    rings = refs[5:]
    core = lax.axis_index("core")
    length, width = state.shape
    half_width = width // 2
    inner = slope.shape[1]
    loads = [
        pltpu.make_async_copy(w, v, load.at[i])
        for i, (w, v) in enumerate(((w_down, v_down), (w_up, v_up), (w_out, v_out), (w_qkv, v_qkv)))
    ]
    for copy in loads:
        copy.start()
    pos = positions()
    greet(pos, False)
    streams, at = [], 0
    for m in range(count):
        take = 3 if m < SPLIT else 6
        sems = [rings[len(rings) - 3 + k].at[m] for k in range(3)]
        streams.append(scatter_of(pos, m, given[m], rings[at : at + take], (sums[m],), sems))
        at += take
    own = [
        Scatter(
            pos,
            SCATTERS[m],
            0,
            v_up if m < 2 else v_down,
            None,
            (boxes[m],),
            (totals[m],),
            o_send.at[m],
            o_recv.at[m],
            None,
            totals[m - 1].shape[-1] if m % 2 else 0,
        )
        for m in range(SPLIT)
    ]

    def carry(at):
        for s in streams:
            s.step(at)

    carry(0)
    pair = Pair(terms, box, p_send, p_recv)
    fill_vector(vec.at[0], small, G_ONE, layer)
    fill_vector(vec.at[1], small, G_TWO, layer)
    acc[...] = jnp.zeros_like(acc)
    tokens = ((0,), (0,))

    def down_rows(t):
        return (t // 2, pl.ds(lax.rem(t, 2) * 2, 2))

    def lower(rows):
        g = grad_state[rows, :]
        grad_low[rows, :] = g.astype(LOW)
        column_sum(acc, 0, g)

    over_rows(length, lower)
    loads[0].wait()

    def contract(t):
        here = tile_at(t)
        w = v_down[down_rows(t)].reshape(TILE, width)
        d_pre = dot(grad_low[...], w, ((1,), (1,))) * slope[:, here]
        d_pre_low[:, here] = d_pre.astype(LOW)
        acc_up[:, here] = jnp.sum(d_pre, axis=0, keepdims=True)

    over_tiles(inner // TILE, contract)
    carry(1)

    def down_grad(t):
        value = dot(hidden[:, tile_at(t)], grad_low[...], tokens)
        v_down[down_rows(t)] = value.reshape(2, RING, 32, width).astype(LOW)

    over_tiles(inner // TILE, down_grad)
    for s in own[2:]:
        s.begin(0)
    loads[1].wait()
    pair.fill(0, lambda t: dot(d_pre_low[...], v_up[t].reshape(TILE, inner), ((1,), (1,))))


    def up_grad(t):
        value = dot(act_two[:, tile_at(t)], d_pre_low[...], tokens)
        v_up[t] = value.reshape(RING, RING, 16, inner).astype(LOW)

    over_tiles(width // TILE, up_grad)
    for s in own[:2]:
        s.begin(0)
    pair.wait(0)

    def second_norm(rows):
        d_act = pair.total(0, rows)
        normed, factor = norm_of(middle[rows, :])
        column_sum(acc, 1, d_act * normed)
        column_sum(acc, 2, d_act)
        g = grad_state[rows, :] + norm_backward(d_act, normed, factor, vec[1])
        new_grad[rows, :] = g
        mid_low[rows, :] = g.astype(LOW)
        column_sum(acc, 3, g)

    over_rows(length, second_norm)
    carry(2)
    loads[2].wait()

    def attn_grad(t):
        here = tile_at(t)
        d_attn[:, here] = dot(mid_low[...], v_out[here, :], ((1,), (1,))).astype(LOW)

    over_tiles(half_width // TILE, attn_grad)

    def out_grad(t):
        value = dot(attn[:, tile_at(t)], mid_low[...], tokens)
        g_out[pl.ds(t * 2, 2)] = value.reshape(2, RING, RING, 8, width).astype(LOW)

    over_tiles(half_width // TILE, out_grad)
    seg_row, seg_col = seg_row_col(segs)
    allowed = allowed_pairs(seg_col, seg_row)
    scale = 1.0 / math.sqrt(HEAD_DIM)
    for h in range(half_width // HEAD_DIM):
        q, k, v = (qkv[:, pl.ds(t * half_width + h * HEAD_DIM, HEAD_DIM)] for t in range(3))
        here = pl.ds(h * HEAD_DIM, HEAD_DIM)
        d_head = d_attn[:, here]
        full = head_probs(q, k, allowed, scale)
        delta = jnp.sum(
            d_head.astype(F32) * attn[:, here].astype(F32), axis=-1, keepdims=True
        )
        d_scores = (full * (dot(d_head, v, ((1,), (1,))) - delta)).astype(LOW)
        ends = (
            dot(d_scores, k) * scale,
            dot(d_scores, q, ((0,), (0,))) * scale,
            dot(full.astype(LOW), d_head, ((0,), (0,))),
        )
        for t, end in enumerate(ends):
            place = pl.ds(t * half_width + h * HEAD_DIM, HEAD_DIM)
            d_qkv[:, place] = end.astype(LOW)
            acc_qkv[:, place] = jnp.sum(end, axis=0, keepdims=True)
        if h == 5:
            for s in own:
                s.onward(0)
    carry(3)
    loads[3].wait()
    pair.fill(1, lambda t: dot(d_qkv[...], v_qkv[tile_at(t), :], ((1,), (1,))))

    def head_grad(t):
        value = dot(act_one[:, tile_at(t)], d_qkv[...], tokens)
        for part in range(3):
            third = value[:, part * half_width : (part + 1) * half_width]
            g_heads[part][t] = third.reshape(RING, RING, 16, half_width).astype(LOW)

    over_tiles(width // TILE, head_grad)
    carry(4)
    pair.wait(1)

    def first_norm(rows):
        d_act = pair.total(1, rows)
        normed, factor = norm_of(state[rows, :])
        column_sum(acc, 4, d_act * normed)
        column_sum(acc, 5, d_act)
        new_grad[rows, :] += norm_backward(d_act, normed, factor, vec[0])

    over_rows(length, first_norm)
    small_grad[...] = jnp.zeros_like(small_grad)
    first = (core == 0).astype(F32)
    for s in range(8):
        here = pl.ds(s * 128, 128)
        target = small_grad.at[s // 2, pl.ds((s % 2) * 2, 2)]
        for vector, row in ((B_DOWN, 0), (G_TWO, 1), (S_TWO, 2), (B_OUT, 3), (G_ONE, 4), (S_ONE, 5)):
            target[vector // 4, vector % 4, 0:1, 0:128] = acc[row : row + 1, here] * first
        block = acc_up[:, pl.ds(s * TILE, TILE)]
        target[B_UP // 4, B_UP % 4, 0:1, :] = block * first
        target[B_UP // 4, B_UP % 4, 1:2, :] = block * (1.0 - first)
        at = (s // 4) * 2 * half_width + (s % 4) * 2 * HEAD_DIM
        heads = []
        for k in range(2):
            value = acc_qkv[:, pl.ds(at + k * HEAD_DIM, HEAD_DIM)]
            heads += [value * first, value * (1.0 - first)]
        target[B_QV // 4, B_QV % 4, 0:1, :] = jnp.concatenate(heads, axis=-1)
    carry(5)
    for s in own:
        s.finish(0)
    carry(6)
    for s in streams:
        s.drain()
    for s in own:
        s.drain((0,))


def backward_block(layer, grad_state, record, segs, small, weights, given):
    state = record[0]
    count = len(given)
    length, width = state.shape
    inner = record[4].shape[1]
    cube = (RING, RING, RING)
    w_up, w_down, w_qkv, w_out = weights
    halves = []
    for w, (share, of) in ((w_up, UP_PART), (w_down, DOWN_PART)):
        rows, cols = w.shape[3:]
        halves += [(rows, cols * share // of), (rows, cols - cols * share // of)]
    ends = [((length, width), F32)] + [((RING, RING) + h, LOW) for h in halves]
    ends += [(cube + (width // 64, width // 2), LOW)] * 3
    ends += [(cube + w_out.shape[3:], LOW), (cube + (8, 256), F32)]
    shapes = [jax.ShapeDtypeStruct(*e) for e in ends]
    shapes += [jax.ShapeDtypeStruct(g.shape[-2:], g.dtype) for g in given]
    bufs = []
    for m, g in enumerate(given):
        bufs += scatter_scratch(g.shape[-2:], g.dtype, 1 if m < SPLIT else 0, False)
    sems = [DMA((count, 18)), DMA((count, 18)), DMA((count, 5))] if count else []
    flat = [w.reshape(-1, w.shape[-1]) for w in (w_qkv, w_out)]
    out = pl.pallas_call(
        functools.partial(backward_kernel, layer, count),
        out_shape=shapes,
        in_specs=[VMEM] * 11 + [ANY] * 4 + [VMEM] * min(count, SPLIT) + [ANY] * max(count - SPLIT, 0),
        out_specs=[VMEM] * (10 + count),
        scratch_shapes=[pltpu.VMEM(w.shape, LOW) for w in flat + [w_up, w_down]]
        + pair_scratch(length, width)
        + [
            pltpu.VMEM((2, 1, width), F32),
            pltpu.VMEM((6, width), F32),
            pltpu.VMEM((1, inner), F32),
            pltpu.VMEM((1, 3 * width // 2), F32),
            pltpu.VMEM((length, width), LOW),
            pltpu.VMEM((length, inner), LOW),
            pltpu.VMEM((length, width), LOW),
            pltpu.VMEM((length, 3 * width // 2), LOW),
            pltpu.VMEM((length, width // 2), LOW),
        ]
        + [pltpu.VMEM((6, RING, RING, r, c // 2), LOW) for r, c in halves]
        + [
            DMA((4,)),
            DMA((2, width // TILE)),
            DMA((2, width // TILE)),
            DMA((SPLIT, 6)),
            DMA((SPLIT, 6)),
        ]
        + bufs
        + sems,
        compiler_params=pltpu.CompilerParams(
            collective_id=4 + layer, has_side_effects=True, vmem_limit_bytes=67043328
        ),
        name="backward_block",
    )(grad_state, *record, segs, small, w_up, w_down, *flat, *given)
    return out[0], list(out[1:10]), list(out[10:])


def finish_kernel(layers, *refs):
    ins, outs = refs[: 9 * layers], refs[9 * layers :]
    o_qkv, o_out, o_up, o_down = outs[:4]
    for l in range(layers):
        up_a, up_b, down_a, down_b, *qkv, out, small = ins[9 * l : 9 * l + 9]
        blocks = up_a.shape[-1] // TILE
        for s in range(8):
            for c in range(2):
                up, at = (up_a, s) if s < blocks else (up_b, s - blocks)
                o_up[l, :, pl.ds((2 * s + c) * TILE, TILE)] = up[c, 0, :, pl.ds(at * TILE, TILE)].astype(F32)
        for c in range(2):
            o_down[l, c, 0] = jnp.concatenate([down_a[c, 0], down_b[c, 0]], axis=-1).astype(F32)
            o_out[l, c, 0] = out[c, 0].astype(F32)
        for k in range(24):
            here = pl.ds((k % 8) * HEAD_DIM, HEAD_DIM)
            both = jnp.concatenate([qkv[k // 8][c, 0, :, here] for c in range(2)], axis=-1)
            o_qkv[l, :, pl.ds(k * 128, 128)] = both.astype(F32)

        @pl.when(pl.program_id(0) == 0)
        def _():
            for v in range(8):
                o = outs[4 + v]
                size = o.shape[1]
                for part in range((size + 255) // 256):
                    span = min(size, 256)
                    o[l : l + 1, pl.ds(part * 256, span)] = (
                        small[0, v, part : part + 1, 0:span] + small[1, v, part : part + 1, 0:span]
                    )


def finish(finals, sizes):
    layers = len(finals)
    in_specs, args = [], []
    for f in finals:
        for m, a in enumerate(f):
            r, c = a.shape[3:]
            args.append(a.reshape(2, 8, r, c))
            if m < 8:
                in_specs.append(pl.BlockSpec((2, 1, r, c), lambda p: (0, p, 0, 0)))
            else:
                in_specs.append(pl.BlockSpec((2, 8, r, c), lambda p: (0, 0, 0, 0)))
    up, up_b, down, down_b, qkv, _, _, out = (a.shape[2:] for a in args[:8])
    up, down = (up[0], up[1] + up_b[1]), (down[0], down[1] + down_b[1])
    shapes, specs = [], []
    for rows, cols in ((qkv[0], 6 * qkv[1]), (0, 0), (up[0], 2 * up[1])):
        if rows:
            shapes.append(jax.ShapeDtypeStruct((layers, 8 * rows, cols), F32))
            specs.append(pl.BlockSpec((layers, rows, cols), lambda p: (0, p, 0)))
        else:
            shapes.append(jax.ShapeDtypeStruct((layers, 2, 8) + out, F32))
            specs.append(pl.BlockSpec((layers, 2, 1) + out, lambda p: (0, 0, p, 0, 0)))
    shapes.append(jax.ShapeDtypeStruct((layers, 2, 8) + down, F32))
    specs.append(pl.BlockSpec((layers, 2, 1) + down, lambda p: (0, 0, p, 0, 0)))
    for size in sizes:
        shapes.append(jax.ShapeDtypeStruct((layers, size), F32))
        specs.append(pl.BlockSpec((layers, size), lambda p: (0, 0)))
    res = pl.pallas_call(
        functools.partial(finish_kernel, layers),
        out_shape=shapes,
        grid=(8,),
        in_specs=in_specs,
        out_specs=specs,
        name="finish",
    )(*args)
    o_out = res[1].reshape(layers, 16 * out[0], out[1])
    o_down = res[3].reshape(layers, 16 * down[0], down[1])
    return (res[0], o_out, res[2], o_down) + tuple(res[4:])


def prepare_kernel(where, up, down, qkv, out, segment_ids, *refs):
    vectors, refs = refs[:8], refs[8:]
    layers = up.shape[0]
    sub, core = where[0], where[1]
    for l in range(layers):
        o_up, o_down, o_qkv, o_out = refs[4 * l : 4 * l + 4]
        o_down[...] = down[l]
        o_out[...] = out[l]
        for s in range(8):
            at = pl.multiple_of((2 * s + core) * TILE, TILE)
            o_up[:, pl.ds(s * TILE, TILE)] = up[l, :, pl.ds(at, TILE)]
        for k in range(12):
            two = []
            for j in range(2):
                pair = qkv[l, :, pl.ds((2 * k + j) * 128, 128)]
                two.append(jnp.where(core == 0, pair[:, :HEAD_DIM], pair[:, HEAD_DIM:]))
            o_qkv[:, pl.ds(k * 128, 128)] = jnp.concatenate(two, axis=-1)
    small, segs = refs[4 * layers :]
    small[...] = jnp.zeros_like(small)
    for v, vector in enumerate(vectors):

        @pl.when(sub == v)
        def _():
            size = vector.shape[1]
            for part in range((size + 255) // 256):
                span = min(size, 256)
                block = vector[:, pl.ds(part * 256, span)].astype(F32)
                for l in range(layers):
                    small[2 * l + part : 2 * l + part + 1, 0:span] = block[l : l + 1]

    segs[...] = jnp.zeros_like(segs)
    for b in range(segs.shape[0]):
        segs[b, 0:1, 0 : segment_ids.shape[1]] = segment_ids[b : b + 1, :].astype(F32)


def prepare(weights, segment_ids, vectors):
    up, down, qkv, out = weights
    layers, rows = up.shape[:2]
    piece, down_rows, out_rows = rows // 8, down.shape[1] // 16, rows // 16
    where = jnp.stack(
        [lax.axis_index("xl") * 4 + lax.axis_index("y"), lax.axis_index("core")]
    ).astype(jnp.int32)
    per_layer = [
        (piece, up.shape[2] // 2),
        (down_rows, down.shape[2]),
        (piece, qkv.shape[2] // 2),
        (out_rows, out.shape[2]),
    ]
    shapes = [jax.ShapeDtypeStruct(e, LOW) for e in per_layer] * layers
    shapes += [jax.ShapeDtypeStruct((8, 256), F32), jax.ShapeDtypeStruct((2, 8, 128), F32)]
    by_row = lambda i, where: (0, where[0], 0)
    by_half = lambda i, where: (0, 8 * where[1] + where[0], 0)
    whole = lambda a: pl.BlockSpec(a.shape, lambda i, where: (0,) * len(a.shape))
    made = pl.pallas_call(
        prepare_kernel,
        out_shape=shapes,
        grid_spec=pltpu.PrefetchScalarGridSpec(
            num_scalar_prefetch=1,
            grid=(1,),
            in_specs=[
                pl.BlockSpec((layers, piece, up.shape[2]), by_row),
                pl.BlockSpec((layers, down_rows, down.shape[2]), by_half),
                pl.BlockSpec((layers, piece, qkv.shape[2]), by_row),
                pl.BlockSpec((layers, out_rows, out.shape[2]), by_half),
                whole(segment_ids),
            ]
            + [whole(v) for v in vectors],
            out_specs=[whole(e) for e in shapes],
        ),
        name="prepare",
    )(where, up, down, qkv, out, segment_ids, *vectors)
    owns = [made[4 * l : 4 * l + 4] for l in range(layers)]
    return owns, made[4 * layers], made[4 * layers + 1]


def per_device(
    inputs,
    segment_ids,
    weight_qkv,
    weight_out,
    weight_up,
    weight_down,
    bias_qv,
    bias_out,
    bias_up,
    bias_down,
    gain_one,
    shift_one,
    gain_two,
    shift_two,
    cotangent,
):
    layers, width = weight_qkv.shape[0], inputs.shape[-1]
    length = inputs.shape[1] * RING
    vectors = (bias_qv, bias_out, bias_up, bias_down, gain_one, shift_one, gain_two, shift_two)
    sizes = [v.shape[1] for v in vectors]
    owns, packed, segs = prepare((weight_up, weight_down, weight_qkv, weight_out), segment_ids, vectors)
    fulls, begun, wholes = gather_all(list(owns[0]) + [packed], list(owns[1]), [inputs, segs])
    state, segs = wholes[0].reshape(length, width), wholes[1]
    small = fulls[4].reshape(8, 8, 8, 256)
    records = []
    weights = [fulls[:4]]
    for l in range(layers):
        carried, parts = (begun, []) if l == 0 else ([], [cotangent])
        flat = [w.reshape(-1, w.shape[-1]) for w in weights[l]]
        made, fulls, wholes = forward_block(l, state, segs, small, flat, list(carried), parts)
        weights.append(fulls)
        new_state, act_one, qkv, attn, middle, act_two, slope, hidden = made
        records.append((state, middle, qkv, attn, slope, hidden, act_one, act_two))
        state = new_state
    grad_state = wholes[0].reshape(length, width)
    pieces = []
    for l in reversed(range(layers)):
        grad_state, pieces, sums = backward_block(
            l, grad_state, records[l], segs, small, weights[l], pieces
        )
    quarter = (RING, length // RING, width)
    finals, others, parts = scatter_all(
        pieces, sums, [state.reshape(quarter), grad_state.reshape(quarter)]
    )
    return (parts[0], parts[1]) + finish([finals, others], sizes)


def solution(mesh):
    torus = Mesh(mesh.devices.reshape(4, 2, 4, 2, 2), AXES)
    tokens = P(("xh", "y", "xl", "core"), "z", None)
    weight = P(None, ("z", "xh"), None)
    vector = P(None, ("z", "xh"))
    return jax.shard_map(
        per_device,
        mesh=torus,
        in_specs=(tokens, P(("xh", "y", "xl", "core"), "z")) + (weight,) * 4 + (vector,) * 8 + (tokens,),
        out_specs=(tokens, tokens) + (weight,) * 4 + (vector,) * 8,
        check_vma=False,
    )
```

```python
import functools
import math

import jax
import jax.numpy as jnp
from jax import lax
from jax.experimental import pallas as pl
from jax.experimental.pallas import tpu as pltpu
from jax.sharding import Mesh
from jax.sharding import PartitionSpec as P

AXES = ("z", "xh", "y", "xl", "core")
RING = 4
ANY = pl.BlockSpec(memory_space=pl.ANY)
VMEM = pl.BlockSpec(memory_space=pltpu.VMEM)
DMA = pltpu.SemaphoreType.DMA
SCATTERS = ("xyz", "yzx", "zxy", "yxz", "xyz", "zyx", "yzx", "yxz", "yzx")
SPLIT = 4
UP_PART, DOWN_PART = (5, 8), (3, 4)
ORDERS = ("xyz", "zxy", "yzx", "yzx")


def positions():
    return {
        "z": lax.axis_index("z"),
        "x": lax.axis_index("xh") * 2 + lax.axis_index("xl"),
        "y": lax.axis_index("y"),
    }


def neighbour(pos, axis, step):
    at = lax.rem(pos[axis] + step + RING, RING)
    if axis == "x":
        return {"xh": at // 2, "xl": lax.rem(at, 2)}
    return {axis: at}


def remote(src, dst, send, recv, target):
    return pltpu.make_async_remote_copy(
        src_ref=src,
        dst_ref=dst,
        send_sem=send,
        recv_sem=recv,
        device_id=target,
        device_id_type=pl.DeviceIdType.MESH,
    )


def greet(pos, with_column):
    barrier = pltpu.get_barrier_semaphore()
    targets = [neighbour(pos, axis, step) for axis in "xyz" for step in (1, -1)]
    if with_column:
        targets.append(neighbour(pos, "z", 2))
    targets.append({"core": 1 - lax.axis_index("core")})
    for target in targets:
        pl.semaphore_signal(
            barrier, inc=1, device_id=target, device_id_type=pl.DeviceIdType.MESH
        )
    pl.semaphore_wait(barrier, len(targets))


def half(ref, which, rows, cols):
    lead = (slice(None),) * (len(ref.shape) - 2)
    if rows % 16 == 0:
        return ref.at[lead + (pl.ds(which * (rows // 2), rows // 2), slice(None))]
    return ref.at[lead + (slice(None), pl.ds(which * (cols // 2), cols // 2))]


class Gather:
    def __init__(self, pos, order, own, full, send, recv):
        self.pos, self.order, self.own, self.full = pos, order, own, full
        self.send, self.recv = send, recv
        self.rows, self.cols = full.shape[-2:]

    def view(self, stage, shift):
        index = {}
        for place, axis in enumerate(self.order):
            if place < stage:
                index[axis] = slice(None)
            elif place == stage:
                index[axis] = lax.rem(self.pos[axis] + shift + RING, RING)
            else:
                index[axis] = self.pos[axis]
        return self.full.at[index["z"], index["x"], index["y"]]

    def copy(self, stage, kind):
        axis = self.order[stage]
        sems = (self.send.at[stage * 4 + kind], self.recv.at[stage * 4 + kind])
        target = neighbour(self.pos, axis, 1 if kind % 2 == 0 else -1)
        if kind < 2:
            src = self.own if stage == 0 else self.view(stage, 0)
            return remote(src, self.view(stage, 0), *sems, target)
        piece = half(self.view(stage, -1 if kind == 2 else 1), kind - 2, self.rows, self.cols)
        return remote(piece, piece, *sems, target)

    def arrive(self, stage, kind):
        sems = (self.send.at[stage * 4 + kind], self.recv.at[stage * 4 + kind])
        axis = self.order[stage]
        if kind < 2:
            piece = self.view(stage, -1 if kind == 0 else 1)
        else:
            piece = half(self.view(stage, 2), kind - 2, self.rows, self.cols)
        remote(piece, piece, *sems, neighbour(self.pos, axis, 1)).wait_recv()

    def begin(self, stage):
        for kind in (0, 1):
            self.copy(stage, kind).start()

    def onward(self, stage):
        for kind in (0, 1):
            self.arrive(stage, kind)
            self.copy(stage, kind + 2).start()

    def finish(self, stage):
        for kind in (2, 3):
            self.arrive(stage, kind)

    def drain(self, stages):
        for stage in stages:
            for kind in range(4):
                self.copy(stage, kind).wait_send()


class Sequences:
    def __init__(self, pos, parts, wholes, sems):
        self.pos, self.parts, self.wholes = pos, parts, wholes
        self.send, self.recv, self.core_send, self.core_recv, self.local = sems
        self.core = lax.axis_index("core")
        self.receiver = pos["z"] // 2 == self.core

    def outward(self, a, b, home):
        return remote(
            self.parts[a].at[b],
            self.wholes[a].at[self.pos["z"]],
            self.send.at[a, b],
            self.recv.at[a, self.pos["z"]],
            {"z": home},
        )

    def crossing(self, a, q):
        piece = self.wholes[a].at[q]
        return remote(
            piece, piece, self.core_send.at[a, q], self.core_recv.at[a, q], {"core": 1 - self.core}
        )

    def staying(self, a, b):
        return pltpu.make_async_copy(
            self.parts[a].at[b], self.wholes[a].at[self.pos["z"]], self.local.at[a]
        )

    def begin(self):
        for a in range(len(self.parts)):
            for b in range(2):
                home = 2 * self.core + b

                @pl.when(home == self.pos["z"])
                def _():
                    self.staying(a, b).start()

                @pl.when(home != self.pos["z"])
                def _():
                    self.outward(a, b, home).start()

    def cross(self):
        @pl.when(self.receiver)
        def _():
            for a in range(len(self.parts)):
                for q in range(RING):

                    @pl.when(q == self.pos["z"])
                    def _():
                        self.staying(a, 0).wait()

                    @pl.when(q != self.pos["z"])
                    def _():
                        piece = self.wholes[a].at[q]
                        remote(
                            piece,
                            piece,
                            self.send.at[a, 0],
                            self.recv.at[a, q],
                            {"z": lax.rem(self.pos["z"] + 1, RING)},
                        ).wait_recv()

                    self.crossing(a, q).start()

    def drain(self):
        for a in range(len(self.parts)):
            for b in range(2):
                home = 2 * self.core + b

                @pl.when(home != self.pos["z"])
                def _():
                    self.outward(a, b, lax.rem(self.pos["z"] + 1, RING)).wait_send()

            for q in range(RING):

                @pl.when(self.receiver)
                def _():
                    self.crossing(a, q).wait_send()

                @pl.when(jnp.logical_not(self.receiver))
                def _():
                    self.crossing(a, q).wait_recv()


def sequence_scratch(moved):
    sems = [DMA((moved, 2)), DMA((moved, RING)), DMA((moved, RING)), DMA((moved, RING)), DMA((moved,))]
    return sems if moved else []


def sequence_shapes(parts):
    return [jax.ShapeDtypeStruct((RING,) + p.shape[1:], p.dtype) for p in parts]


def gather_kernel(count, whole, moved, *refs):
    owns, parts = refs[:count], refs[count : count + moved]
    refs = refs[count + moved :]
    fulls, wholes = refs[:count], refs[count : count + moved]
    send, recv, local = refs[count + moved : count + moved + 3]
    pos = positions()
    greet(pos, True)
    sequences = Sequences(pos, parts, wholes, refs[count + moved + 3 :])
    streams, keeps = [], []
    for m in range(count):
        keeps.append(
            pltpu.make_async_copy(
                owns[m], fulls[m].at[pos["z"], pos["x"], pos["y"]], local.at[m]
            )
        )
        streams.append(
            Gather(pos, ORDERS[m % whole % 4], owns[m], fulls[m], send.at[m], recv.at[m])
        )
    for keep in keeps:
        keep.start()
    for s in streams:
        s.begin(0)
    sequences.begin()
    for stage in range(3):
        running = streams if stage < 2 else streams[:whole]
        for s in running:
            s.onward(stage)
        if stage == 0:
            for keep in keeps:
                keep.wait()
        for m, s in enumerate(running):
            s.finish(stage)
            if stage == 0 or (stage == 1 and m < whole):
                s.begin(stage + 1)
        if stage == 1:
            sequences.cross()
    for m, s in enumerate(streams):
        s.drain(range(3 if m < whole else 2))
    sequences.drain()


def gather_all(owns, begun, parts):
    count, moved = len(owns) + len(begun), len(parts)
    shapes = [
        jax.ShapeDtypeStruct((RING, RING, RING) + o.shape, o.dtype) for o in owns + begun
    ]
    out = pl.pallas_call(
        functools.partial(gather_kernel, count, len(owns), moved),
        out_shape=shapes + sequence_shapes(parts),
        in_specs=[ANY] * (count + moved),
        out_specs=[ANY] * (count + moved),
        scratch_shapes=[DMA((count, 12)), DMA((count, 12)), DMA((count,))]
        + sequence_scratch(moved),
        compiler_params=pltpu.CompilerParams(collective_id=0, has_side_effects=True),
        name="gather_all",
    )(*owns, *begun, *parts)
    return out[: len(owns)], out[len(owns) : count], out[count:]


def scatter_scratch(end, kind, start, last):
    r, c = end
    scratch = [] if start else [pltpu.VMEM((4, RING, RING, r, c // 2), kind)]
    for stage in range(start, 3):
        scratch.append(pltpu.VMEM((6,) + (RING,) * (2 - stage) + (r, c // 2), kind))
    for stage in range(start, 3 if last else 2):
        scratch.append(pltpu.VMEM((RING,) * (2 - stage) + (r, c), kind))
    return scratch


def scatter_of(pos, m, source, bufs, sums, sems):
    start = 1 if m < SPLIT else 0
    stages = 3 - start
    own = None if start else bufs[0]
    rest = list(bufs[1 - start :])
    boxes, more = [None] * start + rest[:stages], rest[stages:]
    sums = ([source] if start else []) + more + list(sums)
    return Scatter(pos, SCATTERS[m], start, None if start else source, own, boxes, sums, *sems)


class Scatter:
    def __init__(self, pos, order, start, grad, own, boxes, sums, send, recv, local, base=0):
        self.pos, self.order, self.start, self.grad = pos, order, start, grad
        self.own, self.boxes, self.sums = own, boxes, sums
        self.send, self.recv, self.local = send, recv, local
        self.part, self.base = sums[0].shape[-1] // 2, base

    def piece(self, stage, shift, which):
        axis = self.order[stage]
        left = [a for a in "zxy" if a in self.order[stage:]]
        source = self.grad if stage == 0 else self.sums[stage - 1]
        at = lax.rem(self.pos[axis] + shift + RING, RING)
        index = tuple(at if a == axis else slice(None) for a in left) + (slice(None),)
        base = self.base if stage == 0 else 0
        return source.at[index + (pl.ds(base + which * self.part, self.part),)]

    def box(self, stage, kind):
        return self.boxes[stage].at[kind]

    def copy(self, stage, kind):
        src, step = {
            0: (lambda: self.piece(stage, 2, 0), 1),
            1: (lambda: self.piece(stage, 1, 1), 1),
            2: (lambda: self.piece(stage, -2, 1), -1),
            3: (lambda: self.piece(stage, -1, 0), -1),
            4: (lambda: self.box(stage, 0), 1),
            5: (lambda: self.box(stage, 2), -1),
        }[kind]
        return remote(
            src(),
            self.box(stage, kind),
            self.send.at[stage * 6 + kind],
            self.recv.at[stage * 6 + kind],
            neighbour(self.pos, self.order[stage], step),
        )

    def loads(self):
        for slot, (shift, which) in enumerate(((1, 0), (-1, 1), (0, 0), (0, 1))):
            yield pltpu.make_async_copy(
                self.piece(0, shift, which), self.own.at[slot], self.local.at[slot]
            )

    def begin(self, stage):
        for kind in range(4):
            self.copy(stage, kind).start()
        if stage == 0 and self.own is not None:
            for load in self.loads():
                load.start()

    def term(self, stage, slot):
        if stage == 0 and self.own is not None:
            return self.own.at[slot]
        shift, which = ((1, 0), (-1, 1), (0, 0), (0, 1))[slot]
        return self.piece(stage, shift, which)

    def add(self, stage, target, terms):
        lead = 2 - stage

        def one(index):
            total = terms[0][index].astype(jnp.float32)
            for t in terms[1:]:
                total = total + t[index].astype(jnp.float32)
            target[index] = total.astype(target.dtype)

        if lead < 2:
            one((slice(None),) * (lead + 2))
            return

        def body(i, carry):
            one((i, slice(None), slice(None), slice(None)))
            return carry

        lax.fori_loop(0, RING, body, 0)

    def onward(self, stage):
        if stage == 0 and self.own is not None:
            for load in self.loads():
                load.wait()
        for slot, kind in ((0, 0), (1, 2)):
            self.copy(stage, kind).wait_recv()
            box = self.box(stage, kind)
            self.add(stage, box, (box, self.term(stage, slot)))
            self.copy(stage, 4 + slot).start()

    def finish(self, stage):
        for kind in (1, 3, 4, 5):
            self.copy(stage, kind).wait_recv()
        lead = (slice(None),) * (3 - stage)
        for which, kinds in ((0, (3, 4)), (1, (1, 5))):
            target = self.sums[stage].at[lead + (pl.ds(which * self.part, self.part),)]
            self.add(
                stage,
                target,
                (self.term(stage, 2 + which),) + tuple(self.box(stage, k) for k in kinds),
            )

    def steps(self):
        return 2 * (3 - self.start) + 1

    def step(self, at):
        if at == 0:
            self.begin(self.start)
        elif at < self.steps():
            stage = self.start + (at - 1) // 2
            if at % 2:
                self.onward(stage)
            else:
                self.finish(stage)
                if stage < 2:
                    self.begin(stage + 1)

    def drain(self, stages=None):
        for stage in range(self.start, 3) if stages is None else stages:
            for kind in range(6):
                self.copy(stage, kind).wait_send()


class Publish:
    def __init__(self, pos, across, source, final, sends, recvs, local):
        self.pos, self.across, self.source, self.final = pos, across, source, final
        self.sends_f, self.recvs_f, self.local = sends, recvs, local
        self.core, self.xl = lax.axis_index("core"), lax.axis_index("xl")
        self.part = source.shape[-1] // 2

    def across_first(self):
        return self.across

    def block(self, shift):
        yi = lax.rem(self.pos["y"] + shift + RING, RING)
        xs = slice(None) if self.across_first() else self.xl
        return self.final.at[self.core, xs, yi]

    def spread(self, kind, own=False):
        sems = (self.sends_f.at[kind], self.recvs_f.at[kind])
        if kind == 5:
            whole = self.final.at[self.core]
            return remote(whole, whole, *sems, {"core": 1 - self.core})
        if kind == 4:
            if self.across_first():
                dst = self.final.at[self.core, self.xl, self.pos["y"]]
                src = self.source
            else:
                src = dst = self.final.at[self.core, self.xl]
            return remote(src, dst, *sems, {"xl": 1 - self.xl})
        target = neighbour(self.pos, "y", 1 if kind % 2 == 0 else -1)
        if kind < 2:
            dst = self.block(0)
            src = dst if self.across_first() else self.source
            return remote(src, dst, *sems, target)
        ref = self.block(-1 if kind == 2 else 1)
        lead = (slice(None),) * (len(ref.shape) - 1)
        ref = ref.at[lead + (pl.ds((kind - 2) * self.part, self.part),)]
        return remote(ref, ref, *sems, target)

    def spread_arrives(self, kind):
        sems = (self.sends_f.at[kind], self.recvs_f.at[kind])
        if kind == 5:
            ref = self.final.at[1 - self.core]
        elif kind == 4:
            ref = self.final.at[self.core, 1 - self.xl]
            if self.across_first():
                ref = ref.at[self.pos["y"]]
        elif kind < 2:
            ref = self.block(-1 if kind == 0 else 1)
        else:
            ref = self.block(2)
            lead = (slice(None),) * (len(ref.shape) - 1)
            ref = ref.at[lead + (pl.ds((kind - 2) * self.part, self.part),)]
        remote(ref, ref, *sems, {"core": 1 - self.core}).wait_recv()

    def keep(self):
        return pltpu.make_async_copy(
            self.source,
            self.final.at[self.core, self.xl, self.pos["y"]],
            self.local,
        )

    def publish(self, step):
        if step == 0:
            self.keep().start()
            for kind in (4,) if self.across_first() else (0, 1):
                self.spread(kind).start()
        elif self.across_first():
            if step == 1:
                self.keep().wait()
                self.spread_arrives(4)
                for kind in (0, 1):
                    self.spread(kind).start()
            elif step == 2:
                for kind in (0, 1):
                    self.spread_arrives(kind)
                    self.spread(kind + 2).start()
            elif step == 3:
                for kind in (2, 3):
                    self.spread_arrives(kind)
        else:
            if step == 1:
                self.keep().wait()
                for kind in (0, 1):
                    self.spread_arrives(kind)
                    self.spread(kind + 2).start()
            elif step == 2:
                for kind in (2, 3):
                    self.spread_arrives(kind)
                self.spread(4).start()
            elif step == 3:
                self.spread_arrives(4)
        if step == 3:
            self.spread(5).start()
        if step == 4:
            self.spread_arrives(5)

    def drain(self):
        for kind in range(6):
            self.spread(kind).wait_send()


MATRICES = 9


def scatter_kernel(moved, *refs):
    grads, given = refs[:MATRICES], refs[MATRICES : 2 * MATRICES]
    wholes, refs = refs[2 * MATRICES : 2 * MATRICES + moved], refs[2 * MATRICES + moved :]
    finals, parts = refs[: 2 * MATRICES], refs[2 * MATRICES : 2 * MATRICES + moved]
    refs = refs[2 * MATRICES + moved :]
    send, recv, local, sends_f, recvs_f, keeps, send_t, recv_t, local_t = refs[-9:]
    pos = positions()
    core = lax.axis_index("core")
    greet(pos, True)
    streams, at = [], 0
    for m in range(MATRICES):
        take = 4 if m < SPLIT else 7
        sems = (send.at[m], recv.at[m], local.at[m])
        streams.append(scatter_of(pos, m, grads[m], refs[at : at + take], (), sems))
        at += take
    news = [
        Publish(
            pos, m % MATRICES in (0, 1, 4, 5, 6), source, finals[m], sends_f.at[m], recvs_f.at[m], keeps.at[m]
        )
        for m, source in enumerate([s.sums[2] for s in streams] + list(given))
    ]
    sender = pos["z"] // 2 == core
    slot = lax.rem(pos["z"], 2)

    def homeward(a, q):
        return remote(
            wholes[a].at[q], parts[a].at[slot], send_t.at[a, q], recv_t.at[a, slot], {"z": q}
        )

    def staying(a):
        return pltpu.make_async_copy(wholes[a].at[pos["z"]], parts[a].at[slot], local_t.at[a])

    for a in range(moved):
        for q in range(RING):

            @pl.when(sender & (pos["z"] == q))
            def _():
                staying(a).start()

            @pl.when(sender & (pos["z"] != q))
            def _():
                homeward(a, q).start()

    for at in range(11):
        for n in news[MATRICES:]:
            if at < 5:
                n.publish(at)
        for s, n in zip(streams, news):
            s.step(at)
            if 0 <= at - s.steps() + 1 < 5:
                n.publish(at - s.steps() + 1)
    for s in streams:
        s.drain()
    for n in news:
        n.drain()
    for a in range(moved):
        for q in range(RING):

            @pl.when(sender & (pos["z"] == q))
            def _():
                staying(a).wait()

            @pl.when(sender & (pos["z"] != q))
            def _():
                homeward(a, q).wait_send()

        for b in range(2):

            @pl.when(2 * core + b != pos["z"])
            def _():
                remote(
                    parts[a].at[b],
                    parts[a].at[b],
                    send_t.at[a, 0],
                    recv_t.at[a, b],
                    {"z": lax.rem(pos["z"] + 1, RING)},
                ).wait_recv()


def scatter_all(grads, given, wholes):
    moved = len(wholes)
    ends = [g.shape[-2:] for g in grads] * 2
    kinds = [g.dtype for g in grads] * 2
    shapes = [jax.ShapeDtypeStruct((2, 2, RING) + e, k) for e, k in zip(ends, kinds)]
    shapes += [jax.ShapeDtypeStruct((2,) + w.shape[1:], w.dtype) for w in wholes]
    bufs = []
    for m in range(MATRICES):
        bufs += scatter_scratch(ends[m], kinds[m], 1 if m < SPLIT else 0, True)
    out = pl.pallas_call(
        functools.partial(scatter_kernel, moved),
        out_shape=shapes,
        in_specs=[VMEM] * SPLIT + [ANY] * (2 * MATRICES - SPLIT + moved),
        out_specs=[ANY] * (2 * MATRICES + moved),
        scratch_shapes=bufs
        + [
            DMA((MATRICES, 18)),
            DMA((MATRICES, 18)),
            DMA((MATRICES, 5)),
            DMA((2 * MATRICES, 6)),
            DMA((2 * MATRICES, 6)),
            DMA((2 * MATRICES,)),
            DMA((moved, RING)),
            DMA((moved, 2)),
            DMA((moved,)),
        ],
        compiler_params=pltpu.CompilerParams(
            collective_id=1, has_side_effects=True, vmem_limit_bytes=62 * 1024 * 1024
        ),
        name="scatter_all",
    )(*grads, *given, *wholes)
    return out[:MATRICES], out[MATRICES : 2 * MATRICES], out[2 * MATRICES :]


NORM_EPS = 1e-05
GELU_COEF = 0.7978845608028654
CUBIC_COEF = 0.044715
HEAD_DIM = 64
LOW = jnp.bfloat16
F32 = jnp.float32
TILE = 256
ROWS = 32
B_QV, B_OUT, B_UP, B_DOWN, G_ONE, S_ONE, G_TWO, S_TWO = range(8)


def dot(left, right, dims=((1,), (0,))):
    return lax.dot_general(left, right, (dims, ((), ())), preferred_element_type=F32)


def tile_at(t, size=TILE):
    return pl.ds(pl.multiple_of(t * size, size), size)


def over_rows(count, body):
    def step(i, carry):
        body(pl.ds(pl.multiple_of(i * ROWS, ROWS), ROWS))
        return carry

    lax.fori_loop(0, count // ROWS, step, 0)


def over_tiles(count, body):
    def step(t, carry):
        body(t)
        return carry

    lax.fori_loop(0, count, step, 0)


def head_probs(q, k, allowed, scale):
    scores = jnp.where(allowed, dot(q, k, ((1,), (1,))) * scale, -jnp.inf)
    top = jnp.max(scores, axis=-1, keepdims=True)
    lse = top + jnp.log(jnp.sum(jnp.exp(scores - top), axis=-1, keepdims=True))
    return jnp.exp(scores - lse)


def allowed_pairs(seg_col, seg_row):
    length = seg_col.shape[0]
    row = lax.broadcasted_iota(jnp.int32, (length, length), 0)
    col = lax.broadcasted_iota(jnp.int32, (length, length), 1)
    return (row >= col) & (seg_col == seg_row)


def norm_of(x):
    center = x - jnp.mean(x, axis=-1, keepdims=True)
    factor = lax.rsqrt(jnp.mean(center * center, axis=-1, keepdims=True) + NORM_EPS)
    return center * factor, factor


def norm_backward(d_act, normed, factor, gain):
    d_norm = d_act * gain
    return factor * (
        d_norm
        - jnp.mean(d_norm, axis=-1, keepdims=True)
        - normed * jnp.mean(d_norm * normed, axis=-1, keepdims=True)
    )


def gelu_pair(pre_act):
    cubic = pre_act * pre_act * pre_act
    tangent = jnp.tanh(GELU_COEF * (pre_act + CUBIC_COEF * cubic))
    gelu_value = 0.5 * pre_act * (1.0 + tangent)
    gelu_slope = 0.5 * (1.0 + tangent) + 0.5 * pre_act * (1.0 - tangent * tangent) * GELU_COEF * (
        1.0 + 3.0 * CUBIC_COEF * pre_act * pre_act
    )
    return gelu_value, gelu_slope


def vector_row(small, shard, vector, layer, part, size):
    return small[shard, vector, pl.ds(2 * layer + part, 1), pl.ds(0, size)]


def fill_vector(target, small, vector, layer):
    for s in range(8):
        target[:, pl.ds(s * 128, 128)] = vector_row(small, s, vector, layer, 0, 128)


class Pair:
    def __init__(self, terms, box, send, recv):
        self.terms, self.box, self.send, self.recv = terms, box, send, recv
        self.other = {"core": 1 - lax.axis_index("core")}

    def copy(self, which, t):
        return remote(
            self.terms.at[which, t],
            self.box.at[which, t],
            self.send.at[which, t],
            self.recv.at[which, t],
            self.other,
        )

    def fill(self, which, make):
        count = self.terms.shape[1]

        def body(t):
            self.terms[which, t] = make(t)

            @pl.when(t > 0)
            def _():
                self.copy(which, t - 1).start()

        over_tiles(count, body)
        self.copy(which, count - 1).start()

    def wait(self, which):
        for t in range(self.terms.shape[1]):
            self.copy(which, t).wait()

    def total(self, which, rows):
        return jnp.concatenate(
            [
                self.terms[which, t, rows, :] + self.box[which, t, rows, :]
                for t in range(self.terms.shape[1])
            ],
            axis=-1,
        )


def greet_pair():
    barrier = pltpu.get_barrier_semaphore()
    pl.semaphore_signal(
        barrier,
        inc=1,
        device_id={"core": 1 - lax.axis_index("core")},
        device_id_type=pl.DeviceIdType.MESH,
    )
    pl.semaphore_wait(barrier, 1)


def nothing(*_):
    pass


def seg_row_col(segs):
    row = jnp.concatenate([segs[q, 0:1, 0:80] for q in range(RING)], axis=-1)
    length = row.shape[1]
    at = lax.broadcasted_iota(jnp.int32, (length, length), 0)
    to = lax.broadcasted_iota(jnp.int32, (length, length), 1)
    return row, jnp.sum(jnp.where(at == to, row, 0.0), axis=-1, keepdims=True)


def forward_kernel(layer, count, moved, *refs):
    state, segs, small, w_up, w_down, w_qkv, w_out = refs[:7]
    parts, refs = refs[7 + count : 7 + count + moved], refs[7 + count + moved :]
    new_state, act_one, qkv, attn, middle, act_two, slope, hidden = refs[:8]
    fulls, wholes = refs[8 : 8 + count], refs[8 + count : 8 + count + moved]
    refs = refs[8 + count + moved :]
    v_qkv, v_out, v_up, v_down, terms, box, vec, vec_up = refs[:8]
    load, p_send, p_recv = refs[8:11]
    rings = refs[11:]
    core = lax.axis_index("core")
    length, width = state.shape
    half_width = width // 2
    loads = [
        pltpu.make_async_copy(w, v, load.at[i])
        for i, (w, v) in enumerate(((w_qkv, v_qkv), (w_out, v_out), (w_up, v_up), (w_down, v_down)))
    ]
    for copy in loads:
        copy.start()
    pos = positions()
    streams = sequences = None
    if count:
        greet(pos, False)
        streams = [
            Gather(pos, ORDERS[m], None, fulls[m], rings[0].at[m], rings[1].at[m])
            for m in range(count)
        ]
        for s in streams:
            s.begin(2)
    elif moved:
        greet(pos, True)
        sequences = Sequences(pos, parts, wholes, rings)
        sequences.begin()
    else:
        greet_pair()
    pair = Pair(terms, box, p_send, p_recv)
    for i, vector in enumerate((G_ONE, S_ONE, B_OUT, G_TWO, S_TWO, B_DOWN)):
        fill_vector(vec.at[i], small, vector, layer)
    for s in range(8):
        vec_up[0:1, pl.ds(s * TILE, TILE)] = vector_row(small, s, B_UP, layer, core, TILE)
    q_bias = []
    for s in range(8):
        row = vector_row(small, s, B_QV, layer, 0, 256)
        for at in (0, 2 * HEAD_DIM):
            q_bias.append(
                jnp.where(
                    core == 0,
                    row[:, at : at + HEAD_DIM],
                    row[:, at + HEAD_DIM : at + 2 * HEAD_DIM],
                )
            )
    vec_up[1:2, pl.ds(0, half_width)] = jnp.concatenate(q_bias[:8], axis=-1)
    vec_up[1:2, pl.ds(half_width, half_width)] = jnp.zeros((1, half_width), F32)
    vec_up[1:2, pl.ds(2 * half_width, half_width)] = jnp.concatenate(q_bias[8:], axis=-1)

    def first_norm(rows):
        normed, _ = norm_of(state[rows, :])
        act_one[rows, :] = (normed * vec[0] + vec[1]).astype(LOW)

    over_rows(length, first_norm)
    loads[0].wait()

    def project(t):
        here = tile_at(t)
        bias = vec_up[1:2, here]
        qkv[:, here] = (dot(act_one[...], v_qkv[:, here]) + bias).astype(LOW)

    over_tiles(3 * half_width // TILE, project)
    seg_row, seg_col = seg_row_col(segs)
    allowed = allowed_pairs(seg_col, seg_row)
    scale = 1.0 / math.sqrt(HEAD_DIM)
    for h in range(half_width // HEAD_DIM):
        q, k, v = (qkv[:, pl.ds(t * half_width + h * HEAD_DIM, HEAD_DIM)] for t in range(3))
        probs = head_probs(q, k, allowed, scale).astype(LOW)
        attn[:, pl.ds(h * HEAD_DIM, HEAD_DIM)] = dot(probs, v).astype(LOW)
    loads[1].wait()
    pair.fill(0, lambda t: dot(attn[...], v_out[:, tile_at(t)]))
    if moved:
        sequences.cross()
    pair.wait(0)

    def second_norm(rows):
        x = state[rows, :] + pair.total(0, rows) + vec[2]
        middle[rows, :] = x
        normed, _ = norm_of(x)
        act_two[rows, :] = (normed * vec[3] + vec[4]).astype(LOW)

    over_rows(length, second_norm)
    loads[2].wait()

    def expand(t):
        here = tile_at(t)
        value, rise = gelu_pair(dot(act_two[...], v_up[:, here]) + vec_up[0:1, here])
        hidden[:, here] = value.astype(LOW)
        slope[:, here] = rise

    over_tiles(slope.shape[1] // TILE, expand)
    if count:
        for s in streams:
            s.onward(2)
    loads[3].wait()
    pair.fill(1, lambda t: dot(hidden[...], v_down[:, tile_at(t)]))
    pair.wait(1)

    def close(rows):
        new_state[rows, :] = middle[rows, :] + pair.total(1, rows) + vec[5]

    over_rows(length, close)
    if count:
        for s in streams:
            s.finish(2)
        for s in streams:
            s.drain((2,))
    if moved:
        sequences.drain()


def weight_scratch(weights):
    w_up, w_down, w_qkv, w_out = weights
    return [pltpu.VMEM(w.shape, LOW) for w in (w_qkv, w_out, w_up, w_down)]


def pair_scratch(length, width):
    shape = (2, width // TILE, length, TILE)
    return [pltpu.VMEM(shape, F32), pltpu.VMEM(shape, F32)]


def forward_block(layer, state, segs, small, weights, begun, parts):
    count, moved = len(begun), len(parts)
    length, width = state.shape
    inner = weights[0].shape[1]
    shapes = [
        ((length, width), F32),
        ((length, width), LOW),
        ((length, 3 * width // 2), LOW),
        ((length, width // 2), LOW),
        ((length, width), F32),
        ((length, width), LOW),
        ((length, inner), F32),
        ((length, inner), LOW),
    ]
    shapes = [jax.ShapeDtypeStruct(*s) for s in shapes]
    shapes += [jax.ShapeDtypeStruct(b.shape, b.dtype) for b in begun]
    out = pl.pallas_call(
        functools.partial(forward_kernel, layer, count, moved),
        out_shape=shapes + sequence_shapes(parts),
        in_specs=[VMEM] * 3 + [ANY] * (4 + count + moved),
        out_specs=[VMEM] * 8 + [ANY] * (count + moved),
        input_output_aliases={7 + m: 8 + m for m in range(count)},
        scratch_shapes=weight_scratch(weights)
        + pair_scratch(length, width)
        + [
            pltpu.VMEM((6, 1, width), F32),
            pltpu.VMEM((2, inner), F32),
            DMA((4,)),
            DMA((2, width // TILE)),
            DMA((2, width // TILE)),
        ]
        + ([DMA((count, 12)), DMA((count, 12))] if count else [])
        + sequence_scratch(moved),
        compiler_params=pltpu.CompilerParams(
            collective_id=2 + layer, has_side_effects=True, vmem_limit_bytes=60 * 1024 * 1024
        ),
        name="forward_block",
    )(state, segs, small, *weights, *begun, *parts)
    return out[:8], out[8 : 8 + count], out[8 + count :]


def column_sum(target, row, value):
    target[row : row + 1, :] += jnp.sum(value, axis=0, keepdims=True)


def backward_kernel(layer, count, *refs):
    grad_state, state, middle, qkv, attn, slope, hidden, act_one, act_two, segs, small = refs[:11]
    w_up, w_down, w_qkv, w_out = refs[11:15]
    given, refs = refs[15 : 15 + count], refs[15 + count :]
    new_grad, totals = refs[0], refs[1:5]
    g_heads, g_out, small_grad = refs[5:8], refs[8], refs[9]
    sums, refs = refs[10 : 10 + count], refs[10 + count :]
    v_qkv, v_out, v_up, v_down, terms, box, vec, acc, acc_up, acc_qkv = refs[:10]
    grad_low, d_pre_low, mid_low, d_qkv, d_attn = refs[10:15]
    boxes, refs = refs[15:19], refs[19:]
    load, p_send, p_recv, o_send, o_recv = refs[:5]
    rings = refs[5:]
    core = lax.axis_index("core")
    length, width = state.shape
    half_width = width // 2
    inner = slope.shape[1]
    loads = [
        pltpu.make_async_copy(w, v, load.at[i])
        for i, (w, v) in enumerate(((w_down, v_down), (w_up, v_up), (w_out, v_out), (w_qkv, v_qkv)))
    ]
    for copy in loads:
        copy.start()
    pos = positions()
    greet(pos, False)
    streams, at = [], 0
    for m in range(count):
        take = 3 if m < SPLIT else 6
        sems = [rings[len(rings) - 3 + k].at[m] for k in range(3)]
        streams.append(scatter_of(pos, m, given[m], rings[at : at + take], (sums[m],), sems))
        at += take
    own = [
        Scatter(
            pos,
            SCATTERS[m],
            0,
            v_up if m < 2 else v_down,
            None,
            (boxes[m],),
            (totals[m],),
            o_send.at[m],
            o_recv.at[m],
            None,
            totals[m - 1].shape[-1] if m % 2 else 0,
        )
        for m in range(SPLIT)
    ]

    def carry(at):
        for s in streams:
            s.step(at)

    carry(0)
    pair = Pair(terms, box, p_send, p_recv)
    fill_vector(vec.at[0], small, G_ONE, layer)
    fill_vector(vec.at[1], small, G_TWO, layer)
    acc[...] = jnp.zeros_like(acc)
    tokens = ((0,), (0,))

    def down_rows(t):
        return (t // 2, pl.ds(lax.rem(t, 2) * 2, 2))

    def lower(rows):
        g = grad_state[rows, :]
        grad_low[rows, :] = g.astype(LOW)
        column_sum(acc, 0, g)

    over_rows(length, lower)
    loads[0].wait()

    def contract(t):
        here = tile_at(t)
        w = v_down[down_rows(t)].reshape(TILE, width)
        d_pre = dot(grad_low[...], w, ((1,), (1,))) * slope[:, here]
        d_pre_low[:, here] = d_pre.astype(LOW)
        acc_up[:, here] = jnp.sum(d_pre, axis=0, keepdims=True)

    over_tiles(inner // TILE, contract)
    carry(1)

    def down_grad(t):
        value = dot(hidden[:, tile_at(t)], grad_low[...], tokens)
        v_down[down_rows(t)] = value.reshape(2, RING, 32, width).astype(LOW)

    over_tiles(inner // TILE, down_grad)
    for s in own[2:]:
        s.begin(0)
    loads[1].wait()
    pair.fill(0, lambda t: dot(d_pre_low[...], v_up[t].reshape(TILE, inner), ((1,), (1,))))


    def up_grad(t):
        value = dot(act_two[:, tile_at(t)], d_pre_low[...], tokens)
        v_up[t] = value.reshape(RING, RING, 16, inner).astype(LOW)

    over_tiles(width // TILE, up_grad)
    for s in own[:2]:
        s.begin(0)
    pair.wait(0)

    def second_norm(rows):
        d_act = pair.total(0, rows)
        normed, factor = norm_of(middle[rows, :])
        column_sum(acc, 1, d_act * normed)
        column_sum(acc, 2, d_act)
        g = grad_state[rows, :] + norm_backward(d_act, normed, factor, vec[1])
        new_grad[rows, :] = g
        mid_low[rows, :] = g.astype(LOW)
        column_sum(acc, 3, g)

    over_rows(length, second_norm)
    carry(2)
    loads[2].wait()

    def attn_grad(t):
        here = tile_at(t)
        d_attn[:, here] = dot(mid_low[...], v_out[here, :], ((1,), (1,))).astype(LOW)

    over_tiles(half_width // TILE, attn_grad)

    def out_grad(t):
        value = dot(attn[:, tile_at(t)], mid_low[...], tokens)
        g_out[pl.ds(t * 2, 2)] = value.reshape(2, RING, RING, 8, width).astype(LOW)

    over_tiles(half_width // TILE, out_grad)
    seg_row, seg_col = seg_row_col(segs)
    allowed = allowed_pairs(seg_col, seg_row)
    scale = 1.0 / math.sqrt(HEAD_DIM)
    for h in range(half_width // HEAD_DIM):
        q, k, v = (qkv[:, pl.ds(t * half_width + h * HEAD_DIM, HEAD_DIM)] for t in range(3))
        here = pl.ds(h * HEAD_DIM, HEAD_DIM)
        d_head = d_attn[:, here]
        full = head_probs(q, k, allowed, scale)
        delta = jnp.sum(
            d_head.astype(F32) * attn[:, here].astype(F32), axis=-1, keepdims=True
        )
        d_scores = (full * (dot(d_head, v, ((1,), (1,))) - delta)).astype(LOW)
        ends = (
            dot(d_scores, k) * scale,
            dot(d_scores, q, ((0,), (0,))) * scale,
            dot(full.astype(LOW), d_head, ((0,), (0,))),
        )
        for t, end in enumerate(ends):
            place = pl.ds(t * half_width + h * HEAD_DIM, HEAD_DIM)
            d_qkv[:, place] = end.astype(LOW)
            acc_qkv[:, place] = jnp.sum(end, axis=0, keepdims=True)
        if h == 5:
            for s in own:
                s.onward(0)
    carry(3)
    loads[3].wait()
    pair.fill(1, lambda t: dot(d_qkv[...], v_qkv[tile_at(t), :], ((1,), (1,))))

    def head_grad(t):
        value = dot(act_one[:, tile_at(t)], d_qkv[...], tokens)
        for part in range(3):
            third = value[:, part * half_width : (part + 1) * half_width]
            g_heads[part][t] = third.reshape(RING, RING, 16, half_width).astype(LOW)

    over_tiles(width // TILE, head_grad)
    carry(4)
    pair.wait(1)

    def first_norm(rows):
        d_act = pair.total(1, rows)
        normed, factor = norm_of(state[rows, :])
        column_sum(acc, 4, d_act * normed)
        column_sum(acc, 5, d_act)
        new_grad[rows, :] += norm_backward(d_act, normed, factor, vec[0])

    over_rows(length, first_norm)
    small_grad[...] = jnp.zeros_like(small_grad)
    first = (core == 0).astype(F32)
    for s in range(8):
        here = pl.ds(s * 128, 128)
        target = small_grad.at[s // 2, pl.ds((s % 2) * 2, 2)]
        for vector, row in ((B_DOWN, 0), (G_TWO, 1), (S_TWO, 2), (B_OUT, 3), (G_ONE, 4), (S_ONE, 5)):
            target[vector // 4, vector % 4, 0:1, 0:128] = acc[row : row + 1, here] * first
        block = acc_up[:, pl.ds(s * TILE, TILE)]
        target[B_UP // 4, B_UP % 4, 0:1, :] = block * first
        target[B_UP // 4, B_UP % 4, 1:2, :] = block * (1.0 - first)
        at = (s // 4) * 2 * half_width + (s % 4) * 2 * HEAD_DIM
        heads = []
        for k in range(2):
            value = acc_qkv[:, pl.ds(at + k * HEAD_DIM, HEAD_DIM)]
            heads += [value * first, value * (1.0 - first)]
        target[B_QV // 4, B_QV % 4, 0:1, :] = jnp.concatenate(heads, axis=-1)
    carry(5)
    for s in own:
        s.finish(0)
    carry(6)
    for s in streams:
        s.drain()
    for s in own:
        s.drain((0,))


def backward_block(layer, grad_state, record, segs, small, weights, given):
    state = record[0]
    count = len(given)
    length, width = state.shape
    inner = record[4].shape[1]
    cube = (RING, RING, RING)
    w_up, w_down, w_qkv, w_out = weights
    halves = []
    for w, (share, of) in ((w_up, UP_PART), (w_down, DOWN_PART)):
        rows, cols = w.shape[3:]
        halves += [(rows, cols * share // of), (rows, cols - cols * share // of)]
    ends = [((length, width), F32)] + [((RING, RING) + h, LOW) for h in halves]
    ends += [(cube + (width // 64, width // 2), LOW)] * 3
    ends += [(cube + w_out.shape[3:], LOW), (cube + (8, 256), F32)]
    shapes = [jax.ShapeDtypeStruct(*e) for e in ends]
    shapes += [jax.ShapeDtypeStruct(g.shape[-2:], g.dtype) for g in given]
    bufs = []
    for m, g in enumerate(given):
        bufs += scatter_scratch(g.shape[-2:], g.dtype, 1 if m < SPLIT else 0, False)
    sems = [DMA((count, 18)), DMA((count, 18)), DMA((count, 5))] if count else []
    flat = [w.reshape(-1, w.shape[-1]) for w in (w_qkv, w_out)]
    out = pl.pallas_call(
        functools.partial(backward_kernel, layer, count),
        out_shape=shapes,
        in_specs=[VMEM] * 11 + [ANY] * 4 + [VMEM] * min(count, SPLIT) + [ANY] * max(count - SPLIT, 0),
        out_specs=[VMEM] * (10 + count),
        scratch_shapes=[pltpu.VMEM(w.shape, LOW) for w in flat + [w_up, w_down]]
        + pair_scratch(length, width)
        + [
            pltpu.VMEM((2, 1, width), F32),
            pltpu.VMEM((6, width), F32),
            pltpu.VMEM((1, inner), F32),
            pltpu.VMEM((1, 3 * width // 2), F32),
            pltpu.VMEM((length, width), LOW),
            pltpu.VMEM((length, inner), LOW),
            pltpu.VMEM((length, width), LOW),
            pltpu.VMEM((length, 3 * width // 2), LOW),
            pltpu.VMEM((length, width // 2), LOW),
        ]
        + [pltpu.VMEM((6, RING, RING, r, c // 2), LOW) for r, c in halves]
        + [
            DMA((4,)),
            DMA((2, width // TILE)),
            DMA((2, width // TILE)),
            DMA((SPLIT, 6)),
            DMA((SPLIT, 6)),
        ]
        + bufs
        + sems,
        compiler_params=pltpu.CompilerParams(
            collective_id=4 + layer, has_side_effects=True, vmem_limit_bytes=67043328
        ),
        name="backward_block",
    )(grad_state, *record, segs, small, w_up, w_down, *flat, *given)
    return out[0], list(out[1:10]), list(out[10:])


def finish_kernel(layers, *refs):
    ins, outs = refs[: 9 * layers], refs[9 * layers :]
    o_qkv, o_out, o_up, o_down = outs[:4]
    for l in range(layers):
        up_a, up_b, down_a, down_b, *qkv, out, small = ins[9 * l : 9 * l + 9]
        blocks = up_a.shape[-1] // TILE
        for s in range(8):
            for c in range(2):
                up, at = (up_a, s) if s < blocks else (up_b, s - blocks)
                o_up[l, :, pl.ds((2 * s + c) * TILE, TILE)] = up[c, 0, :, pl.ds(at * TILE, TILE)].astype(F32)
        for c in range(2):
            o_down[l, c, 0] = jnp.concatenate([down_a[c, 0], down_b[c, 0]], axis=-1).astype(F32)
            o_out[l, c, 0] = out[c, 0].astype(F32)
        for k in range(24):
            here = pl.ds((k % 8) * HEAD_DIM, HEAD_DIM)
            both = jnp.concatenate([qkv[k // 8][c, 0, :, here] for c in range(2)], axis=-1)
            o_qkv[l, :, pl.ds(k * 128, 128)] = both.astype(F32)

        @pl.when(pl.program_id(0) == 0)
        def _():
            for v in range(8):
                o = outs[4 + v]
                size = o.shape[1]
                for part in range((size + 255) // 256):
                    span = min(size, 256)
                    o[l : l + 1, pl.ds(part * 256, span)] = (
                        small[0, v, part : part + 1, 0:span] + small[1, v, part : part + 1, 0:span]
                    )


def finish(finals, sizes):
    layers = len(finals)
    in_specs, args = [], []
    for f in finals:
        for m, a in enumerate(f):
            r, c = a.shape[3:]
            args.append(a.reshape(2, 8, r, c))
            if m < 8:
                in_specs.append(pl.BlockSpec((2, 1, r, c), lambda p: (0, p, 0, 0)))
            else:
                in_specs.append(pl.BlockSpec((2, 8, r, c), lambda p: (0, 0, 0, 0)))
    up, up_b, down, down_b, qkv, _, _, out = (a.shape[2:] for a in args[:8])
    up, down = (up[0], up[1] + up_b[1]), (down[0], down[1] + down_b[1])
    shapes, specs = [], []
    for rows, cols in ((qkv[0], 6 * qkv[1]), (0, 0), (up[0], 2 * up[1])):
        if rows:
            shapes.append(jax.ShapeDtypeStruct((layers, 8 * rows, cols), F32))
            specs.append(pl.BlockSpec((layers, rows, cols), lambda p: (0, p, 0)))
        else:
            shapes.append(jax.ShapeDtypeStruct((layers, 2, 8) + out, F32))
            specs.append(pl.BlockSpec((layers, 2, 1) + out, lambda p: (0, 0, p, 0, 0)))
    shapes.append(jax.ShapeDtypeStruct((layers, 2, 8) + down, F32))
    specs.append(pl.BlockSpec((layers, 2, 1) + down, lambda p: (0, 0, p, 0, 0)))
    for size in sizes:
        shapes.append(jax.ShapeDtypeStruct((layers, size), F32))
        specs.append(pl.BlockSpec((layers, size), lambda p: (0, 0)))
    res = pl.pallas_call(
        functools.partial(finish_kernel, layers),
        out_shape=shapes,
        grid=(8,),
        in_specs=in_specs,
        out_specs=specs,
        name="finish",
    )(*args)
    o_out = res[1].reshape(layers, 16 * out[0], out[1])
    o_down = res[3].reshape(layers, 16 * down[0], down[1])
    return (res[0], o_out, res[2], o_down) + tuple(res[4:])


def prepare_kernel(where, up, down, qkv, out, segment_ids, *refs):
    vectors, refs = refs[:8], refs[8:]
    layers = up.shape[0]
    sub, core = where[0], where[1]
    for l in range(layers):
        o_up, o_down, o_qkv, o_out = refs[4 * l : 4 * l + 4]
        o_down[...] = down[l]
        o_out[...] = out[l]
        for s in range(8):
            at = pl.multiple_of((2 * s + core) * TILE, TILE)
            o_up[:, pl.ds(s * TILE, TILE)] = up[l, :, pl.ds(at, TILE)]
        for k in range(12):
            two = []
            for j in range(2):
                pair = qkv[l, :, pl.ds((2 * k + j) * 128, 128)]
                two.append(jnp.where(core == 0, pair[:, :HEAD_DIM], pair[:, HEAD_DIM:]))
            o_qkv[:, pl.ds(k * 128, 128)] = jnp.concatenate(two, axis=-1)
    small, segs = refs[4 * layers :]
    small[...] = jnp.zeros_like(small)
    for v, vector in enumerate(vectors):

        @pl.when(sub == v)
        def _():
            size = vector.shape[1]
            for part in range((size + 255) // 256):
                span = min(size, 256)
                block = vector[:, pl.ds(part * 256, span)].astype(F32)
                for l in range(layers):
                    small[2 * l + part : 2 * l + part + 1, 0:span] = block[l : l + 1]

    segs[...] = jnp.zeros_like(segs)
    for b in range(segs.shape[0]):
        segs[b, 0:1, 0 : segment_ids.shape[1]] = segment_ids[b : b + 1, :].astype(F32)


def prepare(weights, segment_ids, vectors):
    up, down, qkv, out = weights
    layers, rows = up.shape[:2]
    piece, down_rows, out_rows = rows // 8, down.shape[1] // 16, rows // 16
    where = jnp.stack(
        [lax.axis_index("xl") * 4 + lax.axis_index("y"), lax.axis_index("core")]
    ).astype(jnp.int32)
    per_layer = [
        (piece, up.shape[2] // 2),
        (down_rows, down.shape[2]),
        (piece, qkv.shape[2] // 2),
        (out_rows, out.shape[2]),
    ]
    shapes = [jax.ShapeDtypeStruct(e, LOW) for e in per_layer] * layers
    shapes += [jax.ShapeDtypeStruct((8, 256), F32), jax.ShapeDtypeStruct((2, 8, 128), F32)]
    by_row = lambda i, where: (0, where[0], 0)
    by_half = lambda i, where: (0, 8 * where[1] + where[0], 0)
    whole = lambda a: pl.BlockSpec(a.shape, lambda i, where: (0,) * len(a.shape))
    made = pl.pallas_call(
        prepare_kernel,
        out_shape=shapes,
        grid_spec=pltpu.PrefetchScalarGridSpec(
            num_scalar_prefetch=1,
            grid=(1,),
            in_specs=[
                pl.BlockSpec((layers, piece, up.shape[2]), by_row),
                pl.BlockSpec((layers, down_rows, down.shape[2]), by_half),
                pl.BlockSpec((layers, piece, qkv.shape[2]), by_row),
                pl.BlockSpec((layers, out_rows, out.shape[2]), by_half),
                whole(segment_ids),
            ]
            + [whole(v) for v in vectors],
            out_specs=[whole(e) for e in shapes],
        ),
        name="prepare",
    )(where, up, down, qkv, out, segment_ids, *vectors)
    owns = [made[4 * l : 4 * l + 4] for l in range(layers)]
    return owns, made[4 * layers], made[4 * layers + 1]


def per_device(
    inputs,
    segment_ids,
    weight_qkv,
    weight_out,
    weight_up,
    weight_down,
    bias_qv,
    bias_out,
    bias_up,
    bias_down,
    gain_one,
    shift_one,
    gain_two,
    shift_two,
    cotangent,
):
    layers, width = weight_qkv.shape[0], inputs.shape[-1]
    length = inputs.shape[1] * RING
    vectors = (bias_qv, bias_out, bias_up, bias_down, gain_one, shift_one, gain_two, shift_two)
    sizes = [v.shape[1] for v in vectors]
    owns, packed, segs = prepare((weight_up, weight_down, weight_qkv, weight_out), segment_ids, vectors)
    fulls, begun, wholes = gather_all(list(owns[0]) + [packed], list(owns[1]), [inputs, segs])
    state, segs = wholes[0].reshape(length, width), wholes[1]
    small = fulls[4].reshape(8, 8, 8, 256)
    records = []
    weights = [fulls[:4]]
    for l in range(layers):
        carried, parts = (begun, []) if l == 0 else ([], [cotangent])
        flat = [w.reshape(-1, w.shape[-1]) for w in weights[l]]
        made, fulls, wholes = forward_block(l, state, segs, small, flat, list(carried), parts)
        weights.append(fulls)
        new_state, act_one, qkv, attn, middle, act_two, slope, hidden = made
        records.append((state, middle, qkv, attn, slope, hidden, act_one, act_two))
        state = new_state
    grad_state = wholes[0].reshape(length, width)
    pieces = []
    for l in reversed(range(layers)):
        grad_state, pieces, sums = backward_block(
            l, grad_state, records[l], segs, small, weights[l], pieces
        )
    quarter = (RING, length // RING, width)
    finals, others, parts = scatter_all(
        pieces, sums, [state.reshape(quarter), grad_state.reshape(quarter)]
    )
    return (parts[0], parts[1]) + finish([finals, others], sizes)


def solution(mesh):
    torus = Mesh(mesh.devices.reshape(4, 2, 4, 2, 2), AXES)
    tokens = P(("xh", "y", "xl", "core"), "z", None)
    weight = P(None, ("z", "xh"), None)
    vector = P(None, ("z", "xh"))
    return jax.shard_map(
        per_device,
        mesh=torus,
        in_specs=(tokens, P(("xh", "y", "xl", "core"), "z")) + (weight,) * 4 + (vector,) * 8 + (tokens,),
        out_specs=(tokens, tokens) + (weight,) * 4 + (vector,) * 8,
        check_vma=False,
    )
```

```python
import functools
import math

import jax
import jax.numpy as jnp
from jax import lax
from jax.experimental import pallas as pl
from jax.experimental.pallas import tpu as pltpu
from jax.sharding import Mesh
from jax.sharding import PartitionSpec as P

AXES = ("z", "xh", "y", "xl", "core")
RING = 4
ANY = pl.BlockSpec(memory_space=pl.ANY)
VMEM = pl.BlockSpec(memory_space=pltpu.VMEM)
DMA = pltpu.SemaphoreType.DMA
SCATTERS = ("xyz", "yzx", "zxy", "yxz", "xyz", "zyx", "yzx", "yxz", "yzx")
SPLIT = 4
UP_PART, DOWN_PART = (5, 8), (3, 4)
ORDERS = ("xyz", "zxy", "yzx", "yzx")


def positions():
    return {
        "z": lax.axis_index("z"),
        "x": lax.axis_index("xh") * 2 + lax.axis_index("xl"),
        "y": lax.axis_index("y"),
    }


def neighbour(pos, axis, step):
    at = lax.rem(pos[axis] + step + RING, RING)
    if axis == "x":
        return {"xh": at // 2, "xl": lax.rem(at, 2)}
    return {axis: at}


def remote(src, dst, send, recv, target):
    return pltpu.make_async_remote_copy(
        src_ref=src,
        dst_ref=dst,
        send_sem=send,
        recv_sem=recv,
        device_id=target,
        device_id_type=pl.DeviceIdType.MESH,
    )


def greet(pos, with_column):
    barrier = pltpu.get_barrier_semaphore()
    targets = [neighbour(pos, axis, step) for axis in "xyz" for step in (1, -1)]
    if with_column:
        targets.append(neighbour(pos, "z", 2))
    targets.append({"core": 1 - lax.axis_index("core")})
    for target in targets:
        pl.semaphore_signal(
            barrier, inc=1, device_id=target, device_id_type=pl.DeviceIdType.MESH
        )
    pl.semaphore_wait(barrier, len(targets))


def half(ref, which, rows, cols):
    lead = (slice(None),) * (len(ref.shape) - 2)
    if rows % 16 == 0:
        return ref.at[lead + (pl.ds(which * (rows // 2), rows // 2), slice(None))]
    return ref.at[lead + (slice(None), pl.ds(which * (cols // 2), cols // 2))]


class Gather:
    def __init__(self, pos, order, own, full, send, recv):
        self.pos, self.order, self.own, self.full = pos, order, own, full
        self.send, self.recv = send, recv
        self.rows, self.cols = full.shape[-2:]

    def view(self, stage, shift):
        index = {}
        for place, axis in enumerate(self.order):
            if place < stage:
                index[axis] = slice(None)
            elif place == stage:
                index[axis] = lax.rem(self.pos[axis] + shift + RING, RING)
            else:
                index[axis] = self.pos[axis]
        return self.full.at[index["z"], index["x"], index["y"]]

    def copy(self, stage, kind):
        axis = self.order[stage]
        sems = (self.send.at[stage * 4 + kind], self.recv.at[stage * 4 + kind])
        target = neighbour(self.pos, axis, 1 if kind % 2 == 0 else -1)
        if kind < 2:
            src = self.own if stage == 0 else self.view(stage, 0)
            return remote(src, self.view(stage, 0), *sems, target)
        piece = half(self.view(stage, -1 if kind == 2 else 1), kind - 2, self.rows, self.cols)
        return remote(piece, piece, *sems, target)

    def arrive(self, stage, kind):
        sems = (self.send.at[stage * 4 + kind], self.recv.at[stage * 4 + kind])
        axis = self.order[stage]
        if kind < 2:
            piece = self.view(stage, -1 if kind == 0 else 1)
        else:
            piece = half(self.view(stage, 2), kind - 2, self.rows, self.cols)
        remote(piece, piece, *sems, neighbour(self.pos, axis, 1)).wait_recv()

    def begin(self, stage):
        for kind in (0, 1):
            self.copy(stage, kind).start()

    def onward(self, stage):
        for kind in (0, 1):
            self.arrive(stage, kind)
            self.copy(stage, kind + 2).start()

    def finish(self, stage):
        for kind in (2, 3):
            self.arrive(stage, kind)

    def drain(self, stages):
        for stage in stages:
            for kind in range(4):
                self.copy(stage, kind).wait_send()


class Sequences:
    def __init__(self, pos, parts, wholes, sems):
        self.pos, self.parts, self.wholes = pos, parts, wholes
        self.send, self.recv, self.core_send, self.core_recv, self.local = sems
        self.core = lax.axis_index("core")
        self.receiver = pos["z"] // 2 == self.core

    def outward(self, a, b, home):
        return remote(
            self.parts[a].at[b],
            self.wholes[a].at[self.pos["z"]],
            self.send.at[a, b],
            self.recv.at[a, self.pos["z"]],
            {"z": home},
        )

    def crossing(self, a, q):
        piece = self.wholes[a].at[q]
        return remote(
            piece, piece, self.core_send.at[a, q], self.core_recv.at[a, q], {"core": 1 - self.core}
        )

    def staying(self, a, b):
        return pltpu.make_async_copy(
            self.parts[a].at[b], self.wholes[a].at[self.pos["z"]], self.local.at[a]
        )

    def begin(self):
        for a in range(len(self.parts)):
            for b in range(2):
                home = 2 * self.core + b

                @pl.when(home == self.pos["z"])
                def _():
                    self.staying(a, b).start()

                @pl.when(home != self.pos["z"])
                def _():
                    self.outward(a, b, home).start()

    def cross(self):
        @pl.when(self.receiver)
        def _():
            for a in range(len(self.parts)):
                for q in range(RING):

                    @pl.when(q == self.pos["z"])
                    def _():
                        self.staying(a, 0).wait()

                    @pl.when(q != self.pos["z"])
                    def _():
                        piece = self.wholes[a].at[q]
                        remote(
                            piece,
                            piece,
                            self.send.at[a, 0],
                            self.recv.at[a, q],
                            {"z": lax.rem(self.pos["z"] + 1, RING)},
                        ).wait_recv()

                    self.crossing(a, q).start()

    def drain(self):
        for a in range(len(self.parts)):
            for b in range(2):
                home = 2 * self.core + b

                @pl.when(home != self.pos["z"])
                def _():
                    self.outward(a, b, lax.rem(self.pos["z"] + 1, RING)).wait_send()

            for q in range(RING):

                @pl.when(self.receiver)
                def _():
                    self.crossing(a, q).wait_send()

                @pl.when(jnp.logical_not(self.receiver))
                def _():
                    self.crossing(a, q).wait_recv()


def sequence_scratch(moved):
    sems = [DMA((moved, 2)), DMA((moved, RING)), DMA((moved, RING)), DMA((moved, RING)), DMA((moved,))]
    return sems if moved else []


def sequence_shapes(parts):
    return [jax.ShapeDtypeStruct((RING,) + p.shape[1:], p.dtype) for p in parts]


def gather_kernel(count, whole, moved, *refs):
    owns, parts = refs[:count], refs[count : count + moved]
    refs = refs[count + moved :]
    fulls, wholes = refs[:count], refs[count : count + moved]
    send, recv, local = refs[count + moved : count + moved + 3]
    pos = positions()
    greet(pos, True)
    sequences = Sequences(pos, parts, wholes, refs[count + moved + 3 :])
    streams, keeps = [], []
    for m in range(count):
        keeps.append(
            pltpu.make_async_copy(
                owns[m], fulls[m].at[pos["z"], pos["x"], pos["y"]], local.at[m]
            )
        )
        streams.append(
            Gather(pos, ORDERS[m % whole % 4], owns[m], fulls[m], send.at[m], recv.at[m])
        )
    for keep in keeps:
        keep.start()
    for s in streams:
        s.begin(0)
    sequences.begin()
    for stage in range(3):
        running = streams if stage < 2 else streams[:whole]
        for s in running:
            s.onward(stage)
        if stage == 0:
            for keep in keeps:
                keep.wait()
        for m, s in enumerate(running):
            s.finish(stage)
            if stage == 0 or (stage == 1 and m < whole):
                s.begin(stage + 1)
        if stage == 1:
            sequences.cross()
    for m, s in enumerate(streams):
        s.drain(range(3 if m < whole else 2))
    sequences.drain()


def gather_all(owns, begun, parts):
    count, moved = len(owns) + len(begun), len(parts)
    shapes = [
        jax.ShapeDtypeStruct((RING, RING, RING) + o.shape, o.dtype) for o in owns + begun
    ]
    out = pl.pallas_call(
        functools.partial(gather_kernel, count, len(owns), moved),
        out_shape=shapes + sequence_shapes(parts),
        in_specs=[ANY] * (count + moved),
        out_specs=[ANY] * (count + moved),
        scratch_shapes=[DMA((count, 12)), DMA((count, 12)), DMA((count,))]
        + sequence_scratch(moved),
        compiler_params=pltpu.CompilerParams(collective_id=0, has_side_effects=True),
        name="gather_all",
    )(*owns, *begun, *parts)
    return out[: len(owns)], out[len(owns) : count], out[count:]


def scatter_scratch(end, kind, start, last):
    r, c = end
    scratch = [] if start else [pltpu.VMEM((4, RING, RING, r, c // 2), kind)]
    for stage in range(start, 3):
        scratch.append(pltpu.VMEM((6,) + (RING,) * (2 - stage) + (r, c // 2), kind))
    for stage in range(start, 3 if last else 2):
        scratch.append(pltpu.VMEM((RING,) * (2 - stage) + (r, c), kind))
    return scratch


def scatter_of(pos, m, source, bufs, sums, sems):
    start = 1 if m < SPLIT else 0
    stages = 3 - start
    own = None if start else bufs[0]
    rest = list(bufs[1 - start :])
    boxes, more = [None] * start + rest[:stages], rest[stages:]
    sums = ([source] if start else []) + more + list(sums)
    return Scatter(pos, SCATTERS[m], start, None if start else source, own, boxes, sums, *sems)


class Scatter:
    def __init__(self, pos, order, start, grad, own, boxes, sums, send, recv, local, base=0):
        self.pos, self.order, self.start, self.grad = pos, order, start, grad
        self.own, self.boxes, self.sums = own, boxes, sums
        self.send, self.recv, self.local = send, recv, local
        self.part, self.base = sums[0].shape[-1] // 2, base

    def piece(self, stage, shift, which):
        axis = self.order[stage]
        left = [a for a in "zxy" if a in self.order[stage:]]
        source = self.grad if stage == 0 else self.sums[stage - 1]
        at = lax.rem(self.pos[axis] + shift + RING, RING)
        index = tuple(at if a == axis else slice(None) for a in left) + (slice(None),)
        base = self.base if stage == 0 else 0
        return source.at[index + (pl.ds(base + which * self.part, self.part),)]

    def box(self, stage, kind):
        return self.boxes[stage].at[kind]

    def copy(self, stage, kind):
        src, step = {
            0: (lambda: self.piece(stage, 2, 0), 1),
            1: (lambda: self.piece(stage, 1, 1), 1),
            2: (lambda: self.piece(stage, -2, 1), -1),
            3: (lambda: self.piece(stage, -1, 0), -1),
            4: (lambda: self.box(stage, 0), 1),
            5: (lambda: self.box(stage, 2), -1),
        }[kind]
        return remote(
            src(),
            self.box(stage, kind),
            self.send.at[stage * 6 + kind],
            self.recv.at[stage * 6 + kind],
            neighbour(self.pos, self.order[stage], step),
        )

    def loads(self):
        for slot, (shift, which) in enumerate(((1, 0), (-1, 1), (0, 0), (0, 1))):
            yield pltpu.make_async_copy(
                self.piece(0, shift, which), self.own.at[slot], self.local.at[slot]
            )

    def begin(self, stage):
        for kind in range(4):
            self.copy(stage, kind).start()
        if stage == 0 and self.own is not None:
            for load in self.loads():
                load.start()

    def term(self, stage, slot):
        if stage == 0 and self.own is not None:
            return self.own.at[slot]
        shift, which = ((1, 0), (-1, 1), (0, 0), (0, 1))[slot]
        return self.piece(stage, shift, which)

    def add(self, stage, target, terms):
        lead = 2 - stage

        def one(index):
            total = terms[0][index].astype(jnp.float32)
            for t in terms[1:]:
                total = total + t[index].astype(jnp.float32)
            target[index] = total.astype(target.dtype)

        if lead < 2:
            one((slice(None),) * (lead + 2))
            return

        def body(i, carry):
            one((i, slice(None), slice(None), slice(None)))
            return carry

        lax.fori_loop(0, RING, body, 0)

    def onward(self, stage):
        if stage == 0 and self.own is not None:
            for load in self.loads():
                load.wait()
        for slot, kind in ((0, 0), (1, 2)):
            self.copy(stage, kind).wait_recv()
            box = self.box(stage, kind)
            self.add(stage, box, (box, self.term(stage, slot)))
            self.copy(stage, 4 + slot).start()

    def finish(self, stage):
        for kind in (1, 3, 4, 5):
            self.copy(stage, kind).wait_recv()
        lead = (slice(None),) * (3 - stage)
        for which, kinds in ((0, (3, 4)), (1, (1, 5))):
            target = self.sums[stage].at[lead + (pl.ds(which * self.part, self.part),)]
            self.add(
                stage,
                target,
                (self.term(stage, 2 + which),) + tuple(self.box(stage, k) for k in kinds),
            )

    def steps(self):
        return 2 * (3 - self.start) + 1

    def step(self, at):
        if at == 0:
            self.begin(self.start)
        elif at < self.steps():
            stage = self.start + (at - 1) // 2
            if at % 2:
                self.onward(stage)
            else:
                self.finish(stage)
                if stage < 2:
                    self.begin(stage + 1)

    def drain(self, stages=None):
        for stage in range(self.start, 3) if stages is None else stages:
            for kind in range(6):
                self.copy(stage, kind).wait_send()


class Publish:
    def __init__(self, pos, across, source, final, sends, recvs, local):
        self.pos, self.across, self.source, self.final = pos, across, source, final
        self.sends_f, self.recvs_f, self.local = sends, recvs, local
        self.core, self.xl = lax.axis_index("core"), lax.axis_index("xl")
        self.part = source.shape[-1] // 2

    def across_first(self):
        return self.across

    def block(self, shift):
        yi = lax.rem(self.pos["y"] + shift + RING, RING)
        xs = slice(None) if self.across_first() else self.xl
        return self.final.at[self.core, xs, yi]

    def spread(self, kind, own=False):
        sems = (self.sends_f.at[kind], self.recvs_f.at[kind])
        if kind == 5:
            whole = self.final.at[self.core]
            return remote(whole, whole, *sems, {"core": 1 - self.core})
        if kind == 4:
            if self.across_first():
                dst = self.final.at[self.core, self.xl, self.pos["y"]]
                src = self.source
            else:
                src = dst = self.final.at[self.core, self.xl]
            return remote(src, dst, *sems, {"xl": 1 - self.xl})
        target = neighbour(self.pos, "y", 1 if kind % 2 == 0 else -1)
        if kind < 2:
            dst = self.block(0)
            src = dst if self.across_first() else self.source
            return remote(src, dst, *sems, target)
        ref = self.block(-1 if kind == 2 else 1)
        lead = (slice(None),) * (len(ref.shape) - 1)
        ref = ref.at[lead + (pl.ds((kind - 2) * self.part, self.part),)]
        return remote(ref, ref, *sems, target)

    def spread_arrives(self, kind):
        sems = (self.sends_f.at[kind], self.recvs_f.at[kind])
        if kind == 5:
            ref = self.final.at[1 - self.core]
        elif kind == 4:
            ref = self.final.at[self.core, 1 - self.xl]
            if self.across_first():
                ref = ref.at[self.pos["y"]]
        elif kind < 2:
            ref = self.block(-1 if kind == 0 else 1)
        else:
            ref = self.block(2)
            lead = (slice(None),) * (len(ref.shape) - 1)
            ref = ref.at[lead + (pl.ds((kind - 2) * self.part, self.part),)]
        remote(ref, ref, *sems, {"core": 1 - self.core}).wait_recv()

    def keep(self):
        return pltpu.make_async_copy(
            self.source,
            self.final.at[self.core, self.xl, self.pos["y"]],
            self.local,
        )

    def publish(self, step):
        if step == 0:
            self.keep().start()
            for kind in (4,) if self.across_first() else (0, 1):
                self.spread(kind).start()
        elif self.across_first():
            if step == 1:
                self.keep().wait()
                self.spread_arrives(4)
                for kind in (0, 1):
                    self.spread(kind).start()
            elif step == 2:
                for kind in (0, 1):
                    self.spread_arrives(kind)
                    self.spread(kind + 2).start()
            elif step == 3:
                for kind in (2, 3):
                    self.spread_arrives(kind)
        else:
            if step == 1:
                self.keep().wait()
                for kind in (0, 1):
                    self.spread_arrives(kind)
                    self.spread(kind + 2).start()
            elif step == 2:
                for kind in (2, 3):
                    self.spread_arrives(kind)
                self.spread(4).start()
            elif step == 3:
                self.spread_arrives(4)
        if step == 3:
            self.spread(5).start()
        if step == 4:
            self.spread_arrives(5)

    def drain(self):
        for kind in range(6):
            self.spread(kind).wait_send()


MATRICES = 9


def scatter_kernel(moved, *refs):
    grads, given = refs[:MATRICES], refs[MATRICES : 2 * MATRICES]
    wholes, refs = refs[2 * MATRICES : 2 * MATRICES + moved], refs[2 * MATRICES + moved :]
    finals, parts = refs[: 2 * MATRICES], refs[2 * MATRICES : 2 * MATRICES + moved]
    refs = refs[2 * MATRICES + moved :]
    send, recv, local, sends_f, recvs_f, keeps, send_t, recv_t, local_t = refs[-9:]
    pos = positions()
    core = lax.axis_index("core")
    greet(pos, True)
    streams, at = [], 0
    for m in range(MATRICES):
        take = 4 if m < SPLIT else 7
        sems = (send.at[m], recv.at[m], local.at[m])
        streams.append(scatter_of(pos, m, grads[m], refs[at : at + take], (), sems))
        at += take
    news = [
        Publish(
            pos, m % MATRICES in (0, 1, 4, 5, 6), source, finals[m], sends_f.at[m], recvs_f.at[m], keeps.at[m]
        )
        for m, source in enumerate([s.sums[2] for s in streams] + list(given))
    ]
    sender = pos["z"] // 2 == core
    slot = lax.rem(pos["z"], 2)

    def homeward(a, q):
        return remote(
            wholes[a].at[q], parts[a].at[slot], send_t.at[a, q], recv_t.at[a, slot], {"z": q}
        )

    def staying(a):
        return pltpu.make_async_copy(wholes[a].at[pos["z"]], parts[a].at[slot], local_t.at[a])

    for a in range(moved):
        for q in range(RING):

            @pl.when(sender & (pos["z"] == q))
            def _():
                staying(a).start()

            @pl.when(sender & (pos["z"] != q))
            def _():
                homeward(a, q).start()

    for at in range(11):
        for s, n in zip(streams, news):
            s.step(at)
            if 0 <= at - s.steps() + 1 < 5:
                n.publish(at - s.steps() + 1)
        if at % 2 == 0 and at < 10:
            for n in news[MATRICES:]:
                n.publish(at // 2)
    for s in streams:
        s.drain()
    for n in news:
        n.drain()
    for a in range(moved):
        for q in range(RING):

            @pl.when(sender & (pos["z"] == q))
            def _():
                staying(a).wait()

            @pl.when(sender & (pos["z"] != q))
            def _():
                homeward(a, q).wait_send()

        for b in range(2):

            @pl.when(2 * core + b != pos["z"])
            def _():
                remote(
                    parts[a].at[b],
                    parts[a].at[b],
                    send_t.at[a, 0],
                    recv_t.at[a, b],
                    {"z": lax.rem(pos["z"] + 1, RING)},
                ).wait_recv()


def scatter_all(grads, given, wholes):
    moved = len(wholes)
    ends = [g.shape[-2:] for g in grads] * 2
    kinds = [g.dtype for g in grads] * 2
    shapes = [jax.ShapeDtypeStruct((2, 2, RING) + e, k) for e, k in zip(ends, kinds)]
    shapes += [jax.ShapeDtypeStruct((2,) + w.shape[1:], w.dtype) for w in wholes]
    bufs = []
    for m in range(MATRICES):
        bufs += scatter_scratch(ends[m], kinds[m], 1 if m < SPLIT else 0, True)
    out = pl.pallas_call(
        functools.partial(scatter_kernel, moved),
        out_shape=shapes,
        in_specs=[VMEM] * SPLIT + [ANY] * (2 * MATRICES - SPLIT + moved),
        out_specs=[ANY] * (2 * MATRICES + moved),
        scratch_shapes=bufs
        + [
            DMA((MATRICES, 18)),
            DMA((MATRICES, 18)),
            DMA((MATRICES, 5)),
            DMA((2 * MATRICES, 6)),
            DMA((2 * MATRICES, 6)),
            DMA((2 * MATRICES,)),
            DMA((moved, RING)),
            DMA((moved, 2)),
            DMA((moved,)),
        ],
        compiler_params=pltpu.CompilerParams(
            collective_id=1, has_side_effects=True, vmem_limit_bytes=62 * 1024 * 1024
        ),
        name="scatter_all",
    )(*grads, *given, *wholes)
    return out[:MATRICES], out[MATRICES : 2 * MATRICES], out[2 * MATRICES :]


NORM_EPS = 1e-05
GELU_COEF = 0.7978845608028654
CUBIC_COEF = 0.044715
HEAD_DIM = 64
LOW = jnp.bfloat16
F32 = jnp.float32
TILE = 256
ROWS = 32
B_QV, B_OUT, B_UP, B_DOWN, G_ONE, S_ONE, G_TWO, S_TWO = range(8)


def dot(left, right, dims=((1,), (0,))):
    return lax.dot_general(left, right, (dims, ((), ())), preferred_element_type=F32)


def tile_at(t, size=TILE):
    return pl.ds(pl.multiple_of(t * size, size), size)


def over_rows(count, body):
    def step(i, carry):
        body(pl.ds(pl.multiple_of(i * ROWS, ROWS), ROWS))
        return carry

    lax.fori_loop(0, count // ROWS, step, 0)


def over_tiles(count, body):
    def step(t, carry):
        body(t)
        return carry

    lax.fori_loop(0, count, step, 0)


def head_probs(q, k, allowed, scale):
    scores = jnp.where(allowed, dot(q, k, ((1,), (1,))) * scale, -jnp.inf)
    top = jnp.max(scores, axis=-1, keepdims=True)
    lse = top + jnp.log(jnp.sum(jnp.exp(scores - top), axis=-1, keepdims=True))
    return jnp.exp(scores - lse)


def allowed_pairs(seg_col, seg_row):
    length = seg_col.shape[0]
    row = lax.broadcasted_iota(jnp.int32, (length, length), 0)
    col = lax.broadcasted_iota(jnp.int32, (length, length), 1)
    return (row >= col) & (seg_col == seg_row)


def norm_of(x):
    center = x - jnp.mean(x, axis=-1, keepdims=True)
    factor = lax.rsqrt(jnp.mean(center * center, axis=-1, keepdims=True) + NORM_EPS)
    return center * factor, factor


def norm_backward(d_act, normed, factor, gain):
    d_norm = d_act * gain
    return factor * (
        d_norm
        - jnp.mean(d_norm, axis=-1, keepdims=True)
        - normed * jnp.mean(d_norm * normed, axis=-1, keepdims=True)
    )


def gelu_pair(pre_act):
    cubic = pre_act * pre_act * pre_act
    tangent = jnp.tanh(GELU_COEF * (pre_act + CUBIC_COEF * cubic))
    gelu_value = 0.5 * pre_act * (1.0 + tangent)
    gelu_slope = 0.5 * (1.0 + tangent) + 0.5 * pre_act * (1.0 - tangent * tangent) * GELU_COEF * (
        1.0 + 3.0 * CUBIC_COEF * pre_act * pre_act
    )
    return gelu_value, gelu_slope


def vector_row(small, shard, vector, layer, part, size):
    return small[shard, vector, pl.ds(2 * layer + part, 1), pl.ds(0, size)]


def fill_vector(target, small, vector, layer):
    for s in range(8):
        target[:, pl.ds(s * 128, 128)] = vector_row(small, s, vector, layer, 0, 128)


class Pair:
    def __init__(self, terms, box, send, recv):
        self.terms, self.box, self.send, self.recv = terms, box, send, recv
        self.other = {"core": 1 - lax.axis_index("core")}

    def copy(self, which, t):
        return remote(
            self.terms.at[which, t],
            self.box.at[which, t],
            self.send.at[which, t],
            self.recv.at[which, t],
            self.other,
        )

    def fill(self, which, make):
        count = self.terms.shape[1]

        def body(t):
            self.terms[which, t] = make(t)

            @pl.when(t > 0)
            def _():
                self.copy(which, t - 1).start()

        over_tiles(count, body)
        self.copy(which, count - 1).start()

    def wait(self, which):
        for t in range(self.terms.shape[1]):
            self.copy(which, t).wait()

    def total(self, which, rows):
        return jnp.concatenate(
            [
                self.terms[which, t, rows, :] + self.box[which, t, rows, :]
                for t in range(self.terms.shape[1])
            ],
            axis=-1,
        )


def greet_pair():
    barrier = pltpu.get_barrier_semaphore()
    pl.semaphore_signal(
        barrier,
        inc=1,
        device_id={"core": 1 - lax.axis_index("core")},
        device_id_type=pl.DeviceIdType.MESH,
    )
    pl.semaphore_wait(barrier, 1)


def nothing(*_):
    pass


def seg_row_col(segs):
    row = jnp.concatenate([segs[q, 0:1, 0:80] for q in range(RING)], axis=-1)
    length = row.shape[1]
    at = lax.broadcasted_iota(jnp.int32, (length, length), 0)
    to = lax.broadcasted_iota(jnp.int32, (length, length), 1)
    return row, jnp.sum(jnp.where(at == to, row, 0.0), axis=-1, keepdims=True)


def forward_kernel(layer, count, moved, *refs):
    state, segs, small, w_up, w_down, w_qkv, w_out = refs[:7]
    parts, refs = refs[7 + count : 7 + count + moved], refs[7 + count + moved :]
    new_state, act_one, qkv, attn, middle, act_two, slope, hidden = refs[:8]
    fulls, wholes = refs[8 : 8 + count], refs[8 + count : 8 + count + moved]
    refs = refs[8 + count + moved :]
    v_qkv, v_out, v_up, v_down, terms, box, vec, vec_up = refs[:8]
    load, p_send, p_recv = refs[8:11]
    rings = refs[11:]
    core = lax.axis_index("core")
    length, width = state.shape
    half_width = width // 2
    loads = [
        pltpu.make_async_copy(w, v, load.at[i])
        for i, (w, v) in enumerate(((w_qkv, v_qkv), (w_out, v_out), (w_up, v_up), (w_down, v_down)))
    ]
    for copy in loads:
        copy.start()
    pos = positions()
    streams = sequences = None
    if count:
        greet(pos, False)
        streams = [
            Gather(pos, ORDERS[m], None, fulls[m], rings[0].at[m], rings[1].at[m])
            for m in range(count)
        ]
        for s in streams:
            s.begin(2)
    elif moved:
        greet(pos, True)
        sequences = Sequences(pos, parts, wholes, rings)
        sequences.begin()
    else:
        greet_pair()
    pair = Pair(terms, box, p_send, p_recv)
    for i, vector in enumerate((G_ONE, S_ONE, B_OUT, G_TWO, S_TWO, B_DOWN)):
        fill_vector(vec.at[i], small, vector, layer)
    for s in range(8):
        vec_up[0:1, pl.ds(s * TILE, TILE)] = vector_row(small, s, B_UP, layer, core, TILE)
    q_bias = []
    for s in range(8):
        row = vector_row(small, s, B_QV, layer, 0, 256)
        for at in (0, 2 * HEAD_DIM):
            q_bias.append(
                jnp.where(
                    core == 0,
                    row[:, at : at + HEAD_DIM],
                    row[:, at + HEAD_DIM : at + 2 * HEAD_DIM],
                )
            )
    vec_up[1:2, pl.ds(0, half_width)] = jnp.concatenate(q_bias[:8], axis=-1)
    vec_up[1:2, pl.ds(half_width, half_width)] = jnp.zeros((1, half_width), F32)
    vec_up[1:2, pl.ds(2 * half_width, half_width)] = jnp.concatenate(q_bias[8:], axis=-1)

    def first_norm(rows):
        normed, _ = norm_of(state[rows, :])
        act_one[rows, :] = (normed * vec[0] + vec[1]).astype(LOW)

    over_rows(length, first_norm)
    loads[0].wait()

    def project(t):
        here = tile_at(t)
        bias = vec_up[1:2, here]
        qkv[:, here] = (dot(act_one[...], v_qkv[:, here]) + bias).astype(LOW)

    over_tiles(3 * half_width // TILE, project)
    seg_row, seg_col = seg_row_col(segs)
    allowed = allowed_pairs(seg_col, seg_row)
    scale = 1.0 / math.sqrt(HEAD_DIM)
    for h in range(half_width // HEAD_DIM):
        q, k, v = (qkv[:, pl.ds(t * half_width + h * HEAD_DIM, HEAD_DIM)] for t in range(3))
        probs = head_probs(q, k, allowed, scale).astype(LOW)
        attn[:, pl.ds(h * HEAD_DIM, HEAD_DIM)] = dot(probs, v).astype(LOW)
    loads[1].wait()
    pair.fill(0, lambda t: dot(attn[...], v_out[:, tile_at(t)]))
    if moved:
        sequences.cross()
    pair.wait(0)

    def second_norm(rows):
        x = state[rows, :] + pair.total(0, rows) + vec[2]
        middle[rows, :] = x
        normed, _ = norm_of(x)
        act_two[rows, :] = (normed * vec[3] + vec[4]).astype(LOW)

    over_rows(length, second_norm)
    loads[2].wait()

    def expand(t):
        here = tile_at(t)
        value, rise = gelu_pair(dot(act_two[...], v_up[:, here]) + vec_up[0:1, here])
        hidden[:, here] = value.astype(LOW)
        slope[:, here] = rise

    over_tiles(slope.shape[1] // TILE, expand)
    if count:
        for s in streams:
            s.onward(2)
    loads[3].wait()
    pair.fill(1, lambda t: dot(hidden[...], v_down[:, tile_at(t)]))
    pair.wait(1)

    def close(rows):
        new_state[rows, :] = middle[rows, :] + pair.total(1, rows) + vec[5]

    over_rows(length, close)
    if count:
        for s in streams:
            s.finish(2)
        for s in streams:
            s.drain((2,))
    if moved:
        sequences.drain()


def weight_scratch(weights):
    w_up, w_down, w_qkv, w_out = weights
    return [pltpu.VMEM(w.shape, LOW) for w in (w_qkv, w_out, w_up, w_down)]


def pair_scratch(length, width):
    shape = (2, width // TILE, length, TILE)
    return [pltpu.VMEM(shape, F32), pltpu.VMEM(shape, F32)]


def forward_block(layer, state, segs, small, weights, begun, parts):
    count, moved = len(begun), len(parts)
    length, width = state.shape
    inner = weights[0].shape[1]
    shapes = [
        ((length, width), F32),
        ((length, width), LOW),
        ((length, 3 * width // 2), LOW),
        ((length, width // 2), LOW),
        ((length, width), F32),
        ((length, width), LOW),
        ((length, inner), F32),
        ((length, inner), LOW),
    ]
    shapes = [jax.ShapeDtypeStruct(*s) for s in shapes]
    shapes += [jax.ShapeDtypeStruct(b.shape, b.dtype) for b in begun]
    out = pl.pallas_call(
        functools.partial(forward_kernel, layer, count, moved),
        out_shape=shapes + sequence_shapes(parts),
        in_specs=[VMEM] * 3 + [ANY] * (4 + count + moved),
        out_specs=[VMEM] * 8 + [ANY] * (count + moved),
        input_output_aliases={7 + m: 8 + m for m in range(count)},
        scratch_shapes=weight_scratch(weights)
        + pair_scratch(length, width)
        + [
            pltpu.VMEM((6, 1, width), F32),
            pltpu.VMEM((2, inner), F32),
            DMA((4,)),
            DMA((2, width // TILE)),
            DMA((2, width // TILE)),
        ]
        + ([DMA((count, 12)), DMA((count, 12))] if count else [])
        + sequence_scratch(moved),
        compiler_params=pltpu.CompilerParams(
            collective_id=2 + layer, has_side_effects=True, vmem_limit_bytes=60 * 1024 * 1024
        ),
        name="forward_block",
    )(state, segs, small, *weights, *begun, *parts)
    return out[:8], out[8 : 8 + count], out[8 + count :]


def column_sum(target, row, value):
    target[row : row + 1, :] += jnp.sum(value, axis=0, keepdims=True)


def backward_kernel(layer, count, *refs):
    grad_state, state, middle, qkv, attn, slope, hidden, act_one, act_two, segs, small = refs[:11]
    w_up, w_down, w_qkv, w_out = refs[11:15]
    given, refs = refs[15 : 15 + count], refs[15 + count :]
    new_grad, totals = refs[0], refs[1:5]
    g_heads, g_out, small_grad = refs[5:8], refs[8], refs[9]
    sums, refs = refs[10 : 10 + count], refs[10 + count :]
    v_qkv, v_out, v_up, v_down, terms, box, vec, acc, acc_up, acc_qkv = refs[:10]
    grad_low, d_pre_low, mid_low, d_qkv, d_attn = refs[10:15]
    boxes, refs = refs[15:19], refs[19:]
    load, p_send, p_recv, o_send, o_recv = refs[:5]
    rings = refs[5:]
    core = lax.axis_index("core")
    length, width = state.shape
    half_width = width // 2
    inner = slope.shape[1]
    loads = [
        pltpu.make_async_copy(w, v, load.at[i])
        for i, (w, v) in enumerate(((w_down, v_down), (w_up, v_up), (w_out, v_out), (w_qkv, v_qkv)))
    ]
    for copy in loads:
        copy.start()
    pos = positions()
    greet(pos, False)
    streams, at = [], 0
    for m in range(count):
        take = 3 if m < SPLIT else 6
        sems = [rings[len(rings) - 3 + k].at[m] for k in range(3)]
        streams.append(scatter_of(pos, m, given[m], rings[at : at + take], (sums[m],), sems))
        at += take
    own = [
        Scatter(
            pos,
            SCATTERS[m],
            0,
            v_up if m < 2 else v_down,
            None,
            (boxes[m],),
            (totals[m],),
            o_send.at[m],
            o_recv.at[m],
            None,
            totals[m - 1].shape[-1] if m % 2 else 0,
        )
        for m in range(SPLIT)
    ]

    def carry(at):
        for s in streams:
            s.step(at)

    carry(0)
    pair = Pair(terms, box, p_send, p_recv)
    fill_vector(vec.at[0], small, G_ONE, layer)
    fill_vector(vec.at[1], small, G_TWO, layer)
    acc[...] = jnp.zeros_like(acc)
    tokens = ((0,), (0,))

    def down_rows(t):
        return (t // 2, pl.ds(lax.rem(t, 2) * 2, 2))

    def lower(rows):
        g = grad_state[rows, :]
        grad_low[rows, :] = g.astype(LOW)
        column_sum(acc, 0, g)

    over_rows(length, lower)
    loads[0].wait()

    def contract(t):
        here = tile_at(t)
        w = v_down[down_rows(t)].reshape(TILE, width)
        d_pre = dot(grad_low[...], w, ((1,), (1,))) * slope[:, here]
        d_pre_low[:, here] = d_pre.astype(LOW)
        acc_up[:, here] = jnp.sum(d_pre, axis=0, keepdims=True)

    over_tiles(inner // TILE, contract)
    carry(1)

    def down_grad(t):
        value = dot(hidden[:, tile_at(t)], grad_low[...], tokens)
        v_down[down_rows(t)] = value.reshape(2, RING, 32, width).astype(LOW)

    over_tiles(inner // TILE, down_grad)
    for s in own[2:]:
        s.begin(0)
    loads[1].wait()
    pair.fill(0, lambda t: dot(d_pre_low[...], v_up[t].reshape(TILE, inner), ((1,), (1,))))


    def up_grad(t):
        value = dot(act_two[:, tile_at(t)], d_pre_low[...], tokens)
        v_up[t] = value.reshape(RING, RING, 16, inner).astype(LOW)

    over_tiles(width // TILE, up_grad)
    for s in own[:2]:
        s.begin(0)
    pair.wait(0)

    def second_norm(rows):
        d_act = pair.total(0, rows)
        normed, factor = norm_of(middle[rows, :])
        column_sum(acc, 1, d_act * normed)
        column_sum(acc, 2, d_act)
        g = grad_state[rows, :] + norm_backward(d_act, normed, factor, vec[1])
        new_grad[rows, :] = g
        mid_low[rows, :] = g.astype(LOW)
        column_sum(acc, 3, g)

    over_rows(length, second_norm)
    carry(2)
    loads[2].wait()

    def attn_grad(t):
        here = tile_at(t)
        d_attn[:, here] = dot(mid_low[...], v_out[here, :], ((1,), (1,))).astype(LOW)

    over_tiles(half_width // TILE, attn_grad)

    def out_grad(t):
        value = dot(attn[:, tile_at(t)], mid_low[...], tokens)
        g_out[pl.ds(t * 2, 2)] = value.reshape(2, RING, RING, 8, width).astype(LOW)

    over_tiles(half_width // TILE, out_grad)
    seg_row, seg_col = seg_row_col(segs)
    allowed = allowed_pairs(seg_col, seg_row)
    scale = 1.0 / math.sqrt(HEAD_DIM)
    for h in range(half_width // HEAD_DIM):
        q, k, v = (qkv[:, pl.ds(t * half_width + h * HEAD_DIM, HEAD_DIM)] for t in range(3))
        here = pl.ds(h * HEAD_DIM, HEAD_DIM)
        d_head = d_attn[:, here]
        full = head_probs(q, k, allowed, scale)
        delta = jnp.sum(
            d_head.astype(F32) * attn[:, here].astype(F32), axis=-1, keepdims=True
        )
        d_scores = (full * (dot(d_head, v, ((1,), (1,))) - delta)).astype(LOW)
        ends = (
            dot(d_scores, k) * scale,
            dot(d_scores, q, ((0,), (0,))) * scale,
            dot(full.astype(LOW), d_head, ((0,), (0,))),
        )
        for t, end in enumerate(ends):
            place = pl.ds(t * half_width + h * HEAD_DIM, HEAD_DIM)
            d_qkv[:, place] = end.astype(LOW)
            acc_qkv[:, place] = jnp.sum(end, axis=0, keepdims=True)
        if h == 5:
            for s in own:
                s.onward(0)
    carry(3)
    loads[3].wait()
    pair.fill(1, lambda t: dot(d_qkv[...], v_qkv[tile_at(t), :], ((1,), (1,))))

    def head_grad(t):
        value = dot(act_one[:, tile_at(t)], d_qkv[...], tokens)
        for part in range(3):
            third = value[:, part * half_width : (part + 1) * half_width]
            g_heads[part][t] = third.reshape(RING, RING, 16, half_width).astype(LOW)

    over_tiles(width // TILE, head_grad)
    carry(4)
    pair.wait(1)

    def first_norm(rows):
        d_act = pair.total(1, rows)
        normed, factor = norm_of(state[rows, :])
        column_sum(acc, 4, d_act * normed)
        column_sum(acc, 5, d_act)
        new_grad[rows, :] += norm_backward(d_act, normed, factor, vec[0])

    over_rows(length, first_norm)
    small_grad[...] = jnp.zeros_like(small_grad)
    first = (core == 0).astype(F32)
    for s in range(8):
        here = pl.ds(s * 128, 128)
        target = small_grad.at[s // 2, pl.ds((s % 2) * 2, 2)]
        for vector, row in ((B_DOWN, 0), (G_TWO, 1), (S_TWO, 2), (B_OUT, 3), (G_ONE, 4), (S_ONE, 5)):
            target[vector // 4, vector % 4, 0:1, 0:128] = acc[row : row + 1, here] * first
        block = acc_up[:, pl.ds(s * TILE, TILE)]
        target[B_UP // 4, B_UP % 4, 0:1, :] = block * first
        target[B_UP // 4, B_UP % 4, 1:2, :] = block * (1.0 - first)
        at = (s // 4) * 2 * half_width + (s % 4) * 2 * HEAD_DIM
        heads = []
        for k in range(2):
            value = acc_qkv[:, pl.ds(at + k * HEAD_DIM, HEAD_DIM)]
            heads += [value * first, value * (1.0 - first)]
        target[B_QV // 4, B_QV % 4, 0:1, :] = jnp.concatenate(heads, axis=-1)
    carry(5)
    for s in own:
        s.finish(0)
    carry(6)
    for s in streams:
        s.drain()
    for s in own:
        s.drain((0,))


def backward_block(layer, grad_state, record, segs, small, weights, given):
    state = record[0]
    count = len(given)
    length, width = state.shape
    inner = record[4].shape[1]
    cube = (RING, RING, RING)
    w_up, w_down, w_qkv, w_out = weights
    halves = []
    for w, (share, of) in ((w_up, UP_PART), (w_down, DOWN_PART)):
        rows, cols = w.shape[3:]
        halves += [(rows, cols * share // of), (rows, cols - cols * share // of)]
    ends = [((length, width), F32)] + [((RING, RING) + h, LOW) for h in halves]
    ends += [(cube + (width // 64, width // 2), LOW)] * 3
    ends += [(cube + w_out.shape[3:], LOW), (cube + (8, 256), F32)]
    shapes = [jax.ShapeDtypeStruct(*e) for e in ends]
    shapes += [jax.ShapeDtypeStruct(g.shape[-2:], g.dtype) for g in given]
    bufs = []
    for m, g in enumerate(given):
        bufs += scatter_scratch(g.shape[-2:], g.dtype, 1 if m < SPLIT else 0, False)
    sems = [DMA((count, 18)), DMA((count, 18)), DMA((count, 5))] if count else []
    flat = [w.reshape(-1, w.shape[-1]) for w in (w_qkv, w_out)]
    out = pl.pallas_call(
        functools.partial(backward_kernel, layer, count),
        out_shape=shapes,
        in_specs=[VMEM] * 11 + [ANY] * 4 + [VMEM] * min(count, SPLIT) + [ANY] * max(count - SPLIT, 0),
        out_specs=[VMEM] * (10 + count),
        scratch_shapes=[pltpu.VMEM(w.shape, LOW) for w in flat + [w_up, w_down]]
        + pair_scratch(length, width)
        + [
            pltpu.VMEM((2, 1, width), F32),
            pltpu.VMEM((6, width), F32),
            pltpu.VMEM((1, inner), F32),
            pltpu.VMEM((1, 3 * width // 2), F32),
            pltpu.VMEM((length, width), LOW),
            pltpu.VMEM((length, inner), LOW),
            pltpu.VMEM((length, width), LOW),
            pltpu.VMEM((length, 3 * width // 2), LOW),
            pltpu.VMEM((length, width // 2), LOW),
        ]
        + [pltpu.VMEM((6, RING, RING, r, c // 2), LOW) for r, c in halves]
        + [
            DMA((4,)),
            DMA((2, width // TILE)),
            DMA((2, width // TILE)),
            DMA((SPLIT, 6)),
            DMA((SPLIT, 6)),
        ]
        + bufs
        + sems,
        compiler_params=pltpu.CompilerParams(
            collective_id=4 + layer, has_side_effects=True, vmem_limit_bytes=67043328
        ),
        name="backward_block",
    )(grad_state, *record, segs, small, w_up, w_down, *flat, *given)
    return out[0], list(out[1:10]), list(out[10:])


def finish_kernel(layers, *refs):
    ins, outs = refs[: 9 * layers], refs[9 * layers :]
    o_qkv, o_out, o_up, o_down = outs[:4]
    for l in range(layers):
        up_a, up_b, down_a, down_b, *qkv, out, small = ins[9 * l : 9 * l + 9]
        blocks = up_a.shape[-1] // TILE
        for s in range(8):
            for c in range(2):
                up, at = (up_a, s) if s < blocks else (up_b, s - blocks)
                o_up[l, :, pl.ds((2 * s + c) * TILE, TILE)] = up[c, 0, :, pl.ds(at * TILE, TILE)].astype(F32)
        for c in range(2):
            o_down[l, c, 0] = jnp.concatenate([down_a[c, 0], down_b[c, 0]], axis=-1).astype(F32)
            o_out[l, c, 0] = out[c, 0].astype(F32)
        for k in range(24):
            here = pl.ds((k % 8) * HEAD_DIM, HEAD_DIM)
            both = jnp.concatenate([qkv[k // 8][c, 0, :, here] for c in range(2)], axis=-1)
            o_qkv[l, :, pl.ds(k * 128, 128)] = both.astype(F32)

        @pl.when(pl.program_id(0) == 0)
        def _():
            for v in range(8):
                o = outs[4 + v]
                size = o.shape[1]
                for part in range((size + 255) // 256):
                    span = min(size, 256)
                    o[l : l + 1, pl.ds(part * 256, span)] = (
                        small[0, v, part : part + 1, 0:span] + small[1, v, part : part + 1, 0:span]
                    )


def finish(finals, sizes):
    layers = len(finals)
    in_specs, args = [], []
    for f in finals:
        for m, a in enumerate(f):
            r, c = a.shape[3:]
            args.append(a.reshape(2, 8, r, c))
            if m < 8:
                in_specs.append(pl.BlockSpec((2, 1, r, c), lambda p: (0, p, 0, 0)))
            else:
                in_specs.append(pl.BlockSpec((2, 8, r, c), lambda p: (0, 0, 0, 0)))
    up, up_b, down, down_b, qkv, _, _, out = (a.shape[2:] for a in args[:8])
    up, down = (up[0], up[1] + up_b[1]), (down[0], down[1] + down_b[1])
    shapes, specs = [], []
    for rows, cols in ((qkv[0], 6 * qkv[1]), (0, 0), (up[0], 2 * up[1])):
        if rows:
            shapes.append(jax.ShapeDtypeStruct((layers, 8 * rows, cols), F32))
            specs.append(pl.BlockSpec((layers, rows, cols), lambda p: (0, p, 0)))
        else:
            shapes.append(jax.ShapeDtypeStruct((layers, 2, 8) + out, F32))
            specs.append(pl.BlockSpec((layers, 2, 1) + out, lambda p: (0, 0, p, 0, 0)))
    shapes.append(jax.ShapeDtypeStruct((layers, 2, 8) + down, F32))
    specs.append(pl.BlockSpec((layers, 2, 1) + down, lambda p: (0, 0, p, 0, 0)))
    for size in sizes:
        shapes.append(jax.ShapeDtypeStruct((layers, size), F32))
        specs.append(pl.BlockSpec((layers, size), lambda p: (0, 0)))
    res = pl.pallas_call(
        functools.partial(finish_kernel, layers),
        out_shape=shapes,
        grid=(8,),
        in_specs=in_specs,
        out_specs=specs,
        name="finish",
    )(*args)
    o_out = res[1].reshape(layers, 16 * out[0], out[1])
    o_down = res[3].reshape(layers, 16 * down[0], down[1])
    return (res[0], o_out, res[2], o_down) + tuple(res[4:])


def prepare_kernel(where, up, down, qkv, out, segment_ids, *refs):
    vectors, refs = refs[:8], refs[8:]
    layers = up.shape[0]
    sub, core = where[0], where[1]
    for l in range(layers):
        o_up, o_down, o_qkv, o_out = refs[4 * l : 4 * l + 4]
        o_down[...] = down[l]
        o_out[...] = out[l]
        for s in range(8):
            at = pl.multiple_of((2 * s + core) * TILE, TILE)
            o_up[:, pl.ds(s * TILE, TILE)] = up[l, :, pl.ds(at, TILE)]
        for k in range(12):
            two = []
            for j in range(2):
                pair = qkv[l, :, pl.ds((2 * k + j) * 128, 128)]
                two.append(jnp.where(core == 0, pair[:, :HEAD_DIM], pair[:, HEAD_DIM:]))
            o_qkv[:, pl.ds(k * 128, 128)] = jnp.concatenate(two, axis=-1)
    small, segs = refs[4 * layers :]
    small[...] = jnp.zeros_like(small)
    for v, vector in enumerate(vectors):

        @pl.when(sub == v)
        def _():
            size = vector.shape[1]
            for part in range((size + 255) // 256):
                span = min(size, 256)
                block = vector[:, pl.ds(part * 256, span)].astype(F32)
                for l in range(layers):
                    small[2 * l + part : 2 * l + part + 1, 0:span] = block[l : l + 1]

    segs[...] = jnp.zeros_like(segs)
    for b in range(segs.shape[0]):
        segs[b, 0:1, 0 : segment_ids.shape[1]] = segment_ids[b : b + 1, :].astype(F32)


def prepare(weights, segment_ids, vectors):
    up, down, qkv, out = weights
    layers, rows = up.shape[:2]
    piece, down_rows, out_rows = rows // 8, down.shape[1] // 16, rows // 16
    where = jnp.stack(
        [lax.axis_index("xl") * 4 + lax.axis_index("y"), lax.axis_index("core")]
    ).astype(jnp.int32)
    per_layer = [
        (piece, up.shape[2] // 2),
        (down_rows, down.shape[2]),
        (piece, qkv.shape[2] // 2),
        (out_rows, out.shape[2]),
    ]
    shapes = [jax.ShapeDtypeStruct(e, LOW) for e in per_layer] * layers
    shapes += [jax.ShapeDtypeStruct((8, 256), F32), jax.ShapeDtypeStruct((2, 8, 128), F32)]
    by_row = lambda i, where: (0, where[0], 0)
    by_half = lambda i, where: (0, 8 * where[1] + where[0], 0)
    whole = lambda a: pl.BlockSpec(a.shape, lambda i, where: (0,) * len(a.shape))
    made = pl.pallas_call(
        prepare_kernel,
        out_shape=shapes,
        grid_spec=pltpu.PrefetchScalarGridSpec(
            num_scalar_prefetch=1,
            grid=(1,),
            in_specs=[
                pl.BlockSpec((layers, piece, up.shape[2]), by_row),
                pl.BlockSpec((layers, down_rows, down.shape[2]), by_half),
                pl.BlockSpec((layers, piece, qkv.shape[2]), by_row),
                pl.BlockSpec((layers, out_rows, out.shape[2]), by_half),
                whole(segment_ids),
            ]
            + [whole(v) for v in vectors],
            out_specs=[whole(e) for e in shapes],
        ),
        name="prepare",
    )(where, up, down, qkv, out, segment_ids, *vectors)
    owns = [made[4 * l : 4 * l + 4] for l in range(layers)]
    return owns, made[4 * layers], made[4 * layers + 1]


def per_device(
    inputs,
    segment_ids,
    weight_qkv,
    weight_out,
    weight_up,
    weight_down,
    bias_qv,
    bias_out,
    bias_up,
    bias_down,
    gain_one,
    shift_one,
    gain_two,
    shift_two,
    cotangent,
):
    layers, width = weight_qkv.shape[0], inputs.shape[-1]
    length = inputs.shape[1] * RING
    vectors = (bias_qv, bias_out, bias_up, bias_down, gain_one, shift_one, gain_two, shift_two)
    sizes = [v.shape[1] for v in vectors]
    owns, packed, segs = prepare((weight_up, weight_down, weight_qkv, weight_out), segment_ids, vectors)
    fulls, begun, wholes = gather_all(list(owns[0]) + [packed], list(owns[1]), [inputs, segs])
    state, segs = wholes[0].reshape(length, width), wholes[1]
    small = fulls[4].reshape(8, 8, 8, 256)
    records = []
    weights = [fulls[:4]]
    for l in range(layers):
        carried, parts = (begun, []) if l == 0 else ([], [cotangent])
        flat = [w.reshape(-1, w.shape[-1]) for w in weights[l]]
        made, fulls, wholes = forward_block(l, state, segs, small, flat, list(carried), parts)
        weights.append(fulls)
        new_state, act_one, qkv, attn, middle, act_two, slope, hidden = made
        records.append((state, middle, qkv, attn, slope, hidden, act_one, act_two))
        state = new_state
    grad_state = wholes[0].reshape(length, width)
    pieces = []
    for l in reversed(range(layers)):
        grad_state, pieces, sums = backward_block(
            l, grad_state, records[l], segs, small, weights[l], pieces
        )
    quarter = (RING, length // RING, width)
    finals, others, parts = scatter_all(
        pieces, sums, [state.reshape(quarter), grad_state.reshape(quarter)]
    )
    return (parts[0], parts[1]) + finish([finals, others], sizes)


def solution(mesh):
    torus = Mesh(mesh.devices.reshape(4, 2, 4, 2, 2), AXES)
    tokens = P(("xh", "y", "xl", "core"), "z", None)
    weight = P(None, ("z", "xh"), None)
    vector = P(None, ("z", "xh"))
    return jax.shard_map(
        per_device,
        mesh=torus,
        in_specs=(tokens, P(("xh", "y", "xl", "core"), "z")) + (weight,) * 4 + (vector,) * 8 + (tokens,),
        out_specs=(tokens, tokens) + (weight,) * 4 + (vector,) * 8,
        check_vma=False,
    )
```
